32 devices in a mesh: row: 4 (over y, core), col: 8 (over z, x).
Axes of the slice: x: 2, y: 2, z: 4, core: 2. Of those that a mesh axis runs over, the one named last changes fastest.
Arguments:
- ancestor_inverse: float32 [12288, 12288], P('row', 'col')
- factor: bfloat16 [3, 12288, 512], P(None, ('row', 'col')), may hold values from -0.5 to 0.5
- coupling: float32 [3, 512, 512], replicated, may hold values from -0.25 to 0.25
- diagonal_inverse: float32 [3, 512, 512], replicated, may hold values from -6 to 6
- ancestors: int32 [3, 24], replicated, may hold values from -1 to 23, as said below
Outputs:
- block_columns: float32 [3, 12288, 512], P(None, ('row', 'col'))
- block_rows: float32 [3, 12288, 512], P(None, ('col', 'row'))
- node_blocks: float32 [3, 3, 512, 512], replicated
The draws below stay inside these ranges and needn't reach their ends.
Inputs may be any that keep to these rules, and one draw needn't show every extreme that they name: `ancestors`: row k lists the ancestor block rows of supernode k, blocks of 512 rows: distinct indices in increasing order, then -1 in the slots left. Every block is listed by some supernode.
All inputs are finite; a program needn't handle non-finite values.
Results may differ from the reference program's by a relative error of at most 0.0003.
Values may be sent and summed in bfloat16 or wider, within the bound.
No kernel may reach another device: no remote copies, remote signals or barrier semaphores. Data moves between devices by JAX's collectives and lax.ppermute only.
A program may use at most 128 MiB of HBM per device.

```python
import math
import jax
import jax.numpy as jnp
from jax import lax

ORDER = 12288
SN = 512
NODES = 3
NBLK = 24
PAIRS = 3


def draw_ancestor_inverse(key, part):
    key_noise, key_diag = jax.random.split(jax.random.fold_in(key, 11))
    noise_draw = jax.random.normal(key_noise, (ORDER, ORDER), jnp.float32)
    symmetric = (noise_draw + noise_draw.T) * (0.5 / ORDER) ** 0.5
    diagonal = jnp.exp(jax.random.uniform(key_diag, (ORDER,), jnp.float32, math.log(0.2), 0.0))
    return symmetric + jnp.diag(diagonal)


def draw_ancestors(key, part):
    key_order, key_extra = jax.random.split(jax.random.fold_in(key, 7))
    shuffled = jax.random.permutation(key_order, NBLK).astype(jnp.int32)
    positions = jnp.arange(NBLK, dtype=jnp.int32)
    node_ids = jnp.arange(NODES, dtype=jnp.int32)
    lower_bound = NBLK * node_ids * (node_ids + 1) // (NODES * (NODES + 1))
    upper_bound = NBLK * (node_ids + 1) * (node_ids + 2) // (NODES * (NODES + 1))
    by_place = (positions[None, :] >= lower_bound[:, None]) & (positions[None, :] < upper_bound[:, None])
    primary = jnp.zeros((NODES, NBLK), jnp.bool_).at[:, shuffled].set(by_place)
    additions = jax.random.randint(key_extra, (NODES, NBLK), 0, 3) == 0
    member = primary | additions
    sort_keys = jnp.where(member, positions[None, :], NBLK + positions[None, :])
    ranked = jnp.sort(sort_keys, axis=1)
    return jnp.where(ranked < NBLK, ranked, -1).astype(jnp.int32)


def block_levels(key, shape, cuts, least, largest):
    loudness = 1.0
    for axis_at, blocks in cuts:
        heights = jax.random.uniform(jax.random.fold_in(jax.random.fold_in(key, 6), axis_at), (blocks,), jnp.float32, least / len(cuts), largest / len(cuts))
        loudness = loudness * jnp.repeat(jnp.exp(heights), shape[axis_at] // blocks).reshape((-1,) + (1,) * (len(shape) - 1 - axis_at))
    return loudness


def normal_values(rng, dims, width, reach, shards=(), held_as=jnp.bfloat16):
    drawn = width * jax.random.normal(rng, dims, jnp.float32)
    if shards:
        drawn = drawn * block_levels(rng, dims, shards, -0.22, 0.18)
    return jnp.clip(drawn, -reach, reach).astype(held_as)


def setup_inputs(seed: int = 0) -> dict:
    seeds = jax.random.split(jax.random.key(seed), 6)
    ancestor_inverse = draw_ancestor_inverse(jax.random.fold_in(seeds[5], 71), 0)
    factor = normal_values(seeds[1], (NODES, ORDER, SN), 0.0625, 0.5, ((1, 32),))
    coupling = normal_values(seeds[2], (PAIRS, SN, SN), SN ** -0.5, 0.25, (), jnp.float32)
    diagonal_inverse = normal_values(seeds[3], (NODES, SN, SN), 1.0, 6.0, (), jnp.float32)
    ancestors = draw_ancestors(jax.random.fold_in(seeds[5], 71), 0)
    return {"ancestor_inverse": ancestor_inverse, "factor": factor, "coupling": coupling, "diagonal_inverse": diagonal_inverse, "ancestors": ancestors}


def memberships(ancestors):
    block_ids = jnp.arange(NBLK, dtype=jnp.int32)
    return jnp.any(ancestors[:, :, None] == block_ids[None, None, :], axis=1)


def matmul(left, right):
    return jnp.dot(left, right, precision=lax.Precision.HIGHEST)


def reference(ancestor_inverse, factor, coupling, diagonal_inverse, ancestors):
    member = memberships(ancestors)
    row_mask = jnp.repeat(member, SN, axis=1).astype(jnp.float32)
    columns = []
    solved = {}
    for current in range(NODES):
        lower_part = factor[current].astype(jnp.float32) * row_mask[current][:, None]
        product_sum = matmul(ancestor_inverse, lower_part)
        for earlier in range(current):
            product_sum = product_sum + matmul(columns[earlier], coupling[current * (current - 1) // 2 + earlier])
        column = -product_sum
        for earlier in range(current):
            block_value = -matmul(columns[earlier].T, lower_part)
            for inner in range(current):
                block_value = block_value - matmul(solved[(earlier, inner)], coupling[current * (current - 1) // 2 + inner])
            solved[(earlier, current)] = block_value
            solved[(current, earlier)] = block_value.T
        diag_value = diagonal_inverse[current] - matmul(lower_part.T, column)
        for earlier in range(current):
            diag_value = diag_value - matmul(coupling[current * (current - 1) // 2 + earlier].T, solved[(earlier, current)])
        solved[(current, current)] = diag_value
        columns.append(column)
    block_columns = jnp.stack(columns)
    node_blocks = jnp.stack([jnp.stack([solved[(first_node, second_node)] for second_node in range(NODES)]) for first_node in range(NODES)])
    return block_columns, block_columns, node_blocks
```

```python
import jax
import jax.numpy as jnp
from jax import lax
from jax.sharding import PartitionSpec as P

highest = lax.Precision.HIGHEST
both = ("row", "col")


def matmul(left, right):
    return jnp.dot(left, right, precision=highest)


def left_dot(left, right):
    return lax.dot_general(left, right, (((0,), (0,)), ((), ())), precision=highest)


def pair_index(later, earlier):
    return later * (later - 1) // 2 + earlier


def split_terms(value):
    head = lax.reduce_precision(value, 8, 7)
    return head.astype(jnp.bfloat16), (value - head).astype(jnp.bfloat16)


def pick(stacked, index):
    return lax.dynamic_index_in_dim(stacked, index, 0, keepdims=False)


def ring_order(count):
    return list(range(0, count, 2)) + list(range(count - 1, 0, -2))


def ring_gather(piece, order):
    count = len(order)
    ahead = [(order[at], order[(at + 1) % count]) for at in range(count)]
    back = [(target, source) for source, target in ahead]
    half = piece.shape[0] // 2
    pieces = [piece]
    up = down = piece
    for _ in range(count // 2 - 1):
        up = lax.ppermute(up, "col", ahead)
        down = lax.ppermute(down, "col", back)
        pieces += [up, down]
    far_first = lax.ppermute(up[:half], "col", ahead)
    far_second = lax.ppermute(down[half:], "col", back)
    pieces += [far_first, far_second]
    return jnp.concatenate(pieces, axis=0)


def ring_sources(order, col_index):
    count = len(order)
    place = [0] * count
    for at, device in enumerate(order):
        place[device] = at
    my_place = jnp.asarray(place, jnp.int32)[col_index]
    table = jnp.asarray(order, jnp.int32)
    steps = [0]
    for step in range(1, count // 2):
        steps += [-step, step]
    steps.append(count // 2)
    return [table[(my_place + step) % count] for step in steps]


def row_reduce(partial, row_index, row_count):
    rows, width = partial.shape
    piece = rows // row_count
    core = row_index % 2
    lane = row_index // 2
    lanes = row_count // 2
    sibling = [(at, at ^ 1) for at in range(row_count)]
    grouped = partial.reshape(lanes, 2, piece, width)
    kept = lax.dynamic_index_in_dim(grouped, core, 1, keepdims=False)
    given = lax.dynamic_index_in_dim(grouped, 1 - core, 1, keepdims=False)
    kept = kept + lax.ppermute(given, "row", sibling)
    total = pick(kept, lane)
    for shift in range(1, lanes):
        moves = [(at, (at + 2 * shift) % row_count) for at in range(row_count)]
        total = total + lax.ppermute(pick(kept, (lane + shift) % lanes), "row", moves)
    return total


def reduce_everywhere(value, bits, flat_index, total):
    for bit in bits:
        mine = (flat_index >> bit) & 1
        halves = value.reshape(2, value.shape[0] // 2, value.shape[1])
        moves = [(at, at ^ (1 << bit)) for at in range(total)]
        value = pick(halves, mine) + lax.ppermute(pick(halves, 1 - mine), both, moves)
    return value


def spread_everywhere(value, bits, flat_index, total):
    for bit in reversed(bits):
        mine = (flat_index >> bit) & 1
        moves = [(at, at ^ (1 << bit)) for at in range(total)]
        other = lax.ppermute(value, both, moves)
        first = jnp.where(mine == 0, value, other)
        second = jnp.where(mine == 0, other, value)
        value = jnp.concatenate([first, second], axis=0)
    return value


def bit_orders(row_count, col_count):
    col_bits = col_count.bit_length() - 1
    row_bits = row_count.bit_length() - 1
    x_bits = [0]
    z_bits = list(range(1, col_bits))
    core_bits = [col_bits]
    y_bits = list(range(col_bits + 1, col_bits + row_bits))
    return [
        core_bits + x_bits + y_bits + z_bits,
        core_bits + y_bits + z_bits + x_bits,
        core_bits + z_bits + x_bits + y_bits,
    ]


def local(ancestor_inverse, factor, coupling, diagonal_inverse, ancestors):
    row_count = lax.axis_size("row")
    col_count = lax.axis_size("col")
    total = row_count * col_count
    row_index = lax.axis_index("row")
    col_index = lax.axis_index("col")
    flat_index = row_index * col_count + col_index
    nodes, piece_rows, width = factor.shape
    cols_here = ancestor_inverse.shape[1]
    block_of_row = (flat_index * piece_rows + jnp.arange(piece_rows, dtype=jnp.int32)) // width
    listed = jnp.any(ancestors[:, :, None] == block_of_row[None, None, :], axis=1)
    lower = jnp.where(listed[:, :, None], factor, jnp.zeros_like(factor))

    order = ring_order(col_count)
    gathered = [ring_gather(lower[node], order) for node in range(nodes)]
    blocks = ancestor_inverse.reshape(col_count, piece_rows, cols_here)
    ordered = jnp.concatenate([pick(blocks, at) for at in ring_sources(order, col_index)], axis=0)
    head, tail = split_terms(ordered)

    def product(lower_rows):
        dims = (((0,), (0,)), ((), ()))
        return lax.dot_general(
            head, lower_rows, dims, preferred_element_type=jnp.float32
        ) + lax.dot_general(tail, lower_rows, dims, preferred_element_type=jnp.float32)

    def g(later, earlier):
        return coupling[pair_index(later, earlier)]

    base = {}
    for k in range(nodes):
        for j in range(k):
            value = jnp.zeros((width, width), jnp.float32)
            for i in range(k):
                value = value - matmul(base[j, i], g(k, i))
            base[j, k] = value
            base[k, j] = value.T
        value = diagonal_inverse[k]
        for j in range(k):
            value = value - left_dot(g(k, j), base[j, k])
        base[k, k] = value

    mixed = []
    for k in range(nodes):
        value = lower[k].astype(jnp.float32)
        for j in range(k):
            value = value - matmul(mixed[j], g(k, j))
        mixed.append(value)

    to_rows = [
        (r * col_count + c, c * row_count + r) for r in range(row_count) for c in range(col_count)
    ]
    orders = bit_orders(row_count, col_count)
    by_cols = []
    by_rows = []
    solved = {}
    for k in range(nodes):
        value = row_reduce(product(gathered[k]), row_index, row_count)
        for j in range(k):
            value = value + matmul(by_cols[j], g(k, j))
        by_cols.append(-value)
        by_rows.append(lax.ppermute(by_cols[k], both, to_rows))
        for j in range(k + 1):
            bits = orders[j % len(orders)]
            part = reduce_everywhere(left_dot(mixed[j], by_rows[k]), bits, flat_index, total)
            summed = spread_everywhere(part, bits, flat_index, total)
            solved[j, k] = base[j, k] - summed
            if j < k:
                solved[k, j] = solved[j, k].T
    node_blocks = jnp.stack(
        [jnp.stack([solved[j, k] for k in range(nodes)]) for j in range(nodes)]
    )
    return jnp.stack(by_rows), jnp.stack(by_cols), node_blocks


def solution(mesh):
    placed = (P("row", "col"), P(None, both, None), P(), P(), P())
    return jax.shard_map(
        local,
        mesh=mesh,
        in_specs=placed,
        out_specs=(P(None, both, None), P(None, ("col", "row"), None), P()),
        check_vma=False,
    )
```

```python
import functools

import jax
import jax.numpy as jnp
from jax import lax
from jax.experimental import pallas as pl
from jax.experimental.pallas import tpu as pltpu
from jax.sharding import PartitionSpec as P

both = ("row", "col")
high = lax.Precision.HIGH


def matmul(left, right):
    return jnp.dot(left, right, precision=high)


def left_dot(left, right):
    return lax.dot_general(left, right, (((0,), (0,)), ((), ())), precision=high)


def right_dot(left, right):
    return lax.dot_general(left, right, (((1,), (1,)), ((), ())), precision=high)


def pair_index(later, earlier):
    return later * (later - 1) // 2 + earlier


def pick(stacked, index):
    return lax.dynamic_index_in_dim(stacked, index, 0, keepdims=False)


def after(value, *others):
    return lax.optimization_barrier((value, *others))[0]


def ring_order(count):
    return list(range(0, count, 2)) + list(range(count - 1, 0, -2))


def ring_gather(piece, order):
    count = len(order)
    ahead = [(order[at], order[(at + 1) % count]) for at in range(count)]
    back = [(target, source) for source, target in ahead]
    half = piece.shape[0] // 2
    pieces = [piece]
    up = down = piece
    for _ in range(count // 2 - 1):
        up = lax.ppermute(up, "col", ahead)
        down = lax.ppermute(down, "col", back)
        pieces += [up, down]
    far_first = lax.ppermute(up[:half], "col", ahead)
    far_second = lax.ppermute(down[half:], "col", back)
    pieces += [far_first, far_second]
    return pieces


def ring_sources(order, col_index):
    count = len(order)
    place = [0] * count
    for at, device in enumerate(order):
        place[device] = at
    my_place = jnp.asarray(place, jnp.int32)[col_index]
    table = jnp.asarray(order, jnp.int32)
    steps = [0]
    for step in range(1, count // 2):
        steps += [-step, step]
    steps.append(count // 2)
    return table[(my_place + jnp.asarray(steps, jnp.int32)) % count]


def product_body(count, lanes, piece, sources, core, *refs):
    pieces = refs[: count + 1]
    block, given, kept, total = refs[count + 1 :]
    step = pl.program_id(0)
    value = block[...]
    head = value.astype(jnp.bfloat16)
    tail = (value - head.astype(jnp.float32)).astype(jnp.bfloat16)

    def terms(lower):
        return jnp.dot(lower, head, preferred_element_type=jnp.float32) + jnp.dot(
            lower, tail, preferred_element_type=jnp.float32
        )

    @pl.when(step == 0)
    def _():
        total[...] = terms(pieces[0][...])

    for at in range(1, count - 1):

        @pl.when(step == at)
        def _(at=at):
            total[...] += terms(pieces[at][...])

    @pl.when(step == count - 1)
    def _():
        half = pieces[count - 1].shape[0]
        total[:half, :] += terms(pieces[count - 1][...])
        total[half:, :] += terms(pieces[count][...])
        for lane in range(lanes):
            for side in range(2):
                span = slice((2 * lane + side) * piece, (2 * lane + side + 1) * piece)

                @pl.when(core[0] == side)
                def _(lane=lane, span=span):
                    kept[lane] = total[:, span]

                @pl.when(core[0] != side)
                def _(lane=lane, span=span):
                    given[lane] = total[:, span]


def product(pieces, block, sources, core, lanes):
    count = len(pieces) - 1
    width, piece = pieces[0].shape
    cols = block.shape[1]
    whole = lambda array: pl.BlockSpec(array.shape, lambda step, *_: (0, 0))
    out = pl.BlockSpec((lanes, width, cols // (2 * lanes)), lambda step, *_: (0, 0, 0))
    shape = jax.ShapeDtypeStruct((lanes, width, cols // (2 * lanes)), jnp.float32)
    return pl.pallas_call(
        functools.partial(product_body, count, lanes, cols // (2 * lanes)),
        grid_spec=pltpu.PrefetchScalarGridSpec(
            num_scalar_prefetch=2,
            grid=(count,),
            in_specs=[whole(array) for array in pieces]
            + [pl.BlockSpec((piece, cols), lambda step, sources, core: (sources[step], 0))],
            out_specs=[out, out],
            scratch_shapes=[pltpu.VMEM((width, cols), jnp.float32)],
        ),
        out_shape=[shape, shape],
        compiler_params=pltpu.CompilerParams(
            dimension_semantics=("arbitrary",), vmem_limit_bytes=48 << 20
        ),
        cost_estimate=pl.CostEstimate(
            flops=4 * width * piece * count * cols,
            bytes_accessed=4 * piece * count * cols + 4 * width * cols,
            transcendentals=0,
        ),
        name="product",
    )(sources, core, *pieces, block)


def assemble_body(first_ref, second_ref, base_ref, out_ref):
    row, col = pl.program_id(0), pl.program_id(1)
    high_node = jnp.maximum(row, col)

    def put(value):
        @pl.when(row <= col)
        def _():
            out_ref[...] = value

        @pl.when(row > col)
        def _():
            out_ref[...] = value.T

    @pl.when(high_node < 2)
    def _():
        put(base_ref[...] - first_ref[...])

    @pl.when(high_node >= 2)
    def _():
        put(base_ref[...] - second_ref[...])


def assemble(first, second, base, nodes, width):
    def base_map(row, col):
        low, high_node = jnp.minimum(row, col), jnp.maximum(row, col)
        return (high_node * (high_node + 1) // 2 + low, 0, 0)

    def first_map(row, col):
        at = base_map(row, col)[0]
        return (jnp.where(at < 3, at, 0), 0)

    def second_map(row, col):
        at = base_map(row, col)[0]
        return (jnp.where(at < 3, 0, at - 3), 0)

    return pl.pallas_call(
        assemble_body,
        grid=(nodes, nodes),
        in_specs=[
            pl.BlockSpec((width, width), first_map),
            pl.BlockSpec((width, width), second_map),
            pl.BlockSpec((None, width, width), base_map),
        ],
        out_specs=pl.BlockSpec((None, None, width, width), lambda row, col: (row, col, 0, 0)),
        out_shape=jax.ShapeDtypeStruct((nodes, nodes, width, width), jnp.float32),
        name="assemble",
    )(first, second, base)


def row_reduce(given, kept, row_index, row_count):
    lane = row_index // 2
    lanes = row_count // 2
    sibling = [(at, at ^ 1) for at in range(row_count)]
    kept = kept + lax.ppermute(given, "row", sibling)
    total = pick(kept, lane)
    for shift in range(1, lanes):
        moves = [(at, (at + 2 * shift) % row_count) for at in range(row_count)]
        total = total + lax.ppermute(pick(kept, (lane + shift) % lanes), "row", moves)
    return total


def spread_bits(number, bits):
    return sum(((number >> at) & 1) << bit for at, bit in enumerate(bits))


def gather_bits(index, bits):
    return sum(((index >> bit) & 1) << at for at, bit in enumerate(bits))


def reduce_round(value, bits, flat_index, total):
    count = 1 << len(bits)
    parts = value.reshape(count, value.shape[0] // count, value.shape[1])
    mine = gather_bits(flat_index, bits)
    result = pick(parts, mine)
    for other in range(1, count):
        flip = spread_bits(other, bits)
        moves = [(at, at ^ flip) for at in range(total)]
        result = result + lax.ppermute(pick(parts, mine ^ other), both, moves)
    return result


def spread_round(value, bits, flat_index, total):
    count = 1 << len(bits)
    mine = gather_bits(flat_index, bits)
    result = jnp.zeros((count, *value.shape), value.dtype)
    result = lax.dynamic_update_index_in_dim(result, value, mine, 0)
    for other in range(1, count):
        flip = spread_bits(other, bits)
        moves = [(at, at ^ flip) for at in range(total)]
        part = lax.ppermute(value, both, moves)
        result = lax.dynamic_update_index_in_dim(result, part, mine ^ other, 0)
    return result.reshape(count * value.shape[0], value.shape[1])


def sum_everywhere(value, rounds, flat_index, total):
    for bits in rounds:
        value = reduce_round(value, bits, flat_index, total)
    for bits in reversed(rounds):
        value = spread_round(value, bits, flat_index, total)
    return value


def local(ancestor_inverse, factor, coupling, diagonal_inverse, ancestors):
    row_count = lax.axis_size("row")
    col_count = lax.axis_size("col")
    total = row_count * col_count
    row_index = lax.axis_index("row")
    col_index = lax.axis_index("col")
    flat_index = row_index * col_count + col_index
    nodes, piece_rows, width = factor.shape
    col_bits = col_count.bit_length() - 1
    row_bits = row_count.bit_length() - 1
    rounds = [
        [col_bits],
        [0, *range(col_bits + 1, col_bits + row_bits)],
        list(range(1, col_bits)),
    ]

    block_of_row = (flat_index * piece_rows + jnp.arange(piece_rows, dtype=jnp.int32)) // width
    listed = jnp.any(ancestors[:, :, None] == block_of_row[None, None, :], axis=1)
    lower = jnp.where(listed[:, :, None], factor, jnp.zeros_like(factor))
    lower = [lower[node].T for node in range(nodes)]

    order = ring_order(col_count)
    sources = ring_sources(order, col_index)
    core = (row_index % 2).reshape(1).astype(jnp.int32)
    gathered = [ring_gather(lower[node], order) for node in range(nodes)]

    coupling, diagonal_inverse = lax.optimization_barrier(
        (coupling, diagonal_inverse, gathered[0])
    )[:2]

    def g(later, earlier):
        return coupling[pair_index(later, earlier)]

    base = {}
    for k in range(nodes):
        for j in range(k):
            value = -matmul(base[j, 0], g(k, 0))
            for i in range(1, k):
                value = value - matmul(base[j, i], g(k, i))
            base[j, k] = value
            base[k, j] = value.T
        value = diagonal_inverse[k]
        for j in range(k):
            value = value - left_dot(g(k, j), base[j, k])
        base[k, k] = value
    base = jnp.stack([base[j, k] for k in range(nodes) for j in range(k + 1)])

    mixed = []
    for k in range(nodes):
        value = lower[k].astype(jnp.float32)
        for j in range(k):
            value = value - left_dot(g(k, j), mixed[j])
        mixed.append(value)

    swap = (1 << col_bits) | 1

    def middle(at):
        low, up = at & 1, (at >> col_bits) & 1
        return at if low == up else at ^ swap

    first_moves = [(at, middle(at)) for at in range(total)]
    last_moves = [
        (middle(r * col_count + c), c * row_count + r)
        for r in range(row_count)
        for c in range(col_count)
    ]
    by_cols = []
    by_rows = []
    sums = []
    parts = []
    for k in range(nodes):
        given, kept = product(gathered[k], ancestor_inverse, sources, core, row_count // 2)
        value = row_reduce(given, kept, row_index, row_count)
        for j in range(k):
            value = value + left_dot(g(k, j), by_cols[j])
        by_cols.append(-value)
        by_rows.append(lax.ppermute(lax.ppermute(-value, both, first_moves), both, last_moves))
        parts.append(right_dot(jnp.concatenate(mixed[: k + 1], axis=0), by_rows[k]))
        if k == nodes - 2:
            sums.append(sum_everywhere(jnp.concatenate(parts, axis=0), rounds, flat_index, total))
    sums.append(sum_everywhere(parts[-1], rounds, flat_index, total))
    node_blocks = assemble(sums[0], sums[1], base, nodes, width)
    out_rows = jnp.stack([value.T for value in by_rows])
    out_cols = jnp.stack([value.T for value in by_cols])
    return out_rows, out_cols, node_blocks


def solution(mesh):
    placed = (P("row", "col"), P(None, both, None), P(), P(), P())
    return jax.shard_map(
        local,
        mesh=mesh,
        in_specs=placed,
        out_specs=(P(None, both, None), P(None, ("col", "row"), None), P()),
        check_vma=False,
    )
```

```python
import functools

import jax
import jax.numpy as jnp
from jax import lax
from jax.experimental import pallas as pl
from jax.experimental.pallas import tpu as pltpu
from jax.sharding import PartitionSpec as P

both = ("row", "col")
high = lax.Precision.HIGH


def matmul(left, right):
    return jnp.dot(left, right, precision=high)


def left_dot(left, right):
    return lax.dot_general(left, right, (((0,), (0,)), ((), ())), precision=high)


def right_dot(left, right):
    return lax.dot_general(left, right, (((1,), (1,)), ((), ())), precision=high)


def pair_index(later, earlier):
    return later * (later - 1) // 2 + earlier


def pick(stacked, index):
    return lax.dynamic_index_in_dim(stacked, index, 0, keepdims=False)


def after(value, *others):
    return lax.optimization_barrier((value, *others))[0]


def ring_order(count):
    return list(range(0, count, 2)) + list(range(count - 1, 0, -2))


def ring_gather(piece, order):
    count = len(order)
    ahead = [(order[at], order[(at + 1) % count]) for at in range(count)]
    back = [(target, source) for source, target in ahead]
    half = piece.shape[0] // 2
    pieces = [piece]
    up = down = piece
    for _ in range(count // 2 - 1):
        up = lax.ppermute(up, "col", ahead)
        down = lax.ppermute(down, "col", back)
        pieces += [up, down]
    far_first = lax.ppermute(up[:half], "col", ahead)
    far_second = lax.ppermute(down[half:], "col", back)
    pieces += [far_first, far_second]
    return pieces


def ring_sources(order, col_index):
    count = len(order)
    place = [0] * count
    for at, device in enumerate(order):
        place[device] = at
    my_place = jnp.asarray(place, jnp.int32)[col_index]
    table = jnp.asarray(order, jnp.int32)
    steps = [0]
    for step in range(1, count // 2):
        steps += [-step, step]
    steps.append(count // 2)
    return table[(my_place + jnp.asarray(steps, jnp.int32)) % count]


def product_body(count, split_last, final, lanes, piece, sources, core, *refs):
    total_pieces = count + (1 if split_last else 0)
    pieces = refs[:total_pieces]
    block = refs[total_pieces]
    rest = refs[total_pieces + 1 :]
    if final:
        start, given, kept, total = rest
    else:
        (total,) = rest
    step = pl.program_id(0)
    value = block[...]
    head = value.astype(jnp.bfloat16)
    tail = (value - head.astype(jnp.float32)).astype(jnp.bfloat16)
    terms_here = jnp.concatenate([head, tail], axis=0)

    def terms(lower):
        return jnp.dot(
            jnp.concatenate([lower, lower], axis=1),
            terms_here,
            preferred_element_type=jnp.float32,
        )

    whole_pieces = count - 1 if split_last else count
    for at in range(whole_pieces):

        @pl.when(step == at)
        def _(at=at):
            value = terms(pieces[at][...])
            if at > 0:
                total[...] += value
            elif final:
                total[...] = start[...] + value
            else:
                total[...] = value

    if split_last:

        @pl.when(step == count - 1)
        def _():
            half = pieces[count - 1].shape[0]
            total[:half, :] += terms(pieces[count - 1][...])
            total[half:, :] += terms(pieces[count][...])

    if final:

        @pl.when(step == count - 1)
        def _():
            for lane in range(lanes):
                for side in range(2):
                    span = slice((2 * lane + side) * piece, (2 * lane + side + 1) * piece)

                    @pl.when(core[0] == side)
                    def _(lane=lane, span=span):
                        kept[lane] = total[:, span]

                    @pl.when(core[0] != side)
                    def _(lane=lane, span=span):
                        given[lane] = total[:, span]


def product(pieces, block, sources, core, lanes, start=None, split_last=False):
    final = start is not None
    count = len(pieces) - (1 if split_last else 0)
    width, piece = pieces[0].shape
    cols = block.shape[1]
    out_piece = cols // (2 * lanes)
    whole = lambda array: pl.BlockSpec(array.shape, lambda step, *_: (0,) * len(array.shape))
    in_specs = [whole(array) for array in pieces]
    in_specs.append(pl.BlockSpec((piece, cols), lambda step, sources, core: (sources[step], 0)))
    args = [*pieces, block]
    sum_shape = jax.ShapeDtypeStruct((width, cols), jnp.float32)
    if final:
        in_specs.append(whole(sum_shape))
        args.append(start)
        half_shape = jax.ShapeDtypeStruct((lanes, width, out_piece), jnp.float32)
        out_shape = [half_shape, half_shape]
        out_specs = [whole(half_shape), whole(half_shape)]
        scratch = [pltpu.VMEM((width, cols), jnp.float32)]
    else:
        out_shape, out_specs, scratch = sum_shape, whole(sum_shape), []
    return pl.pallas_call(
        functools.partial(product_body, count, split_last, final, lanes, out_piece),
        grid_spec=pltpu.PrefetchScalarGridSpec(
            num_scalar_prefetch=2,
            grid=(count,),
            in_specs=in_specs,
            out_specs=out_specs,
            scratch_shapes=scratch,
        ),
        out_shape=out_shape,
        compiler_params=pltpu.CompilerParams(
            dimension_semantics=("arbitrary",), vmem_limit_bytes=48 << 20
        ),
        cost_estimate=pl.CostEstimate(
            flops=4 * width * piece * count * cols,
            bytes_accessed=4 * piece * count * cols + 4 * width * cols,
            transcendentals=0,
        ),
        name="product",
    )(sources, core, *args)


pad_rows = 16
lane_step = 128


def scale_of(exponent):
    return jnp.exp2(exponent - 15.0)


def encode_body(count, *refs):
    out = refs[-1]
    value = refs[0][...]
    for ref in refs[1:count]:
        value = value + ref[...]
    rows = value.shape[-2]
    top = jnp.max(jnp.abs(value), axis=-2, keepdims=True)
    exponent = jnp.ceil(jnp.log2(jnp.maximum(top, 1e-30)) + 0.01)
    coded = jnp.round(value * jnp.exp2(15.0 - exponent))
    index = (slice(None),) * (len(value.shape) - 2)
    out[(*index, slice(0, rows), slice(None))] = coded.astype(jnp.int32).astype(jnp.int16)
    wide = jnp.broadcast_to(exponent, (*value.shape[:-2], pad_rows, value.shape[-1]))
    out[(*index, slice(rows, rows + pad_rows), slice(None))] = wide.astype(jnp.int32).astype(
        jnp.int16
    )


def encode(*values):
    shape = values[0].shape
    lead = shape[:-2]
    rows, lanes = shape[-2:]
    zeros = (0,) * (len(lead) + 1)
    return pl.pallas_call(
        functools.partial(encode_body, len(values)),
        grid=(lanes // lane_step,),
        in_specs=[pl.BlockSpec((*lead, rows, lane_step), lambda at: (*zeros, at))] * len(values),
        out_specs=pl.BlockSpec((*lead, rows + pad_rows, lane_step), lambda at: (*zeros, at)),
        out_shape=jax.ShapeDtypeStruct((*lead, rows + pad_rows, lanes), jnp.int16),
        cost_estimate=pl.CostEstimate(
            flops=4 * len(values) * values[0].size,
            bytes_accessed=4 * len(values) * values[0].size + 2 * values[0].size,
            transcendentals=0,
        ),
        name="encode",
    )(*values)


def decode(coded):
    rows = coded.shape[-2] - pad_rows
    exponent = coded[..., rows : rows + 1, :].astype(jnp.float32)
    return coded[..., :rows, :].astype(jnp.float32) * scale_of(exponent)


def assemble_body(first_ref, second_ref, base_ref, out_ref):
    row, col = pl.program_id(0), pl.program_id(1)
    high_node = jnp.maximum(row, col)

    def put(value):
        @pl.when(row <= col)
        def _():
            out_ref[...] = value

        @pl.when(row > col)
        def _():
            out_ref[...] = value.T

    @pl.when(high_node < 2)
    def _():
        put(base_ref[...] - first_ref[...])

    @pl.when(high_node >= 2)
    def _():
        put(base_ref[...] - second_ref[...])


def assemble(first, second, base, nodes, width):
    def base_map(row, col):
        low, high_node = jnp.minimum(row, col), jnp.maximum(row, col)
        return (high_node * (high_node + 1) // 2 + low, 0, 0)

    def first_map(row, col):
        at = base_map(row, col)[0]
        return (jnp.where(at < 3, at, 0), 0)

    def second_map(row, col):
        at = base_map(row, col)[0]
        return (jnp.where(at < 3, 0, at - 3), 0)

    return pl.pallas_call(
        assemble_body,
        grid=(nodes, nodes),
        in_specs=[
            pl.BlockSpec((width, width), first_map),
            pl.BlockSpec((width, width), second_map),
            pl.BlockSpec((None, width, width), base_map),
        ],
        out_specs=pl.BlockSpec((None, None, width, width), lambda row, col: (row, col, 0, 0)),
        out_shape=jax.ShapeDtypeStruct((nodes, nodes, width, width), jnp.float32),
        name="assemble",
    )(first, second, base)


def row_reduce(given, kept, row_index, row_count):
    lane = row_index // 2
    lanes = row_count // 2
    sibling = [(at, at ^ 1) for at in range(row_count)]
    other = lax.ppermute(given, "row", sibling)
    total = pick(kept, lane) + pick(other, lane)
    for shift in range(1, lanes):
        moves = [(at, (at + 2 * shift) % row_count) for at in range(row_count)]
        target = (lane + shift) % lanes
        coded = encode(pick(kept, target), pick(other, target))
        total = total + decode(lax.ppermute(coded, "row", moves))
    return total


def spread_bits(number, bits):
    return sum(((number >> at) & 1) << bit for at, bit in enumerate(bits))


def gather_bits(index, bits):
    return sum(((index >> bit) & 1) << at for at, bit in enumerate(bits))


def reduce_round(value, bits, flat_index, total, coding):
    count = 1 << len(bits)
    parts = value.reshape(count, value.shape[0] // count, value.shape[1])
    mine = gather_bits(flat_index, bits)
    result = pick(parts, mine)
    if coding:
        parts = encode(parts)
    for other in range(1, count):
        flip = spread_bits(other, bits)
        moves = [(at, at ^ flip) for at in range(total)]
        part = lax.ppermute(pick(parts, mine ^ other), both, moves)
        result = result + (decode(part) if coding else part)
    return result


def spread_round(value, bits, flat_index, total):
    count = 1 << len(bits)
    mine = gather_bits(flat_index, bits)
    result = jnp.zeros((count, *value.shape), value.dtype)
    result = lax.dynamic_update_index_in_dim(result, value, mine, 0)
    for other in range(1, count):
        flip = spread_bits(other, bits)
        moves = [(at, at ^ flip) for at in range(total)]
        part = lax.ppermute(value, both, moves)
        result = lax.dynamic_update_index_in_dim(result, part, mine ^ other, 0)
    return result.reshape(count * value.shape[0], *value.shape[1:])


def reduce_everywhere(value, rounds, flat_index, total):
    for at, bits in enumerate(rounds):
        value = reduce_round(value, bits, flat_index, total, at > 0)
    return encode(value)[None]


def spread_everywhere(value, rounds, flat_index, total):
    for bits in reversed(rounds):
        value = spread_round(value, bits, flat_index, total)
    return decode(value).reshape(-1, value.shape[-1])


def local(ancestor_inverse, factor, coupling, diagonal_inverse, ancestors):
    row_count = lax.axis_size("row")
    col_count = lax.axis_size("col")
    total = row_count * col_count
    row_index = lax.axis_index("row")
    col_index = lax.axis_index("col")
    flat_index = row_index * col_count + col_index
    nodes, piece_rows, width = factor.shape
    col_bits = col_count.bit_length() - 1
    row_bits = row_count.bit_length() - 1
    rounds = [
        [col_bits],
        [0, *range(col_bits + 1, col_bits + row_bits)],
        list(range(1, col_bits)),
    ]

    block_of_row = (flat_index * piece_rows + jnp.arange(piece_rows, dtype=jnp.int32)) // width
    listed = jnp.any(ancestors[:, :, None] == block_of_row[None, None, :], axis=1)
    lower = jnp.where(listed[:, :, None], factor, jnp.zeros_like(factor))
    lower = [lower[node].T for node in range(nodes)]

    order = ring_order(col_count)
    sources = ring_sources(order, col_index)
    core = (row_index % 2).reshape(1).astype(jnp.int32)
    gathered = [ring_gather(lower[node], order) for node in range(nodes)]

    coupling, diagonal_inverse = lax.optimization_barrier(
        (coupling, diagonal_inverse, gathered[0])
    )[:2]

    def g(later, earlier):
        return coupling[pair_index(later, earlier)]

    base = {}
    for k in range(nodes):
        for j in range(k):
            value = -matmul(base[j, 0], g(k, 0))
            for i in range(1, k):
                value = value - matmul(base[j, i], g(k, i))
            base[j, k] = value
            base[k, j] = value.T
        value = diagonal_inverse[k]
        for j in range(k):
            value = value - left_dot(g(k, j), base[j, k])
        base[k, k] = value
    base = jnp.stack([base[j, k] for k in range(nodes) for j in range(k + 1)])

    mixed = []
    for k in range(nodes):
        value = lower[k].astype(jnp.float32)
        for j in range(k):
            value = value - left_dot(g(k, j), mixed[j])
        mixed.append(value)

    swap = (1 << col_bits) | 1

    def middle(at):
        low, up = at & 1, (at >> col_bits) & 1
        return at if low == up else at ^ swap

    first_moves = [(at, middle(at)) for at in range(total)]
    last_moves = [
        (middle(r * col_count + c), c * row_count + r)
        for r in range(row_count)
        for c in range(col_count)
    ]
    by_cols = []
    by_rows = []
    parts = []
    reduced = []
    lanes = row_count // 2
    early = 1 + 2 * (col_count // 2 - 2)
    for k in range(nodes):
        start = product(gathered[k][:early], ancestor_inverse, sources[:early], core, lanes)
        given, kept = product(
            gathered[k][early:], ancestor_inverse, sources[early:], core, lanes, start, True
        )
        value = row_reduce(given, kept, row_index, row_count)
        for j in range(k):
            value = value + left_dot(g(k, j), by_cols[j])
        by_cols.append(-value)
        coded = lax.ppermute(encode(-value), both, first_moves)
        by_rows.append(decode(lax.ppermute(coded, both, last_moves)))
        parts.append(right_dot(jnp.concatenate(mixed[: k + 1], axis=0), by_rows[k]))
        if k == nodes - 2:
            joined = jnp.concatenate(parts, axis=0)
            reduced.append(reduce_everywhere(joined, rounds, flat_index, total))
    reduced.append(reduce_everywhere(parts[-1], rounds, flat_index, total))
    out_rows = jnp.stack([value.T for value in by_rows])
    out_cols = jnp.stack([value.T for value in by_cols])
    reduced[-1], base, out_rows, out_cols = lax.optimization_barrier(
        (reduced[-1], base, out_rows, out_cols)
    )
    sums = [spread_everywhere(value, rounds, flat_index, total) for value in reduced]
    node_blocks = assemble(sums[0], sums[1], base, nodes, width)
    return out_rows, out_cols, node_blocks


def solution(mesh):
    placed = (P("row", "col"), P(None, both, None), P(), P(), P())
    return jax.shard_map(
        local,
        mesh=mesh,
        in_specs=placed,
        out_specs=(P(None, both, None), P(None, ("col", "row"), None), P()),
        check_vma=False,
    )
```

```python
import functools

import jax
import jax.numpy as jnp
from jax import lax
from jax.experimental import pallas as pl
from jax.experimental.pallas import tpu as pltpu
from jax.sharding import PartitionSpec as P

both = ("row", "col")
high = lax.Precision.HIGH


def matmul(left, right):
    return jnp.dot(left, right, precision=high)


def left_dot(left, right):
    return lax.dot_general(left, right, (((0,), (0,)), ((), ())), precision=high)


def pair_index(later, earlier):
    return later * (later - 1) // 2 + earlier


def split_terms(value):
    head = lax.reduce_precision(value, 8, 7)
    return head.astype(jnp.bfloat16), (value - head).astype(jnp.bfloat16)


def after(value, *others):
    return lax.optimization_barrier((value, *others))[0]


def ring_order(count):
    return list(range(0, count, 2)) + list(range(count - 1, 0, -2))


def ring_gather(piece, order):
    count = len(order)
    ahead = [(order[at], order[(at + 1) % count]) for at in range(count)]
    back = [(target, source) for source, target in ahead]
    half = piece.shape[0] // 2
    pieces = [piece]
    up = down = piece
    for _ in range(count // 2 - 1):
        up = lax.ppermute(up, "col", ahead)
        down = lax.ppermute(down, "col", back)
        pieces += [up, down]
    far_first = lax.ppermute(up[:half], "col", ahead)
    far_second = lax.ppermute(down[half:], "col", back)
    pieces += [far_first, far_second]
    return pieces


def ring_sources(order, col_index):
    count = len(order)
    place = [0] * count
    for at, device in enumerate(order):
        place[device] = at
    my_place = jnp.asarray(place, jnp.int32)[col_index]
    table = jnp.asarray(order, jnp.int32)
    steps = [0]
    for step in range(1, count // 2):
        steps += [-step, step]
    steps.append(count // 2)
    return table[(my_place + jnp.asarray(steps, jnp.int32)) % count]


def product_body(count, split_last, final, lanes, piece, sources, core, *refs):
    total_pieces = count + (1 if split_last else 0)
    pieces = refs[:total_pieces]
    block = refs[total_pieces]
    rest = refs[total_pieces + 1 :]
    if final:
        start, given, kept, total = rest
    else:
        (total,) = rest
    step = pl.program_id(0)
    value = block[...]
    head = value.astype(jnp.bfloat16)
    tail = (value - head.astype(jnp.float32)).astype(jnp.bfloat16)
    terms_here = jnp.concatenate([head, tail], axis=0)

    def terms(lower):
        return jnp.dot(
            jnp.concatenate([lower, lower], axis=1),
            terms_here,
            preferred_element_type=jnp.float32,
        )

    whole_pieces = count - 1 if split_last else count
    for at in range(whole_pieces):

        @pl.when(step == at)
        def _(at=at):
            value = terms(pieces[at][...])
            if at > 0:
                total[...] += value
            elif final:
                total[...] = start[...] + value
            else:
                total[...] = value

    if split_last:

        @pl.when(step == count - 1)
        def _():
            half = pieces[count - 1].shape[0]
            total[:half, :] += terms(pieces[count - 1][...])
            total[half:, :] += terms(pieces[count][...])

    if final:

        @pl.when(step == count - 1)
        def _():
            for lane in range(lanes):
                for side in range(2):
                    span = slice((2 * lane + side) * piece, (2 * lane + side + 1) * piece)

                    @pl.when(core[0] == side)
                    def _(lane=lane, span=span):
                        kept[lane] = total[:, span]

                    @pl.when(core[0] != side)
                    def _(lane=lane, span=span):
                        given[lane] = total[:, span]


def product(pieces, block, sources, core, lanes, start=None, split_last=False):
    final = start is not None
    count = len(pieces) - (1 if split_last else 0)
    width, piece = pieces[0].shape
    cols = block.shape[1]
    out_piece = cols // (2 * lanes)
    whole = lambda array: pl.BlockSpec(array.shape, lambda step, *_: (0,) * len(array.shape))
    in_specs = [whole(array) for array in pieces]
    in_specs.append(pl.BlockSpec((piece, cols), lambda step, sources, core: (sources[step], 0)))
    args = [*pieces, block]
    sum_shape = jax.ShapeDtypeStruct((width, cols), jnp.float32)
    if final:
        in_specs.append(whole(sum_shape))
        args.append(start)
        half_shape = jax.ShapeDtypeStruct((lanes, width, out_piece), jnp.float32)
        out_shape = [half_shape, half_shape]
        out_specs = [whole(half_shape), whole(half_shape)]
        scratch = [pltpu.VMEM((width, cols), jnp.float32)]
    else:
        out_shape, out_specs, scratch = sum_shape, whole(sum_shape), []
    return pl.pallas_call(
        functools.partial(product_body, count, split_last, final, lanes, out_piece),
        grid_spec=pltpu.PrefetchScalarGridSpec(
            num_scalar_prefetch=2,
            grid=(count,),
            in_specs=in_specs,
            out_specs=out_specs,
            scratch_shapes=scratch,
        ),
        out_shape=out_shape,
        compiler_params=pltpu.CompilerParams(
            dimension_semantics=("arbitrary",), vmem_limit_bytes=48 << 20
        ),
        cost_estimate=pl.CostEstimate(
            flops=4 * width * piece * count * cols,
            bytes_accessed=4 * piece * count * cols + 4 * width * cols,
            transcendentals=0,
        ),
        name="product",
    )(sources, core, *args)


pad_rows = 16


def step_of(lanes):
    return 128 if lanes % 128 == 0 else lanes


def encoded(value):
    top = jnp.max(jnp.abs(value), axis=-2, keepdims=True)
    exponent = jnp.ceil(jnp.log2(jnp.maximum(top, 1e-30)) + 0.01)
    whole = jnp.round(value * jnp.exp2(15.0 - exponent)).astype(jnp.int32)
    wide = jnp.broadcast_to(exponent, (pad_rows, value.shape[-1])).astype(jnp.int32)
    return whole.astype(jnp.int16), wide.astype(jnp.int16)


def put_coded(ref, value, lead=()):
    rows = value.shape[0]
    whole, wide = encoded(value)
    ref[(*lead, slice(0, rows), slice(None))] = whole
    ref[(*lead, slice(rows, rows + pad_rows), slice(None))] = wide


def get_coded(ref, lead=()):
    rows = ref.shape[-2] - pad_rows
    whole = ref[(*lead, slice(0, rows), slice(None))].astype(jnp.int32).astype(jnp.float32)
    wide = ref[(*lead, slice(rows, rows + pad_rows), slice(None))].astype(jnp.int32)
    return whole * jnp.exp2(wide.astype(jnp.float32)[0:1, :] - 15.0)


def simple_call(body, name, args, in_specs, out_shape, out_specs, grid, prefetch=0, **more):
    size = sum(array.size * array.dtype.itemsize for array in args)
    return pl.pallas_call(
        body,
        grid_spec=pltpu.PrefetchScalarGridSpec(
            num_scalar_prefetch=prefetch,
            grid=grid,
            in_specs=in_specs,
            out_specs=out_specs,
            scratch_shapes=more.pop("scratch_shapes", ()),
        ),
        out_shape=out_shape,
        compiler_params=pltpu.CompilerParams(
            dimension_semantics=("arbitrary",) * len(grid), vmem_limit_bytes=48 << 20
        ),
        cost_estimate=pl.CostEstimate(flops=size, bytes_accessed=size, transcendentals=0),
        name=name,
        **more,
    )(*args)


def add_encode_body(shifts, lane, *refs):
    total = refs[2 * (shifts + 1)]
    total[...] = refs[0][...] + refs[1][...]
    for at in range(shifts):
        value = refs[2 * at + 2][...] + refs[2 * at + 3][...]
        put_coded(refs[2 * (shifts + 1) + 1 + at], value)


def add_encode(kept, other, lane, lanes):
    _, rows, width = kept.shape
    lane_step = step_of(width)
    in_specs, args = [], []
    for shift in range(lanes):
        spec = pl.BlockSpec(
            (None, rows, lane_step),
            lambda at, lane, shift=shift: (lax.rem(lane[0] + shift, lanes), 0, at),
        )
        in_specs += [spec, spec]
        args += [kept, other]
    out_specs = [pl.BlockSpec((rows, lane_step), lambda at, lane: (0, at))]
    out_shape = [jax.ShapeDtypeStruct((rows, width), jnp.float32)]
    for _ in range(1, lanes):
        out_specs.append(pl.BlockSpec((rows + pad_rows, lane_step), lambda at, lane: (0, at)))
        out_shape.append(jax.ShapeDtypeStruct((rows + pad_rows, width), jnp.int16))
    return simple_call(
        functools.partial(add_encode_body, lanes - 1), "add_encode", [lane, *args], in_specs,
        out_shape, out_specs, (width // lane_step,), 1,
    )


def split_dots(pairs):
    total = None
    for (left_head, left_tail), right in pairs:
        right_head = right.astype(jnp.bfloat16)
        right_tail = (right - right_head.astype(jnp.float32)).astype(jnp.bfloat16)
        for left, value in ((left_tail, right_head), (left_head, right_tail), (left_head, right_head)):
            part = jnp.dot(left, value, preferred_element_type=jnp.float32)
            total = part if total is None else total + part
    return total


def chain_body(node, lanes, *refs):
    mine, *received = refs[:lanes]
    heads = refs[lanes : lanes + node]
    tails = refs[lanes + node : lanes + 2 * node]
    earlier = refs[lanes + 2 * node : lanes + 3 * node]
    value, coded, turned = refs[-3:]
    total = mine[...]
    for ref in received:
        total = total + get_coded(ref)
    if node:
        total = total + split_dots(
            [((h[...], t[...]), e[...]) for h, t, e in zip(heads, tails, earlier, strict=True)]
        )
    total = -total
    value[...] = total
    put_coded(coded, total)
    turned[...] = total.T


def chain(node, nodes, mine, received, heads, tails, earlier, turned):
    rows, width = mine.shape
    lane_step = step_of(width)
    lanes = 1 + len(received)
    first = node * (node - 1) // 2
    column = lambda rows: pl.BlockSpec((rows, lane_step), lambda at: (0, at))
    in_specs = [column(rows)] + [column(rows + pad_rows)] * len(received)
    factor_specs = [
        pl.BlockSpec((None, rows, rows), lambda at, j=j: (first + j, 0, 0)) for j in range(node)
    ]
    in_specs += factor_specs + factor_specs + [column(rows)] * node
    args = [mine, *received, *[heads] * node, *[tails] * node, *earlier]
    aliases = {}
    if turned is not None:
        aliases = {len(args): 2}
        args.append(turned)
        in_specs.append(pl.BlockSpec(memory_space=pl.ANY))
    return simple_call(
        functools.partial(chain_body, node, lanes), "chain", args, in_specs,
        [
            jax.ShapeDtypeStruct((rows, width), jnp.float32),
            jax.ShapeDtypeStruct((rows + pad_rows, width), jnp.int16),
            jax.ShapeDtypeStruct((nodes, width, rows), jnp.float32),
        ],
        [
            column(rows),
            column(rows + pad_rows),
            pl.BlockSpec((None, lane_step, rows), lambda at: (node, at, 0)),
        ],
        (width // lane_step,), input_output_aliases=aliases,
    )


def turn_body(*refs):
    refs[-1][...] = get_coded(refs[0]).T


def turn(node, nodes, coded, turned):
    padded, width = coded.shape
    lane_step = step_of(width)
    rows = padded - pad_rows
    args, in_specs = [coded], [pl.BlockSpec((padded, lane_step), lambda at: (0, at))]
    aliases = {}
    if turned is not None:
        aliases = {1: 0}
        args.append(turned)
        in_specs.append(pl.BlockSpec(memory_space=pl.ANY))
    return simple_call(
        turn_body, "turn", args, in_specs,
        jax.ShapeDtypeStruct((nodes, width, rows), jnp.float32),
        pl.BlockSpec((None, lane_step, rows), lambda at: (node, at, 0)),
        (width // lane_step,), input_output_aliases=aliases,
    )


def inner_body(half, low, up, head, tail, rows, mine, given):
    value = split_dots([((head[...], tail[...]), rows[...])])

    @pl.when(pl.program_id(0) < half)
    def _():
        mine[...] = value

    @pl.when(pl.program_id(0) >= half)
    def _():
        given[...] = value


def inner(low, up, heads, tails, rows):
    nodes, piece, width = rows.shape
    count = nodes * (nodes + 1) // 2
    half = count // 2
    left = pl.BlockSpec((None, width, piece), lambda at, low, up: (low[at], 0, 0))
    shape = jax.ShapeDtypeStruct((half, width, width), jnp.float32)
    return simple_call(
        functools.partial(inner_body, half), "inner", [low, up, heads, tails, rows],
        [left, left, pl.BlockSpec((None, piece, width), lambda at, low, up: (up[at], 0, 0))],
        [shape, shape],
        [
            pl.BlockSpec((None, width, width), lambda at, *_: (jnp.minimum(at, half - 1), 0, 0)),
            pl.BlockSpec((None, width, width), lambda at, *_: (jnp.maximum(at - half, 0), 0, 0)),
        ],
        (count,), 2,
    )


def share_body(count, received, *refs):
    total = refs[0][...]
    for ref in refs[1 : 1 + received]:
        total = total + get_coded(ref)
    rows = total.shape[0] // count
    for at in range(count):
        put_coded(refs[-1], total[at * rows : (at + 1) * rows, :], (at,))


def share(mine, received, count):
    rows, width = mine.shape
    lane_step = step_of(width)
    column = lambda rows: pl.BlockSpec((rows, lane_step), lambda at: (0, at))
    return simple_call(
        functools.partial(share_body, count, len(received)), "share", [mine, *received],
        [column(rows)] + [column(rows + pad_rows)] * len(received),
        jax.ShapeDtypeStruct((count, rows // count + pad_rows, width), jnp.int16),
        pl.BlockSpec((count, rows // count + pad_rows, lane_step), lambda at: (0, 0, at)),
        (width // lane_step,),
    )


def collect_body(count, source, out):
    total = get_coded(source, (0,))
    for at in range(1, count):
        total = total + get_coded(source, (at,))
    whole, wide = encoded(total)
    rows = total.shape[0]
    for at in range(count):
        out[at, :rows, :] = whole
        out[at, rows:, :] = wide


def collect(parts):
    count, padded, width = parts.shape
    lane_step = step_of(width)
    spec = pl.BlockSpec((count, padded, lane_step), lambda at: (0, 0, at))
    return simple_call(
        functools.partial(collect_body, count), "collect", [parts], [spec],
        jax.ShapeDtypeStruct(parts.shape, jnp.int16), spec, (width // lane_step,),
    )


def finish_body(lanes, nodes, width, place, *refs):
    parts = refs[: 2 * lanes]
    base, out, sums = refs[2 * lanes :]
    step = pl.program_id(0)
    count, padded, _ = parts[0].shape
    rows = padded - pad_rows

    @pl.when(step == 0)
    def _():
        for at, ref in enumerate(parts):
            first = place[at] * (count * rows)
            for piece in range(count):
                start = pl.multiple_of(first + piece * rows, 8)
                sums[pl.ds(start, rows), :] = get_coded(ref, (piece,))

    row, col = step // nodes, step % nodes
    low, up = jnp.minimum(row, col), jnp.maximum(row, col)
    start = pl.multiple_of((up * (up + 1) // 2 + low) * width, width)
    value = base[...] - sums[pl.ds(start, width), :]

    @pl.when(row <= col)
    def _():
        out[...] = value

    @pl.when(row > col)
    def _():
        out[...] = value.T


def finish(place, parts, base, nodes, width):
    lanes = len(parts) // 2

    def base_map(step, place):
        row, col = step // nodes, step % nodes
        low, up = jnp.minimum(row, col), jnp.maximum(row, col)
        return (up * (up + 1) // 2 + low, 0, 0)

    whole = pl.BlockSpec(parts[0].shape, lambda step, place: (0, 0, 0))
    return simple_call(
        functools.partial(finish_body, lanes, nodes, width), "finish", [place, *parts, base],
        [whole] * len(parts) + [pl.BlockSpec((None, width, width), base_map)],
        jax.ShapeDtypeStruct((nodes, nodes, width, width), jnp.float32),
        pl.BlockSpec(
            (None, None, width, width), lambda step, place: (step // nodes, step % nodes, 0, 0)
        ),
        (nodes * nodes,), 1,
        scratch_shapes=[pltpu.VMEM((nodes * (nodes + 1) // 2 * width, width), jnp.float32)],
    )


def local(ancestor_inverse, factor, coupling, diagonal_inverse, ancestors):
    row_count = lax.axis_size("row")
    col_count = lax.axis_size("col")
    total = row_count * col_count
    row_index = lax.axis_index("row")
    col_index = lax.axis_index("col")
    flat_index = row_index * col_count + col_index
    nodes, piece_rows, width = factor.shape
    col_bits = col_count.bit_length() - 1
    block_of_row = (flat_index * piece_rows + jnp.arange(piece_rows, dtype=jnp.int32)) // width
    listed = jnp.any(ancestors[:, :, None] == block_of_row[None, None, :], axis=1)
    lower = jnp.where(listed[:, :, None], factor, jnp.zeros_like(factor))
    lower = [lower[node].T for node in range(nodes)]

    order = ring_order(col_count)
    sources = ring_sources(order, col_index)
    core = (row_index % 2).reshape(1).astype(jnp.int32)
    gathered = [ring_gather(lower[node], order) for node in range(nodes)]

    early_coupling = after(coupling, gathered[0][1])
    turned_heads, turned_tails = split_terms(jnp.swapaxes(early_coupling, 1, 2))
    mixed = []
    for k in range(nodes):
        value = lower[k].astype(jnp.float32)
        for j in range(k):
            value = value - left_dot(early_coupling[pair_index(k, j)], mixed[j])
        mixed.append(value)
    mixed_heads, mixed_tails = split_terms(jnp.stack(mixed))

    swap = (1 << col_bits) | 1

    def middle(at):
        low, up = at & 1, (at >> col_bits) & 1
        return at if low == up else at ^ swap

    first_moves = [(at, middle(at)) for at in range(total)]
    last_moves = [
        (middle(r * col_count + c), c * row_count + r)
        for r in range(row_count)
        for c in range(col_count)
    ]
    lanes = row_count // 2
    lane = row_index // 2
    lane_ref = lane.reshape(1).astype(jnp.int32)
    sibling = [(at, at ^ 1) for at in range(row_count)]
    lane_moves = [
        [(at, (at + 2 * shift) % row_count) for at in range(row_count)]
        for shift in range(1, lanes)
    ]
    early = 1 + 2 * (col_count // 2 - 2)

    def lane_sums(given, kept):
        other = lax.ppermute(given, "row", sibling)
        mine, *coded = add_encode(kept, other, lane_ref, lanes)
        return mine, [
            lax.ppermute(part, "row", moves)
            for part, moves in zip(coded, lane_moves, strict=True)
        ]

    by_cols = []
    out_cols = out_rows = None
    for k in range(nodes):
        start = product(gathered[k][:early], ancestor_inverse, sources[:early], core, lanes)
        given, kept = product(
            gathered[k][early:], ancestor_inverse, sources[early:], core, lanes, start, True
        )
        mine, received = lane_sums(given, kept)
        value, coded, out_cols = chain(
            k, nodes, mine, received, turned_heads, turned_tails, by_cols, out_cols
        )
        by_cols.append(value)
        coded = lax.ppermute(coded, both, first_moves)
        out_rows = turn(k, nodes, lax.ppermute(coded, both, last_moves), out_rows)

    coupling, diagonal_inverse = lax.optimization_barrier(
        (coupling, diagonal_inverse, by_cols[-1])
    )[:2]

    def g(later, earlier):
        return coupling[pair_index(later, earlier)]

    base = {}
    for k in range(nodes):
        for j in range(k):
            value = -matmul(base[j, 0], g(k, 0))
            for i in range(1, k):
                value = value - matmul(base[j, i], g(k, i))
            base[j, k] = value
            base[k, j] = value.T
        value = diagonal_inverse[k]
        for j in range(k):
            value = value - left_dot(g(k, j), base[j, k])
        base[k, k] = value
    base = jnp.stack([base[j, k] for k in range(nodes) for j in range(k + 1)])

    count = nodes * (nodes + 1) // 2
    listing = [(j, k) for k in range(nodes) for j in range(k + 1)]
    turn_to = (core[0] * (count // 2) + jnp.arange(count, dtype=jnp.int32)) % count
    low = jnp.asarray([j for j, _ in listing], jnp.int32)[turn_to]
    up = jnp.asarray([k for _, k in listing], jnp.int32)[turn_to]
    kept, given = inner(low, up, mixed_heads, mixed_tails, out_rows)
    part_rows = kept.shape[0] * width // lanes
    mine, received = lane_sums(
        given.reshape(lanes, part_rows, width), kept.reshape(lanes, part_rows, width)
    )
    shared = share(mine, received, col_count)
    summed = collect(lax.all_to_all(shared, "col", 0, 0, tiled=True))
    summed = lax.all_to_all(summed, "col", 0, 0, tiled=True)
    pieces = [summed] + [lax.ppermute(summed, "row", moves) for moves in lane_moves]
    summed_all = pieces + [lax.ppermute(piece, "row", sibling) for piece in pieces]
    shifts = [(lane - shift) % lanes for shift in range(lanes)]
    place = jnp.stack(
        [core[0] * lanes + at for at in shifts] + [(1 - core[0]) * lanes + at for at in shifts]
    ).astype(jnp.int32)
    summed_all[0], base = lax.optimization_barrier((summed_all[0], base))
    node_blocks = finish(place, summed_all, base, nodes, width)
    return out_rows, out_cols, node_blocks


def solution(mesh):
    placed = (P("row", "col"), P(None, both, None), P(), P(), P())
    return jax.shard_map(
        local,
        mesh=mesh,
        in_specs=placed,
        out_specs=(P(None, both, None), P(None, ("col", "row"), None), P()),
        check_vma=False,
    )
```

```python
import functools

import jax
import jax.numpy as jnp
from jax import lax
from jax.experimental import pallas as pl
from jax.experimental.pallas import tpu as pltpu
from jax.sharding import PartitionSpec as P

both = ("row", "col")
high = lax.Precision.HIGH


def matmul(left, right):
    return jnp.dot(left, right, precision=high)


def left_dot(left, right):
    return lax.dot_general(left, right, (((0,), (0,)), ((), ())), precision=high)


def pair_index(later, earlier):
    return later * (later - 1) // 2 + earlier


def split_terms(value):
    head = lax.reduce_precision(value, 8, 7)
    return head.astype(jnp.bfloat16), (value - head).astype(jnp.bfloat16)


def after(value, *others):
    return lax.optimization_barrier((value, *others))[0]


def ring_order(count):
    return list(range(0, count, 2)) + list(range(count - 1, 0, -2))


def ring_moves(order):
    count = len(order)
    ahead = [(order[at], order[(at + 1) % count]) for at in range(count)]
    return ahead, [(target, source) for source, target in ahead]


def ring_step(pieces, moves, last):
    up, down = (pieces[0], pieces[0]) if len(pieces) == 1 else pieces[-2:]
    if last:
        half = up.shape[0] // 2
        up, down = up[:half], down[half:]
    return [*pieces, lax.ppermute(up, "col", moves[0]), lax.ppermute(down, "col", moves[1])]


def ring_sources(order, col_index):
    count = len(order)
    place = [0] * count
    for at, device in enumerate(order):
        place[device] = at
    my_place = jnp.asarray(place, jnp.int32)[col_index]
    table = jnp.asarray(order, jnp.int32)
    steps = [0]
    for step in range(1, count // 2):
        steps += [-step, step]
    steps.append(count // 2)
    return table[(my_place + jnp.asarray(steps, jnp.int32)) % count]


def two_terms(block):
    value = block[...]
    head = value.astype(jnp.bfloat16)
    tail = (value - head.astype(jnp.float32)).astype(jnp.bfloat16)
    return jnp.concatenate([head, tail], axis=0)


def put_double(doubled, piece, span=slice(None)):
    depth = piece.shape[1]
    doubled[span, :depth] = piece[...]
    doubled[span, depth:] = piece[...]


def partial_body(nodes, count, resume, sources, *refs):
    pieces = refs[: nodes * count]
    block = refs[nodes * count]
    total, doubled = refs[-2:]
    node, step = pl.program_id(0), pl.program_id(1)
    for at, piece in enumerate(pieces):

        @pl.when((node == at // count) & (step == at % count))
        def _(piece=piece):
            put_double(doubled, piece)

    part = jnp.dot(doubled[...], two_terms(block), preferred_element_type=jnp.float32)

    @pl.when(step == 0)
    def _():
        total[...] = refs[nodes * count + 1][...] + part if resume else part

    @pl.when(step > 0)
    def _():
        total[...] += part


def final_body(count, lanes, out_piece, sources, core, *refs):
    pieces = refs[: count + 1]
    block, start, given, kept, total, doubled = refs[count + 1 :]
    step = pl.program_id(0)
    for at in range(count - 1):

        @pl.when(step == at)
        def _(at=at):
            put_double(doubled, pieces[at])

    @pl.when(step == count - 1)
    def _():
        half = pieces[count].shape[0]
        put_double(doubled, pieces[count - 1], slice(0, half))
        put_double(doubled, pieces[count], slice(half, 2 * half))

    part = jnp.dot(doubled[...], two_terms(block), preferred_element_type=jnp.float32)

    @pl.when(step == 0)
    def _():
        total[...] = start[...] + part

    @pl.when(step > 0)
    def _():
        total[...] += part

    @pl.when(step == count - 1)
    def _():
        for lane in range(lanes):
            for side in range(2):
                first = (2 * lane + side) * out_piece

                @pl.when(core[0] == side)
                def _(lane=lane, first=first):
                    kept[lane] = total[:, first : first + out_piece]

                @pl.when(core[0] != side)
                def _(lane=lane, first=first):
                    given[lane] = total[:, first : first + out_piece]


def product_call(body, grid, prefetch, args, in_specs, out_shape, out_specs, scratch, flops, **more):
    return pl.pallas_call(
        body,
        grid_spec=pltpu.PrefetchScalarGridSpec(
            num_scalar_prefetch=prefetch,
            grid=grid,
            in_specs=in_specs,
            out_specs=out_specs,
            scratch_shapes=scratch,
        ),
        out_shape=out_shape,
        compiler_params=pltpu.CompilerParams(
            dimension_semantics=("arbitrary",) * len(grid), vmem_limit_bytes=56 << 20
        ),
        cost_estimate=pl.CostEstimate(
            flops=flops, bytes_accessed=flops // 512, transcendentals=0
        ),
        **more,
    )(*args)


def partial_product(groups, block, sources, start=None):
    nodes, count = len(groups), len(groups[0])
    width, piece = groups[0][0].shape
    cols = block.shape[1]
    pieces = [array for group in groups for array in group]
    total = pl.BlockSpec((None, width, cols), lambda node, step, sources: (node, 0, 0))
    in_specs = [pl.BlockSpec(pieces[0].shape, lambda node, step, sources: (0, 0))] * len(pieces)
    in_specs.append(pl.BlockSpec((piece, cols), lambda node, step, sources: (sources[step], 0)))
    args = [sources, *pieces, block]
    aliases = {}
    if start is not None:
        aliases = {len(args): 0}
        in_specs.append(total)
        args.append(start)
    return product_call(
        functools.partial(partial_body, nodes, count, start is not None),
        (nodes, count), 1, args, in_specs,
        jax.ShapeDtypeStruct((nodes, width, cols), jnp.float32), total,
        [pltpu.VMEM((width, 2 * piece), jnp.bfloat16)],
        4 * nodes * count * width * piece * cols, input_output_aliases=aliases,
    )


def final_product(node, pieces, block, sources, core, lanes, start):
    count = len(pieces) - 1
    width, piece = pieces[0].shape
    cols = block.shape[1]
    out_piece = cols // (2 * lanes)
    half = jax.ShapeDtypeStruct((lanes, width, out_piece), jnp.float32)
    half_spec = pl.BlockSpec(half.shape, lambda step, *_: (0, 0, 0))
    in_specs = [pl.BlockSpec(array.shape, lambda step, *_: (0, 0)) for array in pieces]
    in_specs.append(pl.BlockSpec((piece, cols), lambda step, sources, core: (sources[step], 0)))
    in_specs.append(pl.BlockSpec((None, width, cols), lambda step, *_: (node, 0, 0)))
    return product_call(
        functools.partial(final_body, count, lanes, out_piece), (count,), 2,
        [sources, core, *pieces, block, start], in_specs, [half, half], [half_spec, half_spec],
        [pltpu.VMEM((width, cols), jnp.float32), pltpu.VMEM((width, 2 * piece), jnp.bfloat16)],
        4 * count * width * piece * cols,
    )


pad_rows = 16


def step_of(lanes):
    return 128 if lanes % 128 == 0 else lanes


def encoded(value):
    top = jnp.max(jnp.abs(value), axis=-2, keepdims=True)
    exponent = jnp.ceil(jnp.log2(jnp.maximum(top, 1e-30)) + 0.01)
    whole = jnp.round(value * jnp.exp2(15.0 - exponent)).astype(jnp.int32)
    wide = jnp.broadcast_to(exponent, (pad_rows, value.shape[-1])).astype(jnp.int32)
    return whole.astype(jnp.int16), wide.astype(jnp.int16)


def put_coded(ref, value, lead=()):
    rows = value.shape[0]
    whole, wide = encoded(value)
    ref[(*lead, slice(0, rows), slice(None))] = whole
    ref[(*lead, slice(rows, rows + pad_rows), slice(None))] = wide


def get_coded(ref, lead=()):
    rows = ref.shape[-2] - pad_rows
    whole = ref[(*lead, slice(0, rows), slice(None))].astype(jnp.int32).astype(jnp.float32)
    wide = ref[(*lead, slice(rows, rows + pad_rows), slice(None))].astype(jnp.int32)
    return whole * jnp.exp2(wide.astype(jnp.float32)[0:1, :] - 15.0)


def simple_call(body, args, in_specs, out_shape, out_specs, grid, prefetch=0, **more):
    size = sum(array.size * array.dtype.itemsize for array in args)
    return pl.pallas_call(
        body,
        grid_spec=pltpu.PrefetchScalarGridSpec(
            num_scalar_prefetch=prefetch,
            grid=grid,
            in_specs=in_specs,
            out_specs=out_specs,
            scratch_shapes=more.pop("scratch_shapes", ()),
        ),
        out_shape=out_shape,
        compiler_params=pltpu.CompilerParams(
            dimension_semantics=("arbitrary",) * len(grid), vmem_limit_bytes=48 << 20
        ),
        cost_estimate=pl.CostEstimate(flops=size, bytes_accessed=size, transcendentals=0),
        **more,
    )(*args)


def add_encode_body(shifts, lane, *refs):
    total = refs[2 * (shifts + 1)]
    total[...] = refs[0][...] + refs[1][...]
    for at in range(shifts):
        value = refs[2 * at + 2][...] + refs[2 * at + 3][...]
        put_coded(refs[2 * (shifts + 1) + 1 + at], value)


def add_encode(kept, other, lane, lanes):
    _, rows, width = kept.shape
    lane_step = step_of(width)
    in_specs, args = [], []
    for shift in range(lanes):
        spec = pl.BlockSpec(
            (None, rows, lane_step),
            lambda at, lane, shift=shift: (lax.rem(lane[0] + shift, lanes), 0, at),
        )
        in_specs += [spec, spec]
        args += [kept, other]
    out_specs = [pl.BlockSpec((rows, lane_step), lambda at, lane: (0, at))]
    out_shape = [jax.ShapeDtypeStruct((rows, width), jnp.float32)]
    for _ in range(1, lanes):
        out_specs.append(pl.BlockSpec((rows + pad_rows, lane_step), lambda at, lane: (0, at)))
        out_shape.append(jax.ShapeDtypeStruct((rows + pad_rows, width), jnp.int16))
    return simple_call(
        functools.partial(add_encode_body, lanes - 1), [lane, *args], in_specs,
        out_shape, out_specs, (width // lane_step,), 1,
    )


def split_dots(pairs):
    total = None
    for (left_head, left_tail), right in pairs:
        right_head = right.astype(jnp.bfloat16)
        right_tail = (right - right_head.astype(jnp.float32)).astype(jnp.bfloat16)
        for left, value in ((left_tail, right_head), (left_head, right_tail), (left_head, right_head)):
            part = jnp.dot(left, value, preferred_element_type=jnp.float32)
            total = part if total is None else total + part
    return total


def chain_body(node, lanes, *refs):
    mine, *received = refs[:lanes]
    heads = refs[lanes : lanes + node]
    tails = refs[lanes + node : lanes + 2 * node]
    earlier = refs[lanes + 2 * node : lanes + 3 * node]
    value, coded, turned = refs[-3:]
    total = mine[...]
    for ref in received:
        total = total + get_coded(ref)
    if node:
        total = total + split_dots(
            [((h[...], t[...]), e[...]) for h, t, e in zip(heads, tails, earlier, strict=True)]
        )
    total = -total
    value[...] = total
    put_coded(coded, total)
    turned[...] = total.T


def chain(node, nodes, mine, received, heads, tails, earlier, turned):
    rows, width = mine.shape
    lane_step = step_of(width)
    lanes = 1 + len(received)
    first = node * (node - 1) // 2
    column = lambda rows: pl.BlockSpec((rows, lane_step), lambda at: (0, at))
    in_specs = [column(rows)] + [column(rows + pad_rows)] * len(received)
    factor_specs = [
        pl.BlockSpec((None, rows, rows), lambda at, j=j: (first + j, 0, 0)) for j in range(node)
    ]
    in_specs += factor_specs + factor_specs + [column(rows)] * node
    args = [mine, *received, *[heads] * node, *[tails] * node, *earlier]
    aliases = {}
    if turned is not None:
        aliases = {len(args): 2}
        args.append(turned)
        in_specs.append(pl.BlockSpec(memory_space=pl.ANY))
    return simple_call(
        functools.partial(chain_body, node, lanes), args, in_specs,
        [
            jax.ShapeDtypeStruct((rows, width), jnp.float32),
            jax.ShapeDtypeStruct((rows + pad_rows, width), jnp.int16),
            jax.ShapeDtypeStruct((nodes, width, rows), jnp.float32),
        ],
        [
            column(rows),
            column(rows + pad_rows),
            pl.BlockSpec((None, lane_step, rows), lambda at: (node, at, 0)),
        ],
        (width // lane_step,), input_output_aliases=aliases,
    )


def turn_body(*refs):
    refs[-1][...] = get_coded(refs[0]).T


def turn(node, nodes, coded, turned):
    padded, width = coded.shape
    lane_step = step_of(width)
    rows = padded - pad_rows
    args, in_specs = [coded], [pl.BlockSpec((padded, lane_step), lambda at: (0, at))]
    aliases = {}
    if turned is not None:
        aliases = {1: 0}
        args.append(turned)
        in_specs.append(pl.BlockSpec(memory_space=pl.ANY))
    return simple_call(
        turn_body, args, in_specs,
        jax.ShapeDtypeStruct((nodes, width, rows), jnp.float32),
        pl.BlockSpec((None, lane_step, rows), lambda at: (node, at, 0)),
        (width // lane_step,), input_output_aliases=aliases,
    )


def inner_body(half, low, up, head, tail, rows, mine, given):
    value = split_dots([((head[...], tail[...]), rows[...])])

    @pl.when(pl.program_id(0) < half)
    def _():
        mine[...] = value

    @pl.when(pl.program_id(0) >= half)
    def _():
        given[...] = value


def inner(low, up, heads, tails, rows):
    nodes, piece, width = rows.shape
    count = nodes * (nodes + 1) // 2
    half = count // 2
    left = pl.BlockSpec((None, width, piece), lambda at, low, up: (low[at], 0, 0))
    shape = jax.ShapeDtypeStruct((half, width, width), jnp.float32)
    return simple_call(
        functools.partial(inner_body, half), [low, up, heads, tails, rows],
        [left, left, pl.BlockSpec((None, piece, width), lambda at, low, up: (up[at], 0, 0))],
        [shape, shape],
        [
            pl.BlockSpec((None, width, width), lambda at, *_: (jnp.minimum(at, half - 1), 0, 0)),
            pl.BlockSpec((None, width, width), lambda at, *_: (jnp.maximum(at - half, 0), 0, 0)),
        ],
        (count,), 2,
    )


def share_body(count, received, *refs):
    total = refs[0][...]
    for ref in refs[1 : 1 + received]:
        total = total + get_coded(ref)
    rows = total.shape[0] // count
    for at in range(count):
        put_coded(refs[-1], total[at * rows : (at + 1) * rows, :], (at,))


def share(mine, received, count):
    rows, width = mine.shape
    lane_step = step_of(width)
    column = lambda rows: pl.BlockSpec((rows, lane_step), lambda at: (0, at))
    return simple_call(
        functools.partial(share_body, count, len(received)), [mine, *received],
        [column(rows)] + [column(rows + pad_rows)] * len(received),
        jax.ShapeDtypeStruct((count, rows // count + pad_rows, width), jnp.int16),
        pl.BlockSpec((count, rows // count + pad_rows, lane_step), lambda at: (0, 0, at)),
        (width // lane_step,),
    )


def collect_body(count, source, out):
    total = get_coded(source, (0,))
    for at in range(1, count):
        total = total + get_coded(source, (at,))
    whole, wide = encoded(total)
    rows = total.shape[0]
    for at in range(count):
        out[at, :rows, :] = whole
        out[at, rows:, :] = wide


def collect(parts):
    count, padded, width = parts.shape
    lane_step = step_of(width)
    spec = pl.BlockSpec((count, padded, lane_step), lambda at: (0, 0, at))
    return simple_call(
        functools.partial(collect_body, count), [parts], [spec],
        jax.ShapeDtypeStruct(parts.shape, jnp.int16), spec, (width // lane_step,),
    )


def finish_body(lanes, nodes, width, place, *refs):
    parts = refs[: 2 * lanes]
    base, out, sums = refs[2 * lanes :]
    step = pl.program_id(0)
    count, padded, _ = parts[0].shape
    rows = padded - pad_rows

    @pl.when(step == 0)
    def _():
        for at, ref in enumerate(parts):
            first = place[at] * (count * rows)
            for piece in range(count):
                start = pl.multiple_of(first + piece * rows, 8)
                sums[pl.ds(start, rows), :] = get_coded(ref, (piece,))

    row, col = step // nodes, step % nodes
    low, up = jnp.minimum(row, col), jnp.maximum(row, col)
    start = pl.multiple_of((up * (up + 1) // 2 + low) * width, width)
    value = base[...] - sums[pl.ds(start, width), :]

    @pl.when(row <= col)
    def _():
        out[...] = value

    @pl.when(row > col)
    def _():
        out[...] = value.T


def finish(place, parts, base, nodes, width):
    lanes = len(parts) // 2

    def base_map(step, place):
        row, col = step // nodes, step % nodes
        low, up = jnp.minimum(row, col), jnp.maximum(row, col)
        return (up * (up + 1) // 2 + low, 0, 0)

    whole = pl.BlockSpec(parts[0].shape, lambda step, place: (0, 0, 0))
    return simple_call(
        functools.partial(finish_body, lanes, nodes, width), [place, *parts, base],
        [whole] * len(parts) + [pl.BlockSpec((None, width, width), base_map)],
        jax.ShapeDtypeStruct((nodes, nodes, width, width), jnp.float32),
        pl.BlockSpec(
            (None, None, width, width), lambda step, place: (step // nodes, step % nodes, 0, 0)
        ),
        (nodes * nodes,), 1,
        scratch_shapes=[pltpu.VMEM((nodes * (nodes + 1) // 2 * width, width), jnp.float32)],
    )


def local(ancestor_inverse, factor, coupling, diagonal_inverse, ancestors):
    row_count = lax.axis_size("row")
    col_count = lax.axis_size("col")
    total = row_count * col_count
    row_index = lax.axis_index("row")
    col_index = lax.axis_index("col")
    flat_index = row_index * col_count + col_index
    nodes, piece_rows, width = factor.shape
    col_bits = col_count.bit_length() - 1
    block_of_row = (flat_index * piece_rows + jnp.arange(piece_rows, dtype=jnp.int32)) // width
    listed = jnp.any(ancestors[:, :, None] == block_of_row[None, None, :], axis=1)
    lower = jnp.where(listed[:, :, None], factor, jnp.zeros_like(factor))
    lower = [lower[node].T for node in range(nodes)]

    order = ring_order(col_count)
    sources = ring_sources(order, col_index)
    core = (row_index % 2).reshape(1).astype(jnp.int32)
    moves = ring_moves(order)
    lanes = row_count // 2
    steps = col_count // 2
    near, early = 3, 1 + 2 * (steps - 2)
    gathered = [[lower[node]] for node in range(nodes)]

    def advance(step):
        for node in range(nodes):
            gathered[node] = ring_step(gathered[node], moves, step == steps)

    for step in range(1, steps - 1):
        advance(step)

    early_coupling = after(coupling, gathered[0][1])
    turned_heads, turned_tails = split_terms(jnp.swapaxes(early_coupling, 1, 2))
    mixed = []
    for k in range(nodes):
        value = lower[k].astype(jnp.float32)
        for j in range(k):
            value = value - left_dot(early_coupling[pair_index(k, j)], mixed[j])
        mixed.append(value)
    mixed_heads, mixed_tails = split_terms(jnp.stack(mixed))

    first_pieces = [group[:near] for group in gathered]
    first_pieces[0][0], turned_heads, turned_tails, mixed_heads, mixed_tails = (
        lax.optimization_barrier(
            (first_pieces[0][0], turned_heads, turned_tails, mixed_heads, mixed_tails)
        )
    )
    starts = partial_product(first_pieces, ancestor_inverse, sources[:near])
    advance(steps - 1)
    starts = partial_product(
        [group[near:early] for group in gathered],
        ancestor_inverse,
        sources[near:early],
        starts,
    )
    advance(steps)

    swap = (1 << col_bits) | 1

    def middle(at):
        low, up = at & 1, (at >> col_bits) & 1
        return at if low == up else at ^ swap

    first_moves = [(at, middle(at)) for at in range(total)]
    last_moves = [
        (middle(r * col_count + c), c * row_count + r)
        for r in range(row_count)
        for c in range(col_count)
    ]
    lane = row_index // 2
    lane_ref = lane.reshape(1).astype(jnp.int32)
    sibling = [(at, at ^ 1) for at in range(row_count)]
    lane_moves = [
        [(at, (at + 2 * shift) % row_count) for at in range(row_count)]
        for shift in range(1, lanes)
    ]

    def lane_sums(given, kept):
        other = lax.ppermute(given, "row", sibling)
        mine, *coded = add_encode(kept, other, lane_ref, lanes)
        return mine, [
            lax.ppermute(part, "row", moves)
            for part, moves in zip(coded, lane_moves, strict=True)
        ]

    by_cols = []
    out_cols = out_rows = None
    for k in range(nodes):
        given, kept = final_product(
            k, gathered[k][early:], ancestor_inverse, sources[early:], core, lanes, starts
        )
        row_sums = lane_sums(given, kept)
        value, coded, out_cols = chain(
            k, nodes, *row_sums, turned_heads, turned_tails, by_cols, out_cols
        )
        by_cols.append(value)
        coded = lax.ppermute(coded, both, first_moves)
        coded = lax.ppermute(coded, both, last_moves)
        out_rows = turn(k, nodes, coded, out_rows)

    coupling, diagonal_inverse = lax.optimization_barrier(
        (coupling, diagonal_inverse, by_cols[-1])
    )[:2]

    def g(later, earlier):
        return coupling[pair_index(later, earlier)]

    base = {}
    for k in range(nodes):
        for j in range(k):
            value = -matmul(base[j, 0], g(k, 0))
            for i in range(1, k):
                value = value - matmul(base[j, i], g(k, i))
            base[j, k] = value
            base[k, j] = value.T
        value = diagonal_inverse[k]
        for j in range(k):
            value = value - left_dot(g(k, j), base[j, k])
        base[k, k] = value
    base = jnp.stack([base[j, k] for k in range(nodes) for j in range(k + 1)])

    count = nodes * (nodes + 1) // 2
    listing = [(j, k) for k in range(nodes) for j in range(k + 1)]
    turn_to = (core[0] * (count // 2) + jnp.arange(count, dtype=jnp.int32)) % count
    low = jnp.asarray([j for j, _ in listing], jnp.int32)[turn_to]
    up = jnp.asarray([k for _, k in listing], jnp.int32)[turn_to]
    kept, given = inner(low, up, mixed_heads, mixed_tails, out_rows)
    part_rows = kept.shape[0] * width // lanes
    mine, received = lane_sums(
        given.reshape(lanes, part_rows, width), kept.reshape(lanes, part_rows, width)
    )
    shared = share(mine, received, col_count)
    summed = collect(lax.all_to_all(shared, "col", 0, 0, tiled=True))
    summed = lax.all_to_all(summed, "col", 0, 0, tiled=True)
    pieces = [summed] + [lax.ppermute(summed, "row", moves) for moves in lane_moves]
    summed_all = pieces + [lax.ppermute(piece, "row", sibling) for piece in pieces]
    shifts = [(lane - shift) % lanes for shift in range(lanes)]
    place = jnp.stack(
        [core[0] * lanes + at for at in shifts] + [(1 - core[0]) * lanes + at for at in shifts]
    ).astype(jnp.int32)
    summed_all[0], base = lax.optimization_barrier((summed_all[0], base))
    node_blocks = finish(place, summed_all, base, nodes, width)
    return out_rows, out_cols, node_blocks


def solution(mesh):
    placed = (P("row", "col"), P(None, both, None), P(), P(), P())

    return jax.shard_map(
        local,
        mesh=mesh,
        in_specs=placed,
        out_specs=(P(None, both, None), P(None, ("col", "row"), None), P()),
        check_vma=False,
    )
```

```python
import functools

import jax
import jax.numpy as jnp
from jax import lax
from jax.experimental import pallas as pl
from jax.experimental.pallas import tpu as pltpu
from jax.sharding import PartitionSpec as P

both = ("row", "col")
high = lax.Precision.HIGH


def matmul(left, right):
    return jnp.dot(left, right, precision=high)


def left_dot(left, right):
    return lax.dot_general(left, right, (((0,), (0,)), ((), ())), precision=high)


def pair_index(later, earlier):
    return later * (later - 1) // 2 + earlier


def split_terms(value):
    head = lax.reduce_precision(value, 8, 7)
    return head.astype(jnp.bfloat16), (value - head).astype(jnp.bfloat16)


def after(value, *others):
    return lax.optimization_barrier((value, *others))[0]


def ring_order(count):
    return list(range(0, count, 2)) + list(range(count - 1, 0, -2))


def ring_moves(order):
    count = len(order)
    ahead = [(order[at], order[(at + 1) % count]) for at in range(count)]
    return ahead, [(target, source) for source, target in ahead]


def ring_step(pieces, moves, last):
    up, down = (pieces[0], pieces[0]) if len(pieces) == 1 else pieces[-2:]
    if last:
        half = up.shape[0] // 2
        up, down = up[:half], down[half:]
    return [*pieces, lax.ppermute(up, "col", moves[0]), lax.ppermute(down, "col", moves[1])]


def ring_sources(order, col_index):
    count = len(order)
    place = [0] * count
    for at, device in enumerate(order):
        place[device] = at
    my_place = jnp.asarray(place, jnp.int32)[col_index]
    table = jnp.asarray(order, jnp.int32)
    steps = [0]
    for step in range(1, count // 2):
        steps += [-step, step]
    steps.append(count // 2)
    return table[(my_place + jnp.asarray(steps, jnp.int32)) % count]


def two_terms(block):
    value = block[...]
    head = value.astype(jnp.bfloat16)
    tail = (value - head.astype(jnp.float32)).astype(jnp.bfloat16)
    return jnp.concatenate([head, tail], axis=0)


def put_double(doubled, piece, span=slice(None)):
    depth = piece.shape[1]
    doubled[span, :depth] = piece[...]
    doubled[span, depth:] = piece[...]


def partial_body(nodes, count, resume, sources, *refs):
    pieces = refs[: nodes * count]
    block = refs[nodes * count]
    total, doubled = refs[-2:]
    node, step = pl.program_id(0), pl.program_id(1)
    for at, piece in enumerate(pieces):

        @pl.when((node == at // count) & (step == at % count))
        def _(piece=piece):
            put_double(doubled, piece)

    part = jnp.dot(doubled[...], two_terms(block), preferred_element_type=jnp.float32)

    @pl.when(step == 0)
    def _():
        total[...] = refs[nodes * count + 1][...] + part if resume else part

    @pl.when(step > 0)
    def _():
        total[...] += part


def final_body(count, lanes, out_piece, sources, core, *refs):
    pieces = refs[: count + 1]
    block, start, given, kept, total, doubled = refs[count + 1 :]
    step = pl.program_id(0)
    for at in range(count - 1):

        @pl.when(step == at)
        def _(at=at):
            put_double(doubled, pieces[at])

    @pl.when(step == count - 1)
    def _():
        half = pieces[count].shape[0]
        put_double(doubled, pieces[count - 1], slice(0, half))
        put_double(doubled, pieces[count], slice(half, 2 * half))

    part = jnp.dot(doubled[...], two_terms(block), preferred_element_type=jnp.float32)

    @pl.when(step == 0)
    def _():
        total[...] = start[...] + part

    @pl.when(step > 0)
    def _():
        total[...] += part

    @pl.when(step == count - 1)
    def _():
        for lane in range(lanes):
            for side in range(2):
                first = (2 * lane + side) * out_piece

                @pl.when(core[0] == side)
                def _(lane=lane, first=first):
                    kept[lane] = total[:, first : first + out_piece]

                @pl.when(core[0] != side)
                def _(lane=lane, first=first):
                    given[lane] = total[:, first : first + out_piece]


def product_call(body, grid, prefetch, args, in_specs, out_shape, out_specs, scratch, flops, **more):
    return pl.pallas_call(
        body,
        grid_spec=pltpu.PrefetchScalarGridSpec(
            num_scalar_prefetch=prefetch,
            grid=grid,
            in_specs=in_specs,
            out_specs=out_specs,
            scratch_shapes=scratch,
        ),
        out_shape=out_shape,
        compiler_params=pltpu.CompilerParams(
            dimension_semantics=("arbitrary",) * len(grid), vmem_limit_bytes=56 << 20
        ),
        cost_estimate=pl.CostEstimate(
            flops=flops, bytes_accessed=flops // 512, transcendentals=0
        ),
        **more,
    )(*args)


def partial_product(groups, block, sources, start=None):
    nodes, count = len(groups), len(groups[0])
    width, piece = groups[0][0].shape
    cols = block.shape[1]
    pieces = [array for group in groups for array in group]
    total = pl.BlockSpec((None, width, cols), lambda node, step, sources: (node, 0, 0))
    in_specs = [pl.BlockSpec(pieces[0].shape, lambda node, step, sources: (0, 0))] * len(pieces)
    in_specs.append(pl.BlockSpec((piece, cols), lambda node, step, sources: (sources[step], 0)))
    args = [sources, *pieces, block]
    aliases = {}
    if start is not None:
        aliases = {len(args): 0}
        in_specs.append(total)
        args.append(start)
    return product_call(
        functools.partial(partial_body, nodes, count, start is not None),
        (nodes, count), 1, args, in_specs,
        jax.ShapeDtypeStruct((nodes, width, cols), jnp.float32), total,
        [pltpu.VMEM((width, 2 * piece), jnp.bfloat16)],
        4 * nodes * count * width * piece * cols, input_output_aliases=aliases,
    )


def final_product(node, pieces, block, sources, core, lanes, start):
    count = len(pieces) - 1
    width, piece = pieces[0].shape
    cols = block.shape[1]
    out_piece = cols // (2 * lanes)
    half = jax.ShapeDtypeStruct((lanes, width, out_piece), jnp.float32)
    half_spec = pl.BlockSpec(half.shape, lambda step, *_: (0, 0, 0))
    in_specs = [pl.BlockSpec(array.shape, lambda step, *_: (0, 0)) for array in pieces]
    in_specs.append(pl.BlockSpec((piece, cols), lambda step, sources, core: (sources[step], 0)))
    in_specs.append(pl.BlockSpec((None, width, cols), lambda step, *_: (node, 0, 0)))
    return product_call(
        functools.partial(final_body, count, lanes, out_piece), (count,), 2,
        [sources, core, *pieces, block, start], in_specs, [half, half], [half_spec, half_spec],
        [pltpu.VMEM((width, cols), jnp.float32), pltpu.VMEM((width, 2 * piece), jnp.bfloat16)],
        4 * count * width * piece * cols,
    )


pad_rows = 16


def step_of(lanes):
    return 128 if lanes % 128 == 0 else lanes


def encoded(value):
    top = jnp.max(jnp.abs(value), axis=-2, keepdims=True)
    exponent = jnp.ceil(jnp.log2(jnp.maximum(top, 1e-30)) + 0.01)
    whole = jnp.round(value * jnp.exp2(15.0 - exponent)).astype(jnp.int32)
    wide = jnp.broadcast_to(exponent, (pad_rows, value.shape[-1])).astype(jnp.int32)
    return whole.astype(jnp.int16), wide.astype(jnp.int16)


def put_coded(ref, value, lead=()):
    rows = value.shape[0]
    whole, wide = encoded(value)
    ref[(*lead, slice(0, rows), slice(None))] = whole
    ref[(*lead, slice(rows, rows + pad_rows), slice(None))] = wide


def get_coded(ref, lead=()):
    rows = ref.shape[-2] - pad_rows
    whole = ref[(*lead, slice(0, rows), slice(None))].astype(jnp.int32).astype(jnp.float32)
    wide = ref[(*lead, slice(rows, rows + pad_rows), slice(None))].astype(jnp.int32)
    return whole * jnp.exp2(wide.astype(jnp.float32)[0:1, :] - 15.0)


def simple_call(body, args, in_specs, out_shape, out_specs, grid, prefetch=0, **more):
    size = sum(array.size * array.dtype.itemsize for array in args)
    return pl.pallas_call(
        body,
        grid_spec=pltpu.PrefetchScalarGridSpec(
            num_scalar_prefetch=prefetch,
            grid=grid,
            in_specs=in_specs,
            out_specs=out_specs,
            scratch_shapes=more.pop("scratch_shapes", ()),
        ),
        out_shape=out_shape,
        compiler_params=pltpu.CompilerParams(
            dimension_semantics=("arbitrary",) * len(grid), vmem_limit_bytes=48 << 20
        ),
        cost_estimate=pl.CostEstimate(flops=size, bytes_accessed=size, transcendentals=0),
        **more,
    )(*args)


def add_encode_body(shifts, lane, *refs):
    total = refs[2 * (shifts + 1)]
    total[...] = refs[0][...] + refs[1][...]
    for at in range(shifts):
        value = refs[2 * at + 2][...] + refs[2 * at + 3][...]
        put_coded(refs[2 * (shifts + 1) + 1 + at], value)


def add_encode(kept, other, lane, lanes):
    _, rows, width = kept.shape
    lane_step = step_of(width)
    in_specs, args = [], []
    for shift in range(lanes):
        spec = pl.BlockSpec(
            (None, rows, lane_step),
            lambda at, lane, shift=shift: (lax.rem(lane[0] + shift, lanes), 0, at),
        )
        in_specs += [spec, spec]
        args += [kept, other]
    out_specs = [pl.BlockSpec((rows, lane_step), lambda at, lane: (0, at))]
    out_shape = [jax.ShapeDtypeStruct((rows, width), jnp.float32)]
    for _ in range(1, lanes):
        out_specs.append(pl.BlockSpec((rows + pad_rows, lane_step), lambda at, lane: (0, at)))
        out_shape.append(jax.ShapeDtypeStruct((rows + pad_rows, width), jnp.int16))
    return simple_call(
        functools.partial(add_encode_body, lanes - 1), [lane, *args], in_specs,
        out_shape, out_specs, (width // lane_step,), 1,
    )


def split_dots(pairs):
    total = None
    for (left_head, left_tail), right in pairs:
        right_head = right.astype(jnp.bfloat16)
        right_tail = (right - right_head.astype(jnp.float32)).astype(jnp.bfloat16)
        for left, value in ((left_tail, right_head), (left_head, right_tail), (left_head, right_head)):
            part = jnp.dot(left, value, preferred_element_type=jnp.float32)
            total = part if total is None else total + part
    return total


def chain_body(node, lanes, *refs):
    mine, *received = refs[:lanes]
    heads = refs[lanes : lanes + node]
    tails = refs[lanes + node : lanes + 2 * node]
    earlier = refs[lanes + 2 * node : lanes + 3 * node]
    value, coded, turned = refs[-3:]
    total = mine[...]
    for ref in received:
        total = total + get_coded(ref)
    if node:
        total = total + split_dots(
            [((h[...], t[...]), e[...]) for h, t, e in zip(heads, tails, earlier, strict=True)]
        )
    total = -total
    value[...] = total
    put_coded(coded, total)
    turned[...] = total.T


def chain(node, nodes, mine, received, heads, tails, earlier, turned):
    rows, width = mine.shape
    lane_step = step_of(width)
    lanes = 1 + len(received)
    first = node * (node - 1) // 2
    column = lambda rows: pl.BlockSpec((rows, lane_step), lambda at: (0, at))
    in_specs = [column(rows)] + [column(rows + pad_rows)] * len(received)
    factor_specs = [
        pl.BlockSpec((None, rows, rows), lambda at, j=j: (first + j, 0, 0)) for j in range(node)
    ]
    in_specs += factor_specs + factor_specs + [column(rows)] * node
    args = [mine, *received, *[heads] * node, *[tails] * node, *earlier]
    aliases = {}
    if turned is not None:
        aliases = {len(args): 2}
        args.append(turned)
        in_specs.append(pl.BlockSpec(memory_space=pl.ANY))
    return simple_call(
        functools.partial(chain_body, node, lanes), args, in_specs,
        [
            jax.ShapeDtypeStruct((rows, width), jnp.float32),
            jax.ShapeDtypeStruct((rows + pad_rows, width), jnp.int16),
            jax.ShapeDtypeStruct((nodes, width, rows), jnp.float32),
        ],
        [
            column(rows),
            column(rows + pad_rows),
            pl.BlockSpec((None, lane_step, rows), lambda at: (node, at, 0)),
        ],
        (width // lane_step,), input_output_aliases=aliases,
    )


def turn_body(*refs):
    refs[-1][...] = get_coded(refs[0]).T


def turn(node, nodes, coded, turned):
    padded, width = coded.shape
    lane_step = step_of(width)
    rows = padded - pad_rows
    args, in_specs = [coded], [pl.BlockSpec((padded, lane_step), lambda at: (0, at))]
    aliases = {}
    if turned is not None:
        aliases = {1: 0}
        args.append(turned)
        in_specs.append(pl.BlockSpec(memory_space=pl.ANY))
    return simple_call(
        turn_body, args, in_specs,
        jax.ShapeDtypeStruct((nodes, width, rows), jnp.float32),
        pl.BlockSpec((None, lane_step, rows), lambda at: (node, at, 0)),
        (width // lane_step,), input_output_aliases=aliases,
    )


def inner_body(half, low, up, left, rows, mine, given):
    value = rows[...]
    head = value.astype(jnp.bfloat16)
    tail = (value - head.astype(jnp.float32)).astype(jnp.bfloat16)
    value = jnp.dot(
        left[...], jnp.concatenate([head, tail, head], axis=0), preferred_element_type=jnp.float32
    )

    @pl.when(pl.program_id(0) < half)
    def _():
        mine[...] = value

    @pl.when(pl.program_id(0) >= half)
    def _():
        given[...] = value


def inner(low, up, left, rows):
    nodes, piece, width = rows.shape
    count = nodes * (nodes + 1) // 2
    half = count // 2
    shape = jax.ShapeDtypeStruct((half, width, width), jnp.float32)
    return simple_call(
        functools.partial(inner_body, half), [low, up, left, rows],
        [
            pl.BlockSpec((None, width, left.shape[2]), lambda at, low, up: (low[at], 0, 0)),
            pl.BlockSpec((None, piece, width), lambda at, low, up: (up[at], 0, 0)),
        ],
        [shape, shape],
        [
            pl.BlockSpec((None, width, width), lambda at, *_: (jnp.minimum(at, half - 1), 0, 0)),
            pl.BlockSpec((None, width, width), lambda at, *_: (jnp.maximum(at - half, 0), 0, 0)),
        ],
        (count,), 2,
    )


def deal_body(plain, coded, count, starts, *refs):
    total = refs[0][...]
    for ref in refs[1:plain]:
        total = total + ref[...]
    for ref in refs[plain : plain + coded]:
        total = total + get_coded(ref)
    outs = refs[plain + coded :]
    if count == 1:
        put_coded(outs[0], total)
        return
    whole = outs[-1]
    whole[...] = total
    rows = total.shape[0] // count
    for at in range(count):
        part = whole[pl.ds(pl.multiple_of(starts[at], 8), rows), :]
        if at == 0:
            outs[0][...] = part
        else:
            put_coded(outs[at], part)


def deal(plain, coded, starts):
    rows, width = plain[0].shape
    lane_step = step_of(width)
    count = starts.shape[0]
    column = lambda rows: pl.BlockSpec((rows, lane_step), lambda at, starts: (0, at))
    part = rows // count
    shapes = [jax.ShapeDtypeStruct((part, width), jnp.float32)] if count > 1 else []
    shapes += [jax.ShapeDtypeStruct((part + pad_rows, width), jnp.int16)] * max(count - 1, 1)
    return simple_call(
        functools.partial(deal_body, len(plain), len(coded), count),
        [starts, *plain, *coded],
        [column(rows)] * len(plain) + [column(rows + pad_rows)] * len(coded),
        shapes, [column(shape.shape[0]) for shape in shapes], (width // lane_step,), 1,
        scratch_shapes=[pltpu.VMEM((rows, lane_step), jnp.float32)] if count > 1 else [],
    )


def heap_body(*refs):
    for at, ref in enumerate(refs[:-1]):
        refs[-1][at] = ref[...]


def heap(parts):
    rows, width = parts[0].shape
    lane_step = step_of(width)
    return simple_call(
        heap_body, parts,
        [pl.BlockSpec((rows, lane_step), lambda at: (0, at))] * len(parts),
        jax.ShapeDtypeStruct((len(parts), rows, width), parts[0].dtype),
        pl.BlockSpec((len(parts), rows, lane_step), lambda at: (0, 0, at)),
        (width // lane_step,),
    )


def finish_body(arrays, nodes, width, place, *refs):
    parts = refs[:arrays]
    base, out, sums = refs[arrays:]
    step = pl.program_id(0)
    count, padded, _ = parts[0].shape
    rows = padded - pad_rows

    @pl.when(step == 0)
    def _():
        for at, ref in enumerate(parts):
            for piece in range(count):
                start = pl.multiple_of(place[at * count + piece], 8)
                sums[pl.ds(start, rows), :] = get_coded(ref, (piece,))

    row, col = step // nodes, step % nodes
    low, up = jnp.minimum(row, col), jnp.maximum(row, col)
    start = pl.multiple_of((up * (up + 1) // 2 + low) * width, width)
    value = base[...] - sums[pl.ds(start, width), :]

    @pl.when(row <= col)
    def _():
        out[...] = value

    @pl.when(row > col)
    def _():
        out[...] = value.T


def finish(place, parts, base, nodes, width):
    def base_map(step, place):
        row, col = step // nodes, step % nodes
        low, up = jnp.minimum(row, col), jnp.maximum(row, col)
        return (up * (up + 1) // 2 + low, 0, 0)

    whole = pl.BlockSpec(parts[0].shape, lambda step, place: (0, 0, 0))
    return simple_call(
        functools.partial(finish_body, len(parts), nodes, width), [place, *parts, base],
        [whole] * len(parts) + [pl.BlockSpec((None, width, width), base_map)],
        jax.ShapeDtypeStruct((nodes, nodes, width, width), jnp.float32),
        pl.BlockSpec(
            (None, None, width, width), lambda step, place: (step // nodes, step % nodes, 0, 0)
        ),
        (nodes * nodes,), 1,
        scratch_shapes=[pltpu.VMEM((nodes * (nodes + 1) // 2 * width, width), jnp.float32)],
    )


def spread_bits(number, bits):
    return sum(((number >> at) & 1) << bit for at, bit in enumerate(bits))


def gather_bits(index, bits):
    return sum(((index >> bit) & 1) << at for at, bit in enumerate(bits))


def local(ancestor_inverse, factor, coupling, diagonal_inverse, ancestors):
    row_count = lax.axis_size("row")
    col_count = lax.axis_size("col")
    total = row_count * col_count
    row_index = lax.axis_index("row")
    col_index = lax.axis_index("col")
    flat_index = row_index * col_count + col_index
    nodes, piece_rows, width = factor.shape
    col_bits = col_count.bit_length() - 1
    block_of_row = (flat_index * piece_rows + jnp.arange(piece_rows, dtype=jnp.int32)) // width
    listed = jnp.any(ancestors[:, :, None] == block_of_row[None, None, :], axis=1)
    lower = jnp.where(listed[:, :, None], factor, jnp.zeros_like(factor))
    lower = [lower[node].T for node in range(nodes)]

    order = ring_order(col_count)
    sources = ring_sources(order, col_index)
    core = (row_index % 2).reshape(1).astype(jnp.int32)
    moves = ring_moves(order)
    lanes = row_count // 2
    steps = col_count // 2
    near, early = 3, 1 + 2 * (steps - 2)
    gathered = [[lower[node]] for node in range(nodes)]

    def advance(step):
        for node in range(nodes):
            gathered[node] = ring_step(gathered[node], moves, step == steps)

    for step in range(1, steps - 1):
        advance(step)

    early_coupling = after(coupling, gathered[0][1])
    turned_heads, turned_tails = split_terms(jnp.swapaxes(early_coupling, 1, 2))
    first_pieces = [group[:near] for group in gathered]
    first_pieces[0][0], turned_heads, turned_tails = lax.optimization_barrier(
        (first_pieces[0][0], turned_heads, turned_tails)
    )
    starts = partial_product(first_pieces, ancestor_inverse, sources[:near])
    advance(steps - 1)
    starts = partial_product(
        [group[near:early] for group in gathered],
        ancestor_inverse,
        sources[near:early],
        starts,
    )
    advance(steps)

    swap = (1 << col_bits) | 1

    def middle(at):
        low, up = at & 1, (at >> col_bits) & 1
        return at if low == up else at ^ swap

    first_moves = [(at, middle(at)) for at in range(total)]
    last_moves = [
        (middle(r * col_count + c), c * row_count + r)
        for r in range(row_count)
        for c in range(col_count)
    ]
    lane = row_index // 2
    lane_ref = lane.reshape(1).astype(jnp.int32)
    sibling = [(at, at ^ 1) for at in range(row_count)]
    lane_moves = [
        [(at, (at + 2 * shift) % row_count) for at in range(row_count)]
        for shift in range(1, lanes)
    ]

    def lane_sums(given, kept):
        other = lax.ppermute(given, "row", sibling)
        mine, *coded = add_encode(kept, other, lane_ref, lanes)
        return mine, [
            lax.ppermute(part, "row", moves)
            for part, moves in zip(coded, lane_moves, strict=True)
        ]

    by_cols = []
    out_cols = out_rows = None
    for k in range(nodes):
        given, kept = final_product(
            k, gathered[k][early:], ancestor_inverse, sources[early:], core, lanes, starts
        )
        row_sums = lane_sums(given, kept)
        value, coded, out_cols = chain(
            k, nodes, *row_sums, turned_heads, turned_tails, by_cols, out_cols
        )
        by_cols.append(value)
        coded = lax.ppermute(coded, both, first_moves)
        coded = lax.ppermute(coded, both, last_moves)
        out_rows = turn(k, nodes, coded, out_rows)

    late_coupling = after(coupling, by_cols[-2])
    mixed = []
    for k in range(nodes):
        value = lower[k].astype(jnp.float32)
        for j in range(k):
            value = value - left_dot(late_coupling[pair_index(k, j)], mixed[j])
        mixed.append(value)
    head, tail = split_terms(jnp.stack(mixed))
    left = jnp.concatenate([tail, head, head], axis=2)

    coupling, diagonal_inverse = lax.optimization_barrier(
        (coupling, diagonal_inverse, by_cols[-1])
    )[:2]

    def g(later, earlier):
        return coupling[pair_index(later, earlier)]

    base = {}
    for k in range(nodes):
        for j in range(k):
            value = -matmul(base[j, 0], g(k, 0))
            for i in range(1, k):
                value = value - matmul(base[j, i], g(k, i))
            base[j, k] = value
            base[k, j] = value.T
        value = diagonal_inverse[k]
        for j in range(k):
            value = value - left_dot(g(k, j), base[j, k])
        base[k, k] = value
    base = jnp.stack([base[j, k] for k in range(nodes) for j in range(k + 1)])

    count = nodes * (nodes + 1) // 2
    listing = [(j, k) for k in range(nodes) for j in range(k + 1)]
    turn_to = (core[0] * (count // 2) + jnp.arange(count, dtype=jnp.int32)) % count
    low = jnp.asarray([j for j, _ in listing], jnp.int32)[turn_to]
    up = jnp.asarray([k for _, k in listing], jnp.int32)[turn_to]
    kept, given = inner(low, up, left, out_rows)
    half_rows = kept.shape[0] * width
    kept, given = kept.reshape(half_rows, width), given.reshape(half_rows, width)
    flat_bits = (row_count * col_count).bit_length() - 1
    planes = [[0, *range(col_bits + 1, flat_bits)], list(range(1, col_bits))]
    plane_moves = [
        [[(at, at ^ spread_bits(other, bits)) for at in range(total)] for other in range(1, 1 << len(bits))]
        for bits in planes
    ]
    parts_of = [1 << len(bits) for bits in planes]
    mine_of = [gather_bits(flat_index, bits) for bits in planes]

    def starts_of(level, rows):
        around = mine_of[level] ^ jnp.arange(parts_of[level], dtype=jnp.int32)
        return (around * (rows // parts_of[level])).astype(jnp.int32)

    def exchange(arrays, level):
        return [
            lax.ppermute(array, both, moves)
            for array, moves in zip(arrays, plane_moves[level], strict=True)
        ]

    other = lax.ppermute(given, "row", sibling)
    mine, *coded = deal([kept, other], [], starts_of(0, half_rows))
    coded = exchange(coded, 0)
    mine, *coded = deal([mine], coded, starts_of(1, mine.shape[0]))
    coded = exchange(coded, 1)
    (summed,) = deal([mine], coded, jnp.zeros((1,), jnp.int32))
    pile = heap([summed, *exchange([summed] * (parts_of[1] - 1), 1)])
    piles = [pile, *exchange([pile] * (parts_of[0] - 1), 0)]
    piles += [lax.ppermute(pile, "row", sibling) for pile in piles]
    rows_at = half_rows // (parts_of[0] * parts_of[1])
    around = [mine_of[at] ^ jnp.arange(parts_of[at], dtype=jnp.int32) for at in range(2)]
    within = (around[0][:, None] * parts_of[1] + around[1][None, :]).reshape(-1) * rows_at
    place = jnp.concatenate(
        [core[0] * half_rows + within, (1 - core[0]) * half_rows + within]
    ).astype(jnp.int32)
    pile, base = lax.optimization_barrier((piles[0], base))
    node_blocks = finish(place, [pile, *piles[1:]], base, nodes, width)
    return out_rows, out_cols, node_blocks


def solution(mesh):
    placed = (P("row", "col"), P(None, both, None), P(), P(), P())

    return jax.shard_map(
        local,
        mesh=mesh,
        in_specs=placed,
        out_specs=(P(None, both, None), P(None, ("col", "row"), None), P()),
        check_vma=False,
    )
```

```python
import functools

import jax
import jax.numpy as jnp
from jax import lax
from jax.experimental import pallas as pl
from jax.experimental.pallas import tpu as pltpu
from jax.sharding import PartitionSpec as P

both = ("row", "col")
high = lax.Precision.HIGH


def matmul(left, right):
    return jnp.dot(left, right, precision=high)


def left_dot(left, right):
    return lax.dot_general(left, right, (((0,), (0,)), ((), ())), precision=high)


def pair_index(later, earlier):
    return later * (later - 1) // 2 + earlier


def split_terms(value):
    head = lax.reduce_precision(value, 8, 7)
    return head.astype(jnp.bfloat16), (value - head).astype(jnp.bfloat16)


def after(value, *others):
    return lax.optimization_barrier((value, *others))[0]


def ring_order(count):
    return list(range(0, count, 2)) + list(range(count - 1, 0, -2))


def ring_moves(order):
    count = len(order)
    ahead = [(order[at], order[(at + 1) % count]) for at in range(count)]
    return ahead, [(target, source) for source, target in ahead]


def ring_step(pieces, moves, last):
    up, down = (pieces[0], pieces[0]) if len(pieces) == 1 else pieces[-2:]
    if last:
        half = up.shape[0] // 2
        up, down = up[:half], down[half:]
    return [*pieces, lax.ppermute(up, "col", moves[0]), lax.ppermute(down, "col", moves[1])]


def ring_sources(order, col_index):
    count = len(order)
    place = [0] * count
    for at, device in enumerate(order):
        place[device] = at
    my_place = jnp.asarray(place, jnp.int32)[col_index]
    table = jnp.asarray(order, jnp.int32)
    steps = [0]
    for step in range(1, count // 2):
        steps += [-step, step]
    steps.append(count // 2)
    return table[(my_place + jnp.asarray(steps, jnp.int32)) % count]


def two_terms(block):
    value = block[...]
    head = value.astype(jnp.bfloat16)
    tail = (value - head.astype(jnp.float32)).astype(jnp.bfloat16)
    return jnp.concatenate([head, tail], axis=0)


def put_double(doubled, piece, span=slice(None)):
    depth = piece.shape[1]
    doubled[span, :depth] = piece[...]
    doubled[span, depth:] = piece[...]


def partial_body(nodes, count, resume, sources, *refs):
    pieces = refs[: nodes * count]
    block = refs[nodes * count]
    total, doubled = refs[-2:]
    node, step = pl.program_id(0), pl.program_id(1)
    for at, piece in enumerate(pieces):

        @pl.when((node == at // count) & (step == at % count))
        def _(piece=piece):
            put_double(doubled, piece)

    part = jnp.dot(doubled[...], two_terms(block), preferred_element_type=jnp.float32)

    @pl.when(step == 0)
    def _():
        total[...] = refs[nodes * count + 1][...] + part if resume else part

    @pl.when(step > 0)
    def _():
        total[...] += part


def final_body(count, lanes, out_piece, sources, core, *refs):
    pieces = refs[: count + 1]
    block, start, given, kept, total, doubled = refs[count + 1 :]
    step = pl.program_id(0)
    for at in range(count - 1):

        @pl.when(step == at)
        def _(at=at):
            put_double(doubled, pieces[at])

    @pl.when(step == count - 1)
    def _():
        half = pieces[count].shape[0]
        put_double(doubled, pieces[count - 1], slice(0, half))
        put_double(doubled, pieces[count], slice(half, 2 * half))

    part = jnp.dot(doubled[...], two_terms(block), preferred_element_type=jnp.float32)

    @pl.when(step == 0)
    def _():
        total[...] = start[...] + part

    @pl.when(step > 0)
    def _():
        total[...] += part

    @pl.when(step == count - 1)
    def _():
        for lane in range(lanes):
            for side in range(2):
                first = (2 * lane + side) * out_piece

                @pl.when(core[0] == side)
                def _(lane=lane, first=first):
                    kept[lane] = total[:, first : first + out_piece]

                @pl.when(core[0] != side)
                def _(lane=lane, first=first):
                    given[lane] = total[:, first : first + out_piece]


def product_call(body, grid, prefetch, args, in_specs, out_shape, out_specs, scratch, flops, **more):
    return pl.pallas_call(
        body,
        grid_spec=pltpu.PrefetchScalarGridSpec(
            num_scalar_prefetch=prefetch,
            grid=grid,
            in_specs=in_specs,
            out_specs=out_specs,
            scratch_shapes=scratch,
        ),
        out_shape=out_shape,
        compiler_params=pltpu.CompilerParams(
            dimension_semantics=("arbitrary",) * len(grid), vmem_limit_bytes=56 << 20
        ),
        cost_estimate=pl.CostEstimate(
            flops=flops, bytes_accessed=flops // 512, transcendentals=0
        ),
        **more,
    )(*args)


def partial_product(groups, block, sources, start=None):
    nodes, count = len(groups), len(groups[0])
    width, piece = groups[0][0].shape
    cols = block.shape[1]
    pieces = [array for group in groups for array in group]
    total = pl.BlockSpec((None, width, cols), lambda node, step, sources: (node, 0, 0))
    in_specs = [pl.BlockSpec(pieces[0].shape, lambda node, step, sources: (0, 0))] * len(pieces)
    in_specs.append(pl.BlockSpec((piece, cols), lambda node, step, sources: (sources[step], 0)))
    args = [sources, *pieces, block]
    aliases = {}
    if start is not None:
        aliases = {len(args): 0}
        in_specs.append(total)
        args.append(start)
    return product_call(
        functools.partial(partial_body, nodes, count, start is not None),
        (nodes, count), 1, args, in_specs,
        jax.ShapeDtypeStruct((nodes, width, cols), jnp.float32), total,
        [pltpu.VMEM((width, 2 * piece), jnp.bfloat16)],
        4 * nodes * count * width * piece * cols, input_output_aliases=aliases,
    )


def final_product(node, pieces, block, sources, core, lanes, start):
    count = len(pieces) - 1
    width, piece = pieces[0].shape
    cols = block.shape[1]
    out_piece = cols // (2 * lanes)
    half = jax.ShapeDtypeStruct((lanes, width, out_piece), jnp.float32)
    half_spec = pl.BlockSpec(half.shape, lambda step, *_: (0, 0, 0))
    in_specs = [pl.BlockSpec(array.shape, lambda step, *_: (0, 0)) for array in pieces]
    in_specs.append(pl.BlockSpec((piece, cols), lambda step, sources, core: (sources[step], 0)))
    in_specs.append(pl.BlockSpec((None, width, cols), lambda step, *_: (node, 0, 0)))
    return product_call(
        functools.partial(final_body, count, lanes, out_piece), (count,), 2,
        [sources, core, *pieces, block, start], in_specs, [half, half], [half_spec, half_spec],
        [pltpu.VMEM((width, cols), jnp.float32), pltpu.VMEM((width, 2 * piece), jnp.bfloat16)],
        4 * count * width * piece * cols,
    )


pad_rows = 16


def step_of(lanes):
    return 128 if lanes % 128 == 0 else lanes


def encoded(value):
    top = jnp.max(jnp.abs(value), axis=-2, keepdims=True)
    exponent = jnp.ceil(jnp.log2(jnp.maximum(top, 1e-30)) + 0.01)
    whole = jnp.round(value * jnp.exp2(15.0 - exponent)).astype(jnp.int32)
    wide = jnp.broadcast_to(exponent, (pad_rows, value.shape[-1])).astype(jnp.int32)
    return whole.astype(jnp.int16), wide.astype(jnp.int16)


def put_coded(ref, value, lead=()):
    rows = value.shape[0]
    whole, wide = encoded(value)
    ref[(*lead, slice(0, rows), slice(None))] = whole
    ref[(*lead, slice(rows, rows + pad_rows), slice(None))] = wide


def get_coded(ref, lead=()):
    rows = ref.shape[-2] - pad_rows
    whole = ref[(*lead, slice(0, rows), slice(None))].astype(jnp.int32).astype(jnp.float32)
    wide = ref[(*lead, slice(rows, rows + pad_rows), slice(None))].astype(jnp.int32)
    return whole * jnp.exp2(wide.astype(jnp.float32)[0:1, :] - 15.0)


def simple_call(body, args, in_specs, out_shape, out_specs, grid, prefetch=0, **more):
    size = sum(array.size * array.dtype.itemsize for array in args)
    return pl.pallas_call(
        body,
        grid_spec=pltpu.PrefetchScalarGridSpec(
            num_scalar_prefetch=prefetch,
            grid=grid,
            in_specs=in_specs,
            out_specs=out_specs,
            scratch_shapes=more.pop("scratch_shapes", ()),
        ),
        out_shape=out_shape,
        compiler_params=pltpu.CompilerParams(
            dimension_semantics=("arbitrary",) * len(grid), vmem_limit_bytes=48 << 20
        ),
        cost_estimate=pl.CostEstimate(flops=size, bytes_accessed=size, transcendentals=0),
        **more,
    )(*args)


def prepare_body(nodes, block_rows, first_row, ancestors, *refs):
    source, outs = refs[0], refs[1:]
    rows = source.shape[1]
    slots = ancestors.shape[1]
    row = lax.broadcasted_iota(jnp.int32, (rows, 1), 0) + first_row[0]
    first_block = lax.div(first_row[0], block_rows)
    for node in range(nodes):
        keep = None
        for ahead in range((rows - 1) // block_rows + 2):
            block = first_block + ahead
            listed = ancestors[node, 0] == block
            for slot in range(1, slots):
                listed = listed | (ancestors[node, slot] == block)
            inside = (row >= block * block_rows) & (row < (block + 1) * block_rows) & listed
            keep = inside if keep is None else keep | inside
        value = jnp.where(keep, source[node].astype(jnp.float32), 0.0)
        outs[node][...] = value.T.astype(jnp.bfloat16)


def prepare(factor, ancestors, first_row):
    nodes, rows, width = factor.shape
    shape = jax.ShapeDtypeStruct((width, rows), jnp.bfloat16)
    spec = pl.BlockSpec((width, rows), lambda at, *_: (0, 0))
    return simple_call(
        functools.partial(prepare_body, nodes, width),
        [first_row, ancestors, factor],
        [pl.BlockSpec(factor.shape, lambda at, *_: (0, 0, 0))],
        [shape] * nodes, [spec] * nodes, (1,), 2,
    )


def add_encode_body(shifts, lane, *refs):
    total = refs[2 * (shifts + 1)]
    total[...] = refs[0][...] + refs[1][...]
    for at in range(shifts):
        value = refs[2 * at + 2][...] + refs[2 * at + 3][...]
        put_coded(refs[2 * (shifts + 1) + 1 + at], value)


def add_encode(kept, other, lane, lanes):
    _, rows, width = kept.shape
    lane_step = step_of(width)
    in_specs, args = [], []
    for shift in range(lanes):
        spec = pl.BlockSpec(
            (None, rows, lane_step),
            lambda at, lane, shift=shift: (lax.rem(lane[0] + shift, lanes), 0, at),
        )
        in_specs += [spec, spec]
        args += [kept, other]
    out_specs = [pl.BlockSpec((rows, lane_step), lambda at, lane: (0, at))]
    out_shape = [jax.ShapeDtypeStruct((rows, width), jnp.float32)]
    for _ in range(1, lanes):
        out_specs.append(pl.BlockSpec((rows + pad_rows, lane_step), lambda at, lane: (0, at)))
        out_shape.append(jax.ShapeDtypeStruct((rows + pad_rows, width), jnp.int16))
    return simple_call(
        functools.partial(add_encode_body, lanes - 1), [lane, *args], in_specs,
        out_shape, out_specs, (width // lane_step,), 1,
    )


def split_dots(pairs):
    total = None
    for (left_head, left_tail), right in pairs:
        right_head = right.astype(jnp.bfloat16)
        right_tail = (right - right_head.astype(jnp.float32)).astype(jnp.bfloat16)
        for left, value in ((left_tail, right_head), (left_head, right_tail), (left_head, right_head)):
            part = jnp.dot(left, value, preferred_element_type=jnp.float32)
            total = part if total is None else total + part
    return total


def chain_body(node, lanes, *refs):
    mine, *received = refs[:lanes]
    heads = refs[lanes : lanes + node]
    tails = refs[lanes + node : lanes + 2 * node]
    earlier = refs[lanes + 2 * node : lanes + 3 * node]
    value, coded, turned = refs[-3:]
    total = mine[...]
    for ref in received:
        total = total + get_coded(ref)
    if node:
        total = total + split_dots(
            [((h[...], t[...]), e[...]) for h, t, e in zip(heads, tails, earlier, strict=True)]
        )
    total = -total
    value[...] = total
    put_coded(coded, total)
    turned[...] = total.T


def chain(node, nodes, mine, received, heads, tails, earlier, turned):
    rows, width = mine.shape
    lane_step = step_of(width)
    lanes = 1 + len(received)
    first = node * (node - 1) // 2
    column = lambda rows: pl.BlockSpec((rows, lane_step), lambda at: (0, at))
    in_specs = [column(rows)] + [column(rows + pad_rows)] * len(received)
    factor_specs = [
        pl.BlockSpec((None, rows, rows), lambda at, j=j: (first + j, 0, 0)) for j in range(node)
    ]
    in_specs += factor_specs + factor_specs + [column(rows)] * node
    args = [mine, *received, *[heads] * node, *[tails] * node, *earlier]
    aliases = {}
    if turned is not None:
        aliases = {len(args): 2}
        args.append(turned)
        in_specs.append(pl.BlockSpec(memory_space=pl.ANY))
    return simple_call(
        functools.partial(chain_body, node, lanes), args, in_specs,
        [
            jax.ShapeDtypeStruct((rows, width), jnp.float32),
            jax.ShapeDtypeStruct((rows + pad_rows, width), jnp.int16),
            jax.ShapeDtypeStruct((nodes, width, rows), jnp.float32),
        ],
        [
            column(rows),
            column(rows + pad_rows),
            pl.BlockSpec((None, lane_step, rows), lambda at: (node, at, 0)),
        ],
        (width // lane_step,), input_output_aliases=aliases,
    )


def turn_body(*refs):
    refs[-1][...] = get_coded(refs[0]).T


def turn(node, nodes, coded, turned):
    padded, width = coded.shape
    lane_step = step_of(width)
    rows = padded - pad_rows
    args, in_specs = [coded], [pl.BlockSpec((padded, lane_step), lambda at: (0, at))]
    aliases = {}
    if turned is not None:
        aliases = {1: 0}
        args.append(turned)
        in_specs.append(pl.BlockSpec(memory_space=pl.ANY))
    return simple_call(
        turn_body, args, in_specs,
        jax.ShapeDtypeStruct((nodes, width, rows), jnp.float32),
        pl.BlockSpec((None, lane_step, rows), lambda at: (node, at, 0)),
        (width // lane_step,), input_output_aliases=aliases,
    )


def inner_body(half, low, up, left, rows, mine, given):
    value = rows[...]
    head = value.astype(jnp.bfloat16)
    tail = (value - head.astype(jnp.float32)).astype(jnp.bfloat16)
    value = jnp.dot(
        left[...], jnp.concatenate([head, tail, head], axis=0), preferred_element_type=jnp.float32
    )

    @pl.when(pl.program_id(0) < half)
    def _():
        mine[...] = value

    @pl.when(pl.program_id(0) >= half)
    def _():
        given[...] = value


def inner(low, up, left, rows):
    nodes, piece, width = rows.shape
    count = nodes * (nodes + 1) // 2
    half = count // 2
    shape = jax.ShapeDtypeStruct((half, width, width), jnp.float32)
    return simple_call(
        functools.partial(inner_body, half), [low, up, left, rows],
        [
            pl.BlockSpec((None, width, left.shape[2]), lambda at, low, up: (low[at], 0, 0)),
            pl.BlockSpec((None, piece, width), lambda at, low, up: (up[at], 0, 0)),
        ],
        [shape, shape],
        [
            pl.BlockSpec((None, width, width), lambda at, *_: (jnp.minimum(at, half - 1), 0, 0)),
            pl.BlockSpec((None, width, width), lambda at, *_: (jnp.maximum(at - half, 0), 0, 0)),
        ],
        (count,), 2,
    )


def deal_body(plain, coded, count, starts, *refs):
    total = refs[0][...]
    for ref in refs[1:plain]:
        total = total + ref[...]
    for ref in refs[plain : plain + coded]:
        total = total + get_coded(ref)
    outs = refs[plain + coded :]
    if count == 1:
        put_coded(outs[0], total)
        return
    whole = outs[-1]
    whole[...] = total
    rows = total.shape[0] // count
    for at in range(count):
        part = whole[pl.ds(pl.multiple_of(starts[at], 8), rows), :]
        if at == 0:
            outs[0][...] = part
        else:
            put_coded(outs[at], part)


def deal(plain, coded, starts):
    rows, width = plain[0].shape
    lane_step = step_of(width)
    count = starts.shape[0]
    column = lambda rows: pl.BlockSpec((rows, lane_step), lambda at, starts: (0, at))
    part = rows // count
    shapes = [jax.ShapeDtypeStruct((part, width), jnp.float32)] if count > 1 else []
    shapes += [jax.ShapeDtypeStruct((part + pad_rows, width), jnp.int16)] * max(count - 1, 1)
    return simple_call(
        functools.partial(deal_body, len(plain), len(coded), count),
        [starts, *plain, *coded],
        [column(rows)] * len(plain) + [column(rows + pad_rows)] * len(coded),
        shapes, [column(shape.shape[0]) for shape in shapes], (width // lane_step,), 1,
        scratch_shapes=[pltpu.VMEM((rows, lane_step), jnp.float32)] if count > 1 else [],
    )


def heap_body(*refs):
    for at, ref in enumerate(refs[:-1]):
        refs[-1][at] = ref[...]


def heap(parts):
    rows, width = parts[0].shape
    lane_step = step_of(width)
    return simple_call(
        heap_body, parts,
        [pl.BlockSpec((rows, lane_step), lambda at: (0, at))] * len(parts),
        jax.ShapeDtypeStruct((len(parts), rows, width), parts[0].dtype),
        pl.BlockSpec((len(parts), rows, lane_step), lambda at: (0, 0, at)),
        (width // lane_step,),
    )


def finish_body(arrays, width, place, row_of, col_of, *refs):
    parts = refs[:arrays]
    base, out, sums = refs[arrays:]
    step = pl.program_id(0)
    count, padded, _ = parts[0].shape
    rows = padded - pad_rows

    @pl.when(step == 0)
    def _():
        for at, ref in enumerate(parts):
            for piece in range(count):
                start = pl.multiple_of(place[at * count + piece], 8)
                sums[pl.ds(start, rows), :] = get_coded(ref, (piece,))

    row, col = row_of[step], col_of[step]
    low, up = jnp.minimum(row, col), jnp.maximum(row, col)
    start = pl.multiple_of((up * (up + 1) // 2 + low) * width, width)
    value = base[...] - sums[pl.ds(start, width), :]

    @pl.when(row <= col)
    def _():
        out[...] = value

    @pl.when(row > col)
    def _():
        out[...] = value.T


def finish(place, parts, base, nodes, width):
    visits = []
    for up in range(nodes):
        for low in range(up):
            visits += [(low, up), (up, low)]
        visits.append((up, up))
    row_of = jnp.asarray([row for row, _ in visits], jnp.int32)
    col_of = jnp.asarray([col for _, col in visits], jnp.int32)

    def base_map(step, place, row_of, col_of):
        low = jnp.minimum(row_of[step], col_of[step])
        up = jnp.maximum(row_of[step], col_of[step])
        return (up * (up + 1) // 2 + low, 0, 0)

    whole = pl.BlockSpec(parts[0].shape, lambda step, *_: (0, 0, 0))
    return simple_call(
        functools.partial(finish_body, len(parts), width),
        [place, row_of, col_of, *parts, base],
        [whole] * len(parts) + [pl.BlockSpec((None, width, width), base_map)],
        jax.ShapeDtypeStruct((nodes, nodes, width, width), jnp.float32),
        pl.BlockSpec(
            (None, None, width, width),
            lambda step, place, row_of, col_of: (row_of[step], col_of[step], 0, 0),
        ),
        (nodes * nodes,), 3,
        scratch_shapes=[pltpu.VMEM((nodes * (nodes + 1) // 2 * width, width), jnp.float32)],
    )


def spread_bits(number, bits):
    return sum(((number >> at) & 1) << bit for at, bit in enumerate(bits))


def gather_bits(index, bits):
    return sum(((index >> bit) & 1) << at for at, bit in enumerate(bits))


def local(ancestor_inverse, factor, coupling, diagonal_inverse, ancestors):
    row_count = lax.axis_size("row")
    col_count = lax.axis_size("col")
    total = row_count * col_count
    row_index = lax.axis_index("row")
    col_index = lax.axis_index("col")
    flat_index = row_index * col_count + col_index
    nodes, piece_rows, width = factor.shape
    col_bits = col_count.bit_length() - 1
    first_row = (flat_index * piece_rows).reshape(1).astype(jnp.int32)
    lower = prepare(factor, ancestors, first_row)

    order = ring_order(col_count)
    sources = ring_sources(order, col_index)
    core = (row_index % 2).reshape(1).astype(jnp.int32)
    moves = ring_moves(order)
    lanes = row_count // 2
    steps = col_count // 2
    near, early = 3, 1 + 2 * (steps - 2)
    gathered = [[lower[node]] for node in range(nodes)]

    def advance(step):
        for node in range(nodes):
            gathered[node] = ring_step(gathered[node], moves, step == steps)

    for step in range(1, steps - 1):
        advance(step)

    early_coupling = after(coupling, gathered[0][1])
    turned_heads, turned_tails = split_terms(jnp.swapaxes(early_coupling, 1, 2))
    mixed = []
    for k in range(nodes):
        value = lower[k].astype(jnp.float32)
        for j in range(k):
            value = value - left_dot(early_coupling[pair_index(k, j)], mixed[j])
        mixed.append(value)
    mixed_heads, mixed_tails = split_terms(jnp.stack(mixed))
    left = jnp.concatenate([mixed_tails, mixed_heads, mixed_heads], axis=2)

    first_pieces = [group[:near] for group in gathered]
    first_pieces[0][0], turned_heads, turned_tails, left = lax.optimization_barrier(
        (first_pieces[0][0], turned_heads, turned_tails, left)
    )
    starts = partial_product(first_pieces, ancestor_inverse, sources[:near])
    advance(steps - 1)
    starts = partial_product(
        [group[near:early] for group in gathered],
        ancestor_inverse,
        sources[near:early],
        starts,
    )
    advance(steps)

    swap = (1 << col_bits) | 1

    def middle(at):
        low, up = at & 1, (at >> col_bits) & 1
        return at if low == up else at ^ swap

    first_moves = [(at, middle(at)) for at in range(total)]
    last_moves = [
        (middle(r * col_count + c), c * row_count + r)
        for r in range(row_count)
        for c in range(col_count)
    ]
    lane = row_index // 2
    lane_ref = lane.reshape(1).astype(jnp.int32)
    sibling = [(at, at ^ 1) for at in range(row_count)]
    lane_moves = [
        [(at, (at + 2 * shift) % row_count) for at in range(row_count)]
        for shift in range(1, lanes)
    ]

    def lane_sums(given, kept):
        other = lax.ppermute(given, "row", sibling)
        mine, *coded = add_encode(kept, other, lane_ref, lanes)
        return mine, [
            lax.ppermute(part, "row", moves)
            for part, moves in zip(coded, lane_moves, strict=True)
        ]

    base = {}

    def base_columns(columns, others):
        here, diagonal = lax.optimization_barrier((coupling, diagonal_inverse, *others))[:2]
        for k in columns:
            for j in range(k):
                value = -matmul(base[j, 0], here[pair_index(k, 0)])
                for i in range(1, k):
                    value = value - matmul(base[j, i], here[pair_index(k, i)])
                base[j, k] = value
                base[k, j] = value.T
            value = diagonal[k]
            for j in range(k):
                value = value - left_dot(here[pair_index(k, j)], base[j, k])
            base[k, k] = value

    by_cols = []
    out_cols = out_rows = None
    for k in range(nodes):
        given, kept = final_product(
            k, gathered[k][early:], ancestor_inverse, sources[early:], core, lanes, starts
        )
        row_sums = lane_sums(given, kept)
        if k == nodes - 1:
            base_columns(range(k), by_cols[-1:])
            held = lax.optimization_barrier((row_sums[0], base[k - 1, k - 1]))
            row_sums, base[k - 1, k - 1] = (held[0], row_sums[1]), held[1]
        value, coded, out_cols = chain(
            k, nodes, *row_sums, turned_heads, turned_tails, by_cols, out_cols
        )
        by_cols.append(value)
        coded = lax.ppermute(coded, both, first_moves)
        coded = lax.ppermute(coded, both, last_moves)
        out_rows = turn(k, nodes, coded, out_rows)

    base_columns(range(nodes - 1, nodes), by_cols[-1:])
    base = jnp.stack([base[j, k] for k in range(nodes) for j in range(k + 1)])
    left, base = lax.optimization_barrier((left, base))

    count = nodes * (nodes + 1) // 2
    listing = [(j, k) for k in range(nodes) for j in range(k + 1)]
    turn_to = (core[0] * (count // 2) + jnp.arange(count, dtype=jnp.int32)) % count
    low = jnp.asarray([j for j, _ in listing], jnp.int32)[turn_to]
    up = jnp.asarray([k for _, k in listing], jnp.int32)[turn_to]
    kept, given = inner(low, up, left, out_rows)
    half_rows = kept.shape[0] * width
    kept, given = kept.reshape(half_rows, width), given.reshape(half_rows, width)
    flat_bits = (row_count * col_count).bit_length() - 1
    planes = [[0, *range(col_bits + 1, flat_bits)], list(range(1, col_bits))]
    plane_moves = [
        [[(at, at ^ spread_bits(other, bits)) for at in range(total)] for other in range(1, 1 << len(bits))]
        for bits in planes
    ]
    parts_of = [1 << len(bits) for bits in planes]
    mine_of = [gather_bits(flat_index, bits) for bits in planes]

    def starts_of(level, rows):
        around = mine_of[level] ^ jnp.arange(parts_of[level], dtype=jnp.int32)
        return (around * (rows // parts_of[level])).astype(jnp.int32)

    def exchange(arrays, level):
        return [
            lax.ppermute(array, both, moves)
            for array, moves in zip(arrays, plane_moves[level], strict=True)
        ]

    other = lax.ppermute(given, "row", sibling)
    mine, *coded = deal([kept, other], [], starts_of(0, half_rows))
    coded = exchange(coded, 0)
    mine, *coded = deal([mine], coded, starts_of(1, mine.shape[0]))
    coded = exchange(coded, 1)
    (summed,) = deal([mine], coded, jnp.zeros((1,), jnp.int32))
    pile = heap([summed, *exchange([summed] * (parts_of[1] - 1), 1)])
    piles = [pile, *exchange([pile] * (parts_of[0] - 1), 0)]
    piles += [lax.ppermute(pile, "row", sibling) for pile in piles]
    rows_at = half_rows // (parts_of[0] * parts_of[1])
    around = [mine_of[at] ^ jnp.arange(parts_of[at], dtype=jnp.int32) for at in range(2)]
    within = (around[0][:, None] * parts_of[1] + around[1][None, :]).reshape(-1) * rows_at
    place = jnp.concatenate(
        [core[0] * half_rows + within, (1 - core[0]) * half_rows + within]
    ).astype(jnp.int32)
    pile, base = lax.optimization_barrier((piles[0], base))
    node_blocks = finish(place, [pile, *piles[1:]], base, nodes, width)
    return out_rows, out_cols, node_blocks


def solution(mesh):
    placed = (P("row", "col"), P(None, both, None), P(), P(), P())

    return jax.shard_map(
        local,
        mesh=mesh,
        in_specs=placed,
        out_specs=(P(None, both, None), P(None, ("col", "row"), None), P()),
        check_vma=False,
    )
```

```python
import functools

import jax
import jax.numpy as jnp
from jax import lax
from jax.experimental import pallas as pl
from jax.experimental.pallas import tpu as pltpu
from jax.sharding import PartitionSpec as P

both = ("row", "col")
high = lax.Precision.HIGH


def matmul(left, right):
    return jnp.dot(left, right, precision=high)


def left_dot(left, right):
    return lax.dot_general(left, right, (((0,), (0,)), ((), ())), precision=high)


def pair_index(later, earlier):
    return later * (later - 1) // 2 + earlier


def split_terms(value):
    head = lax.reduce_precision(value, 8, 7)
    return head.astype(jnp.bfloat16), (value - head).astype(jnp.bfloat16)


def after(value, *others):
    return lax.optimization_barrier((value, *others))[0]


def ring_order(count):
    return list(range(0, count, 2)) + list(range(count - 1, 0, -2))


def ring_moves(order):
    count = len(order)
    ahead = [(order[at], order[(at + 1) % count]) for at in range(count)]
    return ahead, [(target, source) for source, target in ahead]


def ring_step(pieces, moves, last):
    up, down = (pieces[0], pieces[0]) if len(pieces) == 1 else pieces[-2:]
    if last:
        half = up.shape[0] // 2
        up, down = up[:half], down[half:]
    return [*pieces, lax.ppermute(up, "col", moves[0]), lax.ppermute(down, "col", moves[1])]


def ring_sources(order, col_index):
    count = len(order)
    place = [0] * count
    for at, device in enumerate(order):
        place[device] = at
    my_place = jnp.asarray(place, jnp.int32)[col_index]
    table = jnp.asarray(order, jnp.int32)
    steps = [0]
    for step in range(1, count // 2):
        steps += [-step, step]
    steps.append(count // 2)
    return table[(my_place + jnp.asarray(steps, jnp.int32)) % count]


def two_terms(block):
    value = block[...]
    head = value.astype(jnp.bfloat16)
    tail = (value - head.astype(jnp.float32)).astype(jnp.bfloat16)
    return jnp.concatenate([head, tail], axis=0)


def put_double(doubled, piece, span=slice(None)):
    depth = piece.shape[1]
    doubled[span, :depth] = piece[...]
    doubled[span, depth:] = piece[...]


def partial_body(nodes, count, resume, sources, *refs):
    pieces = refs[: nodes * count]
    block = refs[nodes * count]
    total, doubled = refs[-2:]
    node, step = pl.program_id(0), pl.program_id(1)
    for at, piece in enumerate(pieces):

        @pl.when((node == at // count) & (step == at % count))
        def _(piece=piece):
            put_double(doubled, piece)

    part = jnp.dot(doubled[...], two_terms(block), preferred_element_type=jnp.float32)

    @pl.when(step == 0)
    def _():
        total[...] = refs[nodes * count + 1][...] + part if resume else part

    @pl.when(step > 0)
    def _():
        total[...] += part


def final_body(count, lanes, out_piece, sources, core, *refs):
    pieces = refs[: count + 1]
    block, start, given, kept, total, doubled = refs[count + 1 :]
    step = pl.program_id(0)
    for at in range(count - 1):

        @pl.when(step == at)
        def _(at=at):
            put_double(doubled, pieces[at])

    @pl.when(step == count - 1)
    def _():
        half = pieces[count].shape[0]
        put_double(doubled, pieces[count - 1], slice(0, half))
        put_double(doubled, pieces[count], slice(half, 2 * half))

    part = jnp.dot(doubled[...], two_terms(block), preferred_element_type=jnp.float32)

    @pl.when(step == 0)
    def _():
        total[...] = start[...] + part

    @pl.when(step > 0)
    def _():
        total[...] += part

    @pl.when(step == count - 1)
    def _():
        for lane in range(lanes):
            for side in range(2):
                first = (2 * lane + side) * out_piece

                @pl.when(core[0] == side)
                def _(lane=lane, first=first):
                    kept[lane] = total[:, first : first + out_piece]

                @pl.when(core[0] != side)
                def _(lane=lane, first=first):
                    given[lane] = total[:, first : first + out_piece]


def product_call(body, grid, prefetch, args, in_specs, out_shape, out_specs, scratch, flops, **more):
    return pl.pallas_call(
        body,
        grid_spec=pltpu.PrefetchScalarGridSpec(
            num_scalar_prefetch=prefetch,
            grid=grid,
            in_specs=in_specs,
            out_specs=out_specs,
            scratch_shapes=scratch,
        ),
        out_shape=out_shape,
        compiler_params=pltpu.CompilerParams(
            dimension_semantics=("arbitrary",) * len(grid), vmem_limit_bytes=56 << 20
        ),
        cost_estimate=pl.CostEstimate(
            flops=flops, bytes_accessed=flops // 512, transcendentals=0
        ),
        **more,
    )(*args)


def partial_product(groups, block, sources, start=None):
    nodes, count = len(groups), len(groups[0])
    width, piece = groups[0][0].shape
    cols = block.shape[1]
    pieces = [array for group in groups for array in group]
    total = pl.BlockSpec((None, width, cols), lambda node, step, sources: (node, 0, 0))
    in_specs = [pl.BlockSpec(pieces[0].shape, lambda node, step, sources: (0, 0))] * len(pieces)
    in_specs.append(pl.BlockSpec((piece, cols), lambda node, step, sources: (sources[step], 0)))
    args = [sources, *pieces, block]
    aliases = {}
    if start is not None:
        aliases = {len(args): 0}
        in_specs.append(total)
        args.append(start)
    return product_call(
        functools.partial(partial_body, nodes, count, start is not None),
        (nodes, count), 1, args, in_specs,
        jax.ShapeDtypeStruct((nodes, width, cols), jnp.float32), total,
        [pltpu.VMEM((width, 2 * piece), jnp.bfloat16)],
        4 * nodes * count * width * piece * cols, input_output_aliases=aliases,
    )


def final_product(node, pieces, block, sources, core, lanes, start):
    count = len(pieces) - 1
    width, piece = pieces[0].shape
    cols = block.shape[1]
    out_piece = cols // (2 * lanes)
    half = jax.ShapeDtypeStruct((lanes, width, out_piece), jnp.float32)
    half_spec = pl.BlockSpec(half.shape, lambda step, *_: (0, 0, 0))
    in_specs = [pl.BlockSpec(array.shape, lambda step, *_: (0, 0)) for array in pieces]
    in_specs.append(pl.BlockSpec((piece, cols), lambda step, sources, core: (sources[step], 0)))
    in_specs.append(pl.BlockSpec((None, width, cols), lambda step, *_: (node, 0, 0)))
    return product_call(
        functools.partial(final_body, count, lanes, out_piece), (count,), 2,
        [sources, core, *pieces, block, start], in_specs, [half, half], [half_spec, half_spec],
        [pltpu.VMEM((width, cols), jnp.float32), pltpu.VMEM((width, 2 * piece), jnp.bfloat16)],
        4 * count * width * piece * cols,
    )


pad_rows = 16


def step_of(lanes):
    return 128 if lanes % 128 == 0 else lanes


def encoded(value):
    top = jnp.max(jnp.abs(value), axis=-2, keepdims=True)
    exponent = jnp.ceil(jnp.log2(jnp.maximum(top, 1e-30)) + 0.01)
    whole = jnp.round(value * jnp.exp2(15.0 - exponent)).astype(jnp.int32)
    wide = jnp.broadcast_to(exponent, (pad_rows, value.shape[-1])).astype(jnp.int32)
    return whole.astype(jnp.int16), wide.astype(jnp.int16)


def put_coded(ref, value, lead=()):
    rows = value.shape[0]
    whole, wide = encoded(value)
    ref[(*lead, slice(0, rows), slice(None))] = whole
    ref[(*lead, slice(rows, rows + pad_rows), slice(None))] = wide


def get_coded(ref, lead=()):
    rows = ref.shape[-2] - pad_rows
    whole = ref[(*lead, slice(0, rows), slice(None))].astype(jnp.int32).astype(jnp.float32)
    wide = ref[(*lead, slice(rows, rows + pad_rows), slice(None))].astype(jnp.int32)
    return whole * jnp.exp2(wide.astype(jnp.float32)[0:1, :] - 15.0)


def simple_call(body, args, in_specs, out_shape, out_specs, grid, prefetch=0, **more):
    size = sum(array.size * array.dtype.itemsize for array in args)
    return pl.pallas_call(
        body,
        grid_spec=pltpu.PrefetchScalarGridSpec(
            num_scalar_prefetch=prefetch,
            grid=grid,
            in_specs=in_specs,
            out_specs=out_specs,
            scratch_shapes=more.pop("scratch_shapes", ()),
        ),
        out_shape=out_shape,
        compiler_params=pltpu.CompilerParams(
            dimension_semantics=("arbitrary",) * len(grid), vmem_limit_bytes=48 << 20
        ),
        cost_estimate=pl.CostEstimate(flops=size, bytes_accessed=size, transcendentals=0),
        **more,
    )(*args)


def prepare_body(nodes, block_rows, first_row, ancestors, *refs):
    source, outs = refs[0], refs[1:]
    rows = source.shape[1]
    slots = ancestors.shape[1]
    row = lax.broadcasted_iota(jnp.int32, (rows, 1), 0) + first_row[0]
    first_block = lax.div(first_row[0], block_rows)
    for node in range(nodes):
        keep = None
        for ahead in range((rows - 1) // block_rows + 2):
            block = first_block + ahead
            listed = ancestors[node, 0] == block
            for slot in range(1, slots):
                listed = listed | (ancestors[node, slot] == block)
            inside = (row >= block * block_rows) & (row < (block + 1) * block_rows) & listed
            keep = inside if keep is None else keep | inside
        value = jnp.where(keep, source[node].astype(jnp.float32), 0.0)
        turned = value.T.astype(jnp.bfloat16)
        outs[node][...] = turned
        outs[nodes][node] = turned


def prepare(factor, ancestors, first_row):
    nodes, rows, width = factor.shape
    shape = jax.ShapeDtypeStruct((width, rows), jnp.bfloat16)
    spec = pl.BlockSpec((width, rows), lambda at, *_: (0, 0))
    return simple_call(
        functools.partial(prepare_body, nodes, width),
        [first_row, ancestors, factor],
        [pl.BlockSpec(factor.shape, lambda at, *_: (0, 0, 0))],
        [shape] * nodes + [jax.ShapeDtypeStruct((nodes, width, rows), jnp.bfloat16)],
        [spec] * nodes + [pl.BlockSpec((nodes, width, rows), lambda at, *_: (0, 0, 0))],
        (1,), 2,
    )


def add_encode_body(shifts, lane, *refs):
    total = refs[2 * (shifts + 1)]
    total[...] = refs[0][...] + refs[1][...]
    for at in range(shifts):
        value = refs[2 * at + 2][...] + refs[2 * at + 3][...]
        put_coded(refs[2 * (shifts + 1) + 1 + at], value)


def add_encode(kept, other, lane, lanes):
    _, rows, width = kept.shape
    lane_step = step_of(width)
    in_specs, args = [], []
    for shift in range(lanes):
        spec = pl.BlockSpec(
            (None, rows, lane_step),
            lambda at, lane, shift=shift: (lax.rem(lane[0] + shift, lanes), 0, at),
        )
        in_specs += [spec, spec]
        args += [kept, other]
    out_specs = [pl.BlockSpec((rows, lane_step), lambda at, lane: (0, at))]
    out_shape = [jax.ShapeDtypeStruct((rows, width), jnp.float32)]
    for _ in range(1, lanes):
        out_specs.append(pl.BlockSpec((rows + pad_rows, lane_step), lambda at, lane: (0, at)))
        out_shape.append(jax.ShapeDtypeStruct((rows + pad_rows, width), jnp.int16))
    return simple_call(
        functools.partial(add_encode_body, lanes - 1), [lane, *args], in_specs,
        out_shape, out_specs, (width // lane_step,), 1,
    )


def split_dots(pairs):
    total = None
    for (left_head, left_tail), right in pairs:
        right_head = right.astype(jnp.bfloat16)
        right_tail = (right - right_head.astype(jnp.float32)).astype(jnp.bfloat16)
        for left, value in ((left_tail, right_head), (left_head, right_tail), (left_head, right_head)):
            part = jnp.dot(left, value, preferred_element_type=jnp.float32)
            total = part if total is None else total + part
    return total


def chain_body(node, lanes, *refs):
    mine, *received = refs[:lanes]
    heads = refs[lanes : lanes + node]
    tails = refs[lanes + node : lanes + 2 * node]
    earlier = refs[lanes + 2 * node : lanes + 3 * node]
    value, coded, turned = refs[-3:]
    total = mine[...]
    for ref in received:
        total = total + get_coded(ref)
    if node:
        total = total + split_dots(
            [((h[...], t[...]), e[...]) for h, t, e in zip(heads, tails, earlier, strict=True)]
        )
    total = -total
    value[...] = total
    put_coded(coded, total)
    turned[...] = total.T


def chain(node, nodes, mine, received, heads, tails, earlier, turned):
    rows, width = mine.shape
    lane_step = step_of(width)
    lanes = 1 + len(received)
    first = node * (node - 1) // 2
    column = lambda rows: pl.BlockSpec((rows, lane_step), lambda at: (0, at))
    in_specs = [column(rows)] + [column(rows + pad_rows)] * len(received)
    factor_specs = [
        pl.BlockSpec((None, rows, rows), lambda at, j=j: (first + j, 0, 0)) for j in range(node)
    ]
    in_specs += factor_specs + factor_specs + [column(rows)] * node
    args = [mine, *received, *[heads] * node, *[tails] * node, *earlier]
    aliases = {}
    if turned is not None:
        aliases = {len(args): 2}
        args.append(turned)
        in_specs.append(pl.BlockSpec(memory_space=pl.ANY))
    return simple_call(
        functools.partial(chain_body, node, lanes), args, in_specs,
        [
            jax.ShapeDtypeStruct((rows, width), jnp.float32),
            jax.ShapeDtypeStruct((rows + pad_rows, width), jnp.int16),
            jax.ShapeDtypeStruct((nodes, width, rows), jnp.float32),
        ],
        [
            column(rows),
            column(rows + pad_rows),
            pl.BlockSpec((None, lane_step, rows), lambda at: (node, at, 0)),
        ],
        (width // lane_step,), input_output_aliases=aliases,
    )


def turn_body(*refs):
    refs[-1][...] = get_coded(refs[0]).T


def turn(node, nodes, coded, turned):
    padded, width = coded.shape
    lane_step = step_of(width)
    rows = padded - pad_rows
    args, in_specs = [coded], [pl.BlockSpec((padded, lane_step), lambda at: (0, at))]
    aliases = {}
    if turned is not None:
        aliases = {1: 0}
        args.append(turned)
        in_specs.append(pl.BlockSpec(memory_space=pl.ANY))
    return simple_call(
        turn_body, args, in_specs,
        jax.ShapeDtypeStruct((nodes, width, rows), jnp.float32),
        pl.BlockSpec((None, lane_step, rows), lambda at: (node, at, 0)),
        (width // lane_step,), input_output_aliases=aliases,
    )


def inner_body(half, low, up, left, rows, mine, given):
    value = rows[...]
    head = value.astype(jnp.bfloat16)
    tail = (value - head.astype(jnp.float32)).astype(jnp.bfloat16)
    value = jnp.dot(
        left[...], jnp.concatenate([head, tail, head], axis=0), preferred_element_type=jnp.float32
    )

    @pl.when(pl.program_id(0) < half)
    def _():
        mine[...] = value

    @pl.when(pl.program_id(0) >= half)
    def _():
        given[...] = value


def inner(low, up, left, rows):
    nodes, piece, width = rows.shape
    count = nodes * (nodes + 1) // 2
    half = count // 2
    shape = jax.ShapeDtypeStruct((half, width, width), jnp.float32)
    return simple_call(
        functools.partial(inner_body, half), [low, up, left, rows],
        [
            pl.BlockSpec((None, width, left.shape[2]), lambda at, low, up: (low[at], 0, 0)),
            pl.BlockSpec((None, piece, width), lambda at, low, up: (up[at], 0, 0)),
        ],
        [shape, shape],
        [
            pl.BlockSpec((None, width, width), lambda at, *_: (jnp.minimum(at, half - 1), 0, 0)),
            pl.BlockSpec((None, width, width), lambda at, *_: (jnp.maximum(at - half, 0), 0, 0)),
        ],
        (count,), 2,
    )


def deal_body(plain, coded, count, starts, *refs):
    total = refs[0][...]
    for ref in refs[1:plain]:
        total = total + ref[...]
    for ref in refs[plain : plain + coded]:
        total = total + get_coded(ref)
    outs = refs[plain + coded :]
    if count == 1:
        put_coded(outs[0], total)
        return
    whole = outs[-1]
    whole[...] = total
    rows = total.shape[0] // count
    for at in range(count):
        part = whole[pl.ds(pl.multiple_of(starts[at], 8), rows), :]
        if at == 0:
            outs[0][...] = part
        else:
            put_coded(outs[at], part)


def deal(plain, coded, starts):
    rows, width = plain[0].shape
    lane_step = step_of(width)
    count = starts.shape[0]
    column = lambda rows: pl.BlockSpec((rows, lane_step), lambda at, starts: (0, at))
    part = rows // count
    shapes = [jax.ShapeDtypeStruct((part, width), jnp.float32)] if count > 1 else []
    shapes += [jax.ShapeDtypeStruct((part + pad_rows, width), jnp.int16)] * max(count - 1, 1)
    return simple_call(
        functools.partial(deal_body, len(plain), len(coded), count),
        [starts, *plain, *coded],
        [column(rows)] * len(plain) + [column(rows + pad_rows)] * len(coded),
        shapes, [column(shape.shape[0]) for shape in shapes], (width // lane_step,), 1,
        scratch_shapes=[pltpu.VMEM((rows, lane_step), jnp.float32)] if count > 1 else [],
    )


def heap_body(*refs):
    for at, ref in enumerate(refs[:-1]):
        refs[-1][at] = ref[...]


def heap(parts):
    rows, width = parts[0].shape
    lane_step = step_of(width)
    return simple_call(
        heap_body, parts,
        [pl.BlockSpec((rows, lane_step), lambda at: (0, at))] * len(parts),
        jax.ShapeDtypeStruct((len(parts), rows, width), parts[0].dtype),
        pl.BlockSpec((len(parts), rows, lane_step), lambda at: (0, 0, at)),
        (width // lane_step,),
    )


def finish_body(arrays, width, place, row_of, col_of, *refs):
    parts = refs[:arrays]
    base, out, sums = refs[arrays:]
    step = pl.program_id(0)
    count, padded, _ = parts[0].shape
    rows = padded - pad_rows

    @pl.when(step == 0)
    def _():
        for at, ref in enumerate(parts):
            for piece in range(count):
                start = pl.multiple_of(place[at * count + piece], 8)
                sums[pl.ds(start, rows), :] = get_coded(ref, (piece,))

    row, col = row_of[step], col_of[step]
    low, up = jnp.minimum(row, col), jnp.maximum(row, col)
    start = pl.multiple_of((up * (up + 1) // 2 + low) * width, width)
    value = base[...] - sums[pl.ds(start, width), :]

    @pl.when(row <= col)
    def _():
        out[...] = value

    @pl.when(row > col)
    def _():
        out[...] = value.T


def finish(place, parts, base, nodes, width):
    visits = []
    for up in range(nodes):
        for low in range(up):
            visits += [(low, up), (up, low)]
        visits.append((up, up))
    row_of = jnp.asarray([row for row, _ in visits], jnp.int32)
    col_of = jnp.asarray([col for _, col in visits], jnp.int32)

    def base_map(step, place, row_of, col_of):
        low = jnp.minimum(row_of[step], col_of[step])
        up = jnp.maximum(row_of[step], col_of[step])
        return (up * (up + 1) // 2 + low, 0, 0)

    whole = pl.BlockSpec(parts[0].shape, lambda step, *_: (0, 0, 0))
    return simple_call(
        functools.partial(finish_body, len(parts), width),
        [place, row_of, col_of, *parts, base],
        [whole] * len(parts) + [pl.BlockSpec((None, width, width), base_map)],
        jax.ShapeDtypeStruct((nodes, nodes, width, width), jnp.float32),
        pl.BlockSpec(
            (None, None, width, width),
            lambda step, place, row_of, col_of: (row_of[step], col_of[step], 0, 0),
        ),
        (nodes * nodes,), 3,
        scratch_shapes=[pltpu.VMEM((nodes * (nodes + 1) // 2 * width, width), jnp.float32)],
    )


def spread_bits(number, bits):
    return sum(((number >> at) & 1) << bit for at, bit in enumerate(bits))


def gather_bits(index, bits):
    return sum(((index >> bit) & 1) << at for at, bit in enumerate(bits))


def local(ancestor_inverse, factor, coupling, diagonal_inverse, ancestors):
    row_count = lax.axis_size("row")
    col_count = lax.axis_size("col")
    total = row_count * col_count
    row_index = lax.axis_index("row")
    col_index = lax.axis_index("col")
    flat_index = row_index * col_count + col_index
    nodes, piece_rows, width = factor.shape
    col_bits = col_count.bit_length() - 1
    first_row = (flat_index * piece_rows).reshape(1).astype(jnp.int32)
    *lower, lower_stack = prepare(factor, ancestors, first_row)

    order = ring_order(col_count)
    sources = ring_sources(order, col_index)
    core = (row_index % 2).reshape(1).astype(jnp.int32)
    moves = ring_moves(order)
    lanes = row_count // 2
    steps = col_count // 2
    near, early = 3, 1 + 2 * (steps - 2)
    gathered = [[lower[node]] for node in range(nodes)]

    def advance(step):
        for node in range(nodes):
            gathered[node] = ring_step(gathered[node], moves, step == steps)

    for step in range(1, steps - 1):
        advance(step)

    early_coupling = after(coupling, gathered[0][1])
    turned_heads, turned_tails = split_terms(jnp.swapaxes(early_coupling, 1, 2))
    first_pieces = [group[:near] for group in gathered]
    first_pieces[0][0], turned_heads, turned_tails = lax.optimization_barrier(
        (first_pieces[0][0], turned_heads, turned_tails)
    )
    starts = partial_product(first_pieces, ancestor_inverse, sources[:near])
    advance(steps - 1)
    starts = partial_product(
        [group[near:early] for group in gathered],
        ancestor_inverse,
        sources[near:early],
        starts,
    )
    advance(steps)

    swap = (1 << col_bits) | 1

    def middle(at):
        low, up = at & 1, (at >> col_bits) & 1
        return at if low == up else at ^ swap

    first_moves = [(at, middle(at)) for at in range(total)]
    last_moves = [
        (middle(r * col_count + c), c * row_count + r)
        for r in range(row_count)
        for c in range(col_count)
    ]
    lower_stack = lax.ppermute(
        lower_stack,
        both,
        [(c * row_count + r, r * col_count + c) for r in range(row_count) for c in range(col_count)],
    )

    lane = row_index // 2
    lane_ref = lane.reshape(1).astype(jnp.int32)
    sibling = [(at, at ^ 1) for at in range(row_count)]
    lane_moves = [
        [(at, (at + 2 * shift) % row_count) for at in range(row_count)]
        for shift in range(1, lanes)
    ]

    def lane_sums(given, kept):
        other = lax.ppermute(given, "row", sibling)
        mine, *coded = add_encode(kept, other, lane_ref, lanes)
        return mine, [
            lax.ppermute(part, "row", moves)
            for part, moves in zip(coded, lane_moves, strict=True)
        ]

    base = {}

    def base_columns(columns, others):
        here, diagonal = lax.optimization_barrier((coupling, diagonal_inverse, *others))[:2]
        for k in columns:
            for j in range(k):
                value = -matmul(base[j, 0], here[pair_index(k, 0)])
                for i in range(1, k):
                    value = value - matmul(base[j, i], here[pair_index(k, i)])
                base[j, k] = value
                base[k, j] = value.T
            value = diagonal[k]
            for j in range(k):
                value = value - left_dot(here[pair_index(k, j)], base[j, k])
            base[k, k] = value

    by_cols = []
    out_cols = out_rows = None
    for k in range(nodes):
        given, kept = final_product(
            k, gathered[k][early:], ancestor_inverse, sources[early:], core, lanes, starts
        )
        row_sums = lane_sums(given, kept)
        if k == nodes - 1:
            base_columns(range(k), by_cols[-1:])
            held = lax.optimization_barrier((row_sums[0], base[k - 1, k - 1]))
            row_sums, base[k - 1, k - 1] = (held[0], row_sums[1]), held[1]
        value, coded, out_cols = chain(
            k, nodes, *row_sums, turned_heads, turned_tails, by_cols, out_cols
        )
        by_cols.append(value)
        coded = lax.ppermute(coded, both, first_moves)
        coded = lax.ppermute(coded, both, last_moves)
        out_rows = turn(k, nodes, coded, out_rows)

    lower_stack, late_coupling, _ = lax.optimization_barrier((lower_stack, coupling, by_cols[-2]))
    mixed = []
    for k in range(nodes):
        value = lower_stack[k].astype(jnp.float32)
        for j in range(k):
            value = value - left_dot(late_coupling[pair_index(k, j)], mixed[j])
        mixed.append(value)
    mixed_heads, mixed_tails = split_terms(jnp.stack(mixed))
    left = jnp.concatenate([mixed_tails, mixed_heads, mixed_heads], axis=2)

    count = nodes * (nodes + 1) // 2
    listing = [(j, k) for k in range(nodes) for j in range(k + 1)]
    turn_to = (core[0] * (count // 2) + jnp.arange(count, dtype=jnp.int32)) % count
    low = jnp.asarray([j for j, _ in listing], jnp.int32)[turn_to]
    up = jnp.asarray([k for _, k in listing], jnp.int32)[turn_to]
    kept, given = inner(low, up, left, out_cols)
    half_rows = kept.shape[0] * width
    kept, given = kept.reshape(half_rows, width), given.reshape(half_rows, width)
    flat_bits = (row_count * col_count).bit_length() - 1
    planes = [[0, *range(col_bits + 1, flat_bits)], list(range(1, col_bits))]
    plane_moves = [
        [[(at, at ^ spread_bits(other, bits)) for at in range(total)] for other in range(1, 1 << len(bits))]
        for bits in planes
    ]
    parts_of = [1 << len(bits) for bits in planes]
    mine_of = [gather_bits(flat_index, bits) for bits in planes]

    def starts_of(level, rows):
        around = mine_of[level] ^ jnp.arange(parts_of[level], dtype=jnp.int32)
        return (around * (rows // parts_of[level])).astype(jnp.int32)

    def exchange(arrays, level):
        return [
            lax.ppermute(array, both, moves)
            for array, moves in zip(arrays, plane_moves[level], strict=True)
        ]

    other = lax.ppermute(given, "row", sibling)
    mine, *coded = deal([kept, other], [], starts_of(0, half_rows))
    coded = exchange(coded, 0)
    base_columns(range(nodes - 1, nodes), [mine])
    base = jnp.stack([base[j, k] for k in range(nodes) for j in range(k + 1)])
    mine, base = lax.optimization_barrier((mine, base))
    mine, *coded = deal([mine], coded, starts_of(1, mine.shape[0]))
    coded = exchange(coded, 1)
    (summed,) = deal([mine], coded, jnp.zeros((1,), jnp.int32))
    pile = heap([summed, *exchange([summed] * (parts_of[1] - 1), 1)])
    piles = [pile, *exchange([pile] * (parts_of[0] - 1), 0)]
    piles += [lax.ppermute(pile, "row", sibling) for pile in piles]
    rows_at = half_rows // (parts_of[0] * parts_of[1])
    around = [mine_of[at] ^ jnp.arange(parts_of[at], dtype=jnp.int32) for at in range(2)]
    within = (around[0][:, None] * parts_of[1] + around[1][None, :]).reshape(-1) * rows_at
    place = jnp.concatenate(
        [core[0] * half_rows + within, (1 - core[0]) * half_rows + within]
    ).astype(jnp.int32)
    pile, base = lax.optimization_barrier((piles[0], base))
    node_blocks = finish(place, [pile, *piles[1:]], base, nodes, width)
    return out_rows, out_cols, node_blocks


def solution(mesh):
    placed = (P("row", "col"), P(None, both, None), P(), P(), P())

    return jax.shard_map(
        local,
        mesh=mesh,
        in_specs=placed,
        out_specs=(P(None, both, None), P(None, ("col", "row"), None), P()),
        check_vma=False,
    )
```

```python
import functools

import jax
import jax.numpy as jnp
from jax import lax
from jax.experimental import pallas as pl
from jax.experimental.pallas import tpu as pltpu
from jax.sharding import PartitionSpec as P

both = ("row", "col")
high = lax.Precision.HIGH


def matmul(left, right):
    return jnp.dot(left, right, precision=high)


def left_dot(left, right):
    return lax.dot_general(left, right, (((0,), (0,)), ((), ())), precision=high)


def pair_index(later, earlier):
    return later * (later - 1) // 2 + earlier


def split_terms(value):
    head = lax.reduce_precision(value, 8, 7)
    return head.astype(jnp.bfloat16), (value - head).astype(jnp.bfloat16)


def after(value, *others):
    return lax.optimization_barrier((value, *others))[0]


def ring_order(count):
    return list(range(0, count, 2)) + list(range(count - 1, 0, -2))


def ring_moves(order):
    count = len(order)
    ahead = [(order[at], order[(at + 1) % count]) for at in range(count)]
    return ahead, [(target, source) for source, target in ahead]


def ring_step(pieces, moves, last):
    up, down = (pieces[0], pieces[0]) if len(pieces) == 1 else pieces[-2:]
    if last:
        half = up.shape[0] // 2
        up, down = up[:half], down[half:]
    return [*pieces, lax.ppermute(up, "col", moves[0]), lax.ppermute(down, "col", moves[1])]


def ring_sources(order, col_index):
    count = len(order)
    place = [0] * count
    for at, device in enumerate(order):
        place[device] = at
    my_place = jnp.asarray(place, jnp.int32)[col_index]
    table = jnp.asarray(order, jnp.int32)
    steps = [0]
    for step in range(1, count // 2):
        steps += [-step, step]
    steps.append(count // 2)
    return table[(my_place + jnp.asarray(steps, jnp.int32)) % count]


def two_terms(block):
    value = block[...]
    head = value.astype(jnp.bfloat16)
    tail = (value - head.astype(jnp.float32)).astype(jnp.bfloat16)
    return jnp.concatenate([head, tail], axis=0)


def put_double(doubled, piece, span=slice(None)):
    depth = piece.shape[1]
    doubled[span, :depth] = piece[...]
    doubled[span, depth:] = piece[...]


def partial_body(nodes, count, resume, sources, *refs):
    pieces = refs[: nodes * count]
    block = refs[nodes * count]
    total, doubled = refs[-2:]
    node, step = pl.program_id(0), pl.program_id(1)
    for at, piece in enumerate(pieces):

        @pl.when((node == at // count) & (step == at % count))
        def _(piece=piece):
            put_double(doubled, piece)

    part = jnp.dot(doubled[...], two_terms(block), preferred_element_type=jnp.float32)

    @pl.when(step == 0)
    def _():
        total[...] = refs[nodes * count + 1][...] + part if resume else part

    @pl.when(step > 0)
    def _():
        total[...] += part


def final_body(count, lanes, out_piece, sources, core, *refs):
    pieces = refs[: count + 1]
    block, start, given, kept, total, doubled = refs[count + 1 :]
    step = pl.program_id(0)
    for at in range(count - 1):

        @pl.when(step == at)
        def _(at=at):
            put_double(doubled, pieces[at])

    @pl.when(step == count - 1)
    def _():
        half = pieces[count].shape[0]
        put_double(doubled, pieces[count - 1], slice(0, half))
        put_double(doubled, pieces[count], slice(half, 2 * half))

    part = jnp.dot(doubled[...], two_terms(block), preferred_element_type=jnp.float32)

    @pl.when(step == 0)
    def _():
        total[...] = start[...] + part

    @pl.when(step > 0)
    def _():
        total[...] += part

    @pl.when(step == count - 1)
    def _():
        for lane in range(lanes):
            for side in range(2):
                first = (2 * lane + side) * out_piece

                @pl.when(core[0] == side)
                def _(lane=lane, first=first):
                    kept[lane] = total[:, first : first + out_piece]

                @pl.when(core[0] != side)
                def _(lane=lane, first=first):
                    given[lane] = total[:, first : first + out_piece]


def product_call(body, grid, prefetch, args, in_specs, out_shape, out_specs, scratch, flops, **more):
    return pl.pallas_call(
        body,
        grid_spec=pltpu.PrefetchScalarGridSpec(
            num_scalar_prefetch=prefetch,
            grid=grid,
            in_specs=in_specs,
            out_specs=out_specs,
            scratch_shapes=scratch,
        ),
        out_shape=out_shape,
        compiler_params=pltpu.CompilerParams(
            dimension_semantics=("arbitrary",) * len(grid), vmem_limit_bytes=56 << 20
        ),
        cost_estimate=pl.CostEstimate(
            flops=flops, bytes_accessed=flops // 512, transcendentals=0
        ),
        **more,
    )(*args)


def partial_product(groups, block, sources, start=None):
    nodes, count = len(groups), len(groups[0])
    width, piece = groups[0][0].shape
    cols = block.shape[1]
    pieces = [array for group in groups for array in group]
    total = pl.BlockSpec((None, width, cols), lambda node, step, sources: (node, 0, 0))
    in_specs = [pl.BlockSpec(pieces[0].shape, lambda node, step, sources: (0, 0))] * len(pieces)
    in_specs.append(pl.BlockSpec((piece, cols), lambda node, step, sources: (sources[step], 0)))
    args = [sources, *pieces, block]
    aliases = {}
    if start is not None:
        aliases = {len(args): 0}
        in_specs.append(total)
        args.append(start)
    return product_call(
        functools.partial(partial_body, nodes, count, start is not None),
        (nodes, count), 1, args, in_specs,
        jax.ShapeDtypeStruct((nodes, width, cols), jnp.float32), total,
        [pltpu.VMEM((width, 2 * piece), jnp.bfloat16)],
        4 * nodes * count * width * piece * cols, input_output_aliases=aliases,
    )


def final_product(node, pieces, block, sources, core, lanes, start):
    count = len(pieces) - 1
    width, piece = pieces[0].shape
    cols = block.shape[1]
    out_piece = cols // (2 * lanes)
    half = jax.ShapeDtypeStruct((lanes, width, out_piece), jnp.float32)
    half_spec = pl.BlockSpec(half.shape, lambda step, *_: (0, 0, 0))
    in_specs = [pl.BlockSpec(array.shape, lambda step, *_: (0, 0)) for array in pieces]
    in_specs.append(pl.BlockSpec((piece, cols), lambda step, sources, core: (sources[step], 0)))
    in_specs.append(pl.BlockSpec((None, width, cols), lambda step, *_: (node, 0, 0)))
    return product_call(
        functools.partial(final_body, count, lanes, out_piece), (count,), 2,
        [sources, core, *pieces, block, start], in_specs, [half, half], [half_spec, half_spec],
        [pltpu.VMEM((width, cols), jnp.float32), pltpu.VMEM((width, 2 * piece), jnp.bfloat16)],
        4 * count * width * piece * cols,
    )


pad_rows = 16


def step_of(lanes):
    return 128 if lanes % 128 == 0 else lanes


def encoded(value):
    top = jnp.max(jnp.abs(value), axis=-2, keepdims=True)
    exponent = jnp.ceil(jnp.log2(jnp.maximum(top, 1e-30)) + 0.01)
    whole = jnp.round(value * jnp.exp2(15.0 - exponent)).astype(jnp.int32)
    wide = jnp.broadcast_to(exponent, (pad_rows, value.shape[-1])).astype(jnp.int32)
    return whole.astype(jnp.int16), wide.astype(jnp.int16)


def put_coded(ref, value, lead=()):
    rows = value.shape[0]
    whole, wide = encoded(value)
    ref[(*lead, slice(0, rows), slice(None))] = whole
    ref[(*lead, slice(rows, rows + pad_rows), slice(None))] = wide


def get_coded(ref, lead=()):
    rows = ref.shape[-2] - pad_rows
    whole = ref[(*lead, slice(0, rows), slice(None))].astype(jnp.int32).astype(jnp.float32)
    wide = ref[(*lead, slice(rows, rows + pad_rows), slice(None))].astype(jnp.int32)
    return whole * jnp.exp2(wide.astype(jnp.float32)[0:1, :] - 15.0)


def simple_call(body, args, in_specs, out_shape, out_specs, grid, prefetch=0, **more):
    size = sum(array.size * array.dtype.itemsize for array in args)
    return pl.pallas_call(
        body,
        grid_spec=pltpu.PrefetchScalarGridSpec(
            num_scalar_prefetch=prefetch,
            grid=grid,
            in_specs=in_specs,
            out_specs=out_specs,
            scratch_shapes=more.pop("scratch_shapes", ()),
        ),
        out_shape=out_shape,
        compiler_params=pltpu.CompilerParams(
            dimension_semantics=("arbitrary",) * len(grid), vmem_limit_bytes=48 << 20
        ),
        cost_estimate=pl.CostEstimate(flops=size, bytes_accessed=size, transcendentals=0),
        **more,
    )(*args)


def prepare_body(nodes, block_rows, first_row, ancestors, *refs):
    source, outs = refs[0], refs[1:]
    rows = source.shape[1]
    slots = ancestors.shape[1]
    row = lax.broadcasted_iota(jnp.int32, (rows, 1), 0) + first_row[0]
    first_block = lax.div(first_row[0], block_rows)
    for node in range(nodes):
        keep = None
        for ahead in range((rows - 1) // block_rows + 2):
            block = first_block + ahead
            listed = ancestors[node, 0] == block
            for slot in range(1, slots):
                listed = listed | (ancestors[node, slot] == block)
            inside = (row >= block * block_rows) & (row < (block + 1) * block_rows) & listed
            keep = inside if keep is None else keep | inside
        value = jnp.where(keep, source[node].astype(jnp.float32), 0.0)
        turned = value.T.astype(jnp.bfloat16)
        outs[node][...] = turned
        outs[nodes][node] = turned


def prepare(factor, ancestors, first_row):
    nodes, rows, width = factor.shape
    shape = jax.ShapeDtypeStruct((width, rows), jnp.bfloat16)
    spec = pl.BlockSpec((width, rows), lambda at, *_: (0, 0))
    return simple_call(
        functools.partial(prepare_body, nodes, width),
        [first_row, ancestors, factor],
        [pl.BlockSpec(factor.shape, lambda at, *_: (0, 0, 0))],
        [shape] * nodes + [jax.ShapeDtypeStruct((nodes, width, rows), jnp.bfloat16)],
        [spec] * nodes + [pl.BlockSpec((nodes, width, rows), lambda at, *_: (0, 0, 0))],
        (1,), 2,
    )


def add_encode_body(shifts, lane, *refs):
    total = refs[2 * (shifts + 1)]
    total[...] = refs[0][...] + refs[1][...]
    for at in range(shifts):
        value = refs[2 * at + 2][...] + refs[2 * at + 3][...]
        put_coded(refs[2 * (shifts + 1) + 1 + at], value)


def add_encode(kept, other, lane, lanes):
    _, rows, width = kept.shape
    lane_step = step_of(width)
    in_specs, args = [], []
    for shift in range(lanes):
        spec = pl.BlockSpec(
            (None, rows, lane_step),
            lambda at, lane, shift=shift: (lax.rem(lane[0] + shift, lanes), 0, at),
        )
        in_specs += [spec, spec]
        args += [kept, other]
    out_specs = [pl.BlockSpec((rows, lane_step), lambda at, lane: (0, at))]
    out_shape = [jax.ShapeDtypeStruct((rows, width), jnp.float32)]
    for _ in range(1, lanes):
        out_specs.append(pl.BlockSpec((rows + pad_rows, lane_step), lambda at, lane: (0, at)))
        out_shape.append(jax.ShapeDtypeStruct((rows + pad_rows, width), jnp.int16))
    return simple_call(
        functools.partial(add_encode_body, lanes - 1), [lane, *args], in_specs,
        out_shape, out_specs, (width // lane_step,), 1,
    )


def split_dots(pairs):
    total = None
    for (left_head, left_tail), right in pairs:
        right_head = right.astype(jnp.bfloat16)
        right_tail = (right - right_head.astype(jnp.float32)).astype(jnp.bfloat16)
        for left, value in ((left_tail, right_head), (left_head, right_tail), (left_head, right_head)):
            part = jnp.dot(left, value, preferred_element_type=jnp.float32)
            total = part if total is None else total + part
    return total


def chain_body(node, lanes, *refs):
    mine, *received = refs[:lanes]
    heads = refs[lanes : lanes + node]
    tails = refs[lanes + node : lanes + 2 * node]
    earlier = refs[lanes + 2 * node : lanes + 3 * node]
    value, coded, turned = refs[-3:]
    total = mine[...]
    for ref in received:
        total = total + get_coded(ref)
    if node:
        total = total + split_dots(
            [((h[...], t[...]), e[...]) for h, t, e in zip(heads, tails, earlier, strict=True)]
        )
    total = -total
    value[...] = total
    put_coded(coded, total)
    turned[...] = total.T


def chain(node, nodes, mine, received, heads, tails, earlier, turned):
    rows, width = mine.shape
    lane_step = step_of(width)
    lanes = 1 + len(received)
    first = node * (node - 1) // 2
    column = lambda rows: pl.BlockSpec((rows, lane_step), lambda at: (0, at))
    in_specs = [column(rows)] + [column(rows + pad_rows)] * len(received)
    factor_specs = [
        pl.BlockSpec((None, rows, rows), lambda at, j=j: (first + j, 0, 0)) for j in range(node)
    ]
    in_specs += factor_specs + factor_specs + [column(rows)] * node
    args = [mine, *received, *[heads] * node, *[tails] * node, *earlier]
    aliases = {}
    if turned is not None:
        aliases = {len(args): 2}
        args.append(turned)
        in_specs.append(pl.BlockSpec(memory_space=pl.ANY))
    return simple_call(
        functools.partial(chain_body, node, lanes), args, in_specs,
        [
            jax.ShapeDtypeStruct((rows, width), jnp.float32),
            jax.ShapeDtypeStruct((rows + pad_rows, width), jnp.int16),
            jax.ShapeDtypeStruct((nodes, width, rows), jnp.float32),
        ],
        [
            column(rows),
            column(rows + pad_rows),
            pl.BlockSpec((None, lane_step, rows), lambda at: (node, at, 0)),
        ],
        (width // lane_step,), input_output_aliases=aliases,
    )


def turn_body(*refs):
    refs[-1][...] = get_coded(refs[0]).T


def turn(node, nodes, coded, turned):
    padded, width = coded.shape
    lane_step = step_of(width)
    rows = padded - pad_rows
    args, in_specs = [coded], [pl.BlockSpec((padded, lane_step), lambda at: (0, at))]
    aliases = {}
    if turned is not None:
        aliases = {1: 0}
        args.append(turned)
        in_specs.append(pl.BlockSpec(memory_space=pl.ANY))
    return simple_call(
        turn_body, args, in_specs,
        jax.ShapeDtypeStruct((nodes, width, rows), jnp.float32),
        pl.BlockSpec((None, lane_step, rows), lambda at: (node, at, 0)),
        (width // lane_step,), input_output_aliases=aliases,
    )


def inner_body(half, low, up, left, rows, mine, given):
    value = rows[...]
    head = value.astype(jnp.bfloat16)
    tail = (value - head.astype(jnp.float32)).astype(jnp.bfloat16)
    value = jnp.dot(
        left[...], jnp.concatenate([head, tail, head], axis=0), preferred_element_type=jnp.float32
    )

    @pl.when(pl.program_id(0) < half)
    def _():
        mine[...] = value

    @pl.when(pl.program_id(0) >= half)
    def _():
        given[...] = value


def inner(low, up, left, rows):
    nodes, piece, width = rows.shape
    count = nodes * (nodes + 1) // 2
    half = count // 2
    shape = jax.ShapeDtypeStruct((half, width, width), jnp.float32)
    return simple_call(
        functools.partial(inner_body, half), [low, up, left, rows],
        [
            pl.BlockSpec((None, width, left.shape[2]), lambda at, low, up: (low[at], 0, 0)),
            pl.BlockSpec((None, piece, width), lambda at, low, up: (up[at], 0, 0)),
        ],
        [shape, shape],
        [
            pl.BlockSpec((None, width, width), lambda at, *_: (jnp.minimum(at, half - 1), 0, 0)),
            pl.BlockSpec((None, width, width), lambda at, *_: (jnp.maximum(at - half, 0), 0, 0)),
        ],
        (count,), 2,
    )


def deal_body(plain, coded, count, starts, *refs):
    total = refs[0][...]
    for ref in refs[1:plain]:
        total = total + ref[...]
    for ref in refs[plain : plain + coded]:
        total = total + get_coded(ref)
    outs = refs[plain + coded :]
    if count == 1:
        put_coded(outs[0], total)
        return
    whole = outs[-1]
    whole[...] = total
    rows = total.shape[0] // count
    for at in range(count):
        part = whole[pl.ds(pl.multiple_of(starts[at], 8), rows), :]
        if at == 0:
            outs[0][...] = part
        else:
            put_coded(outs[at], part)


def deal(plain, coded, starts):
    rows, width = plain[0].shape
    lane_step = step_of(width)
    count = starts.shape[0]
    column = lambda rows: pl.BlockSpec((rows, lane_step), lambda at, starts: (0, at))
    part = rows // count
    shapes = [jax.ShapeDtypeStruct((part, width), jnp.float32)] if count > 1 else []
    shapes += [jax.ShapeDtypeStruct((part + pad_rows, width), jnp.int16)] * max(count - 1, 1)
    return simple_call(
        functools.partial(deal_body, len(plain), len(coded), count),
        [starts, *plain, *coded],
        [column(rows)] * len(plain) + [column(rows + pad_rows)] * len(coded),
        shapes, [column(shape.shape[0]) for shape in shapes], (width // lane_step,), 1,
        scratch_shapes=[pltpu.VMEM((rows, lane_step), jnp.float32)] if count > 1 else [],
    )


def heap_body(*refs):
    for at, ref in enumerate(refs[:-1]):
        refs[-1][at] = ref[...]


def heap(parts):
    rows, width = parts[0].shape
    lane_step = step_of(width)
    return simple_call(
        heap_body, parts,
        [pl.BlockSpec((rows, lane_step), lambda at: (0, at))] * len(parts),
        jax.ShapeDtypeStruct((len(parts), rows, width), parts[0].dtype),
        pl.BlockSpec((len(parts), rows, lane_step), lambda at: (0, 0, at)),
        (width // lane_step,),
    )


def finish_body(arrays, width, place, row_of, col_of, *refs):
    parts = refs[:arrays]
    base, out, sums = refs[arrays:]
    step = pl.program_id(0)
    count, padded, _ = parts[0].shape
    rows = padded - pad_rows

    @pl.when(step == 0)
    def _():
        for at, ref in enumerate(parts):
            for piece in range(count):
                start = pl.multiple_of(place[at * count + piece], 8)
                sums[pl.ds(start, rows), :] = get_coded(ref, (piece,))

    row, col = row_of[step], col_of[step]
    low, up = jnp.minimum(row, col), jnp.maximum(row, col)
    start = pl.multiple_of((up * (up + 1) // 2 + low) * width, width)
    value = base[...] - sums[pl.ds(start, width), :]

    @pl.when(row <= col)
    def _():
        out[...] = value

    @pl.when(row > col)
    def _():
        out[...] = value.T


def finish(place, parts, base, nodes, width):
    visits = []
    for up in range(nodes):
        for low in range(up):
            visits += [(low, up), (up, low)]
        visits.append((up, up))
    row_of = jnp.asarray([row for row, _ in visits], jnp.int32)
    col_of = jnp.asarray([col for _, col in visits], jnp.int32)

    def base_map(step, place, row_of, col_of):
        low = jnp.minimum(row_of[step], col_of[step])
        up = jnp.maximum(row_of[step], col_of[step])
        return (up * (up + 1) // 2 + low, 0, 0)

    whole = pl.BlockSpec(parts[0].shape, lambda step, *_: (0, 0, 0))
    return simple_call(
        functools.partial(finish_body, len(parts), width),
        [place, row_of, col_of, *parts, base],
        [whole] * len(parts) + [pl.BlockSpec((None, width, width), base_map)],
        jax.ShapeDtypeStruct((nodes, nodes, width, width), jnp.float32),
        pl.BlockSpec(
            (None, None, width, width),
            lambda step, place, row_of, col_of: (row_of[step], col_of[step], 0, 0),
        ),
        (nodes * nodes,), 3,
        scratch_shapes=[pltpu.VMEM((nodes * (nodes + 1) // 2 * width, width), jnp.float32)],
    )


def spread_bits(number, bits):
    return sum(((number >> at) & 1) << bit for at, bit in enumerate(bits))


def gather_bits(index, bits):
    return sum(((index >> bit) & 1) << at for at, bit in enumerate(bits))


def local(ancestor_inverse, factor, coupling, diagonal_inverse, ancestors):
    row_count = lax.axis_size("row")
    col_count = lax.axis_size("col")
    total = row_count * col_count
    row_index = lax.axis_index("row")
    col_index = lax.axis_index("col")
    flat_index = row_index * col_count + col_index
    nodes, piece_rows, width = factor.shape
    col_bits = col_count.bit_length() - 1
    first_row = (flat_index * piece_rows).reshape(1).astype(jnp.int32)
    *lower, lower_stack = prepare(factor, ancestors, first_row)

    order = ring_order(col_count)
    sources = ring_sources(order, col_index)
    core = (row_index % 2).reshape(1).astype(jnp.int32)
    moves = ring_moves(order)
    lanes = row_count // 2
    steps = col_count // 2
    near, early = 3, 1 + 2 * (steps - 2)
    gathered = [[lower[node]] for node in range(nodes)]

    def advance(step):
        for node in range(nodes):
            gathered[node] = ring_step(gathered[node], moves, step == steps)

    for step in range(1, steps - 1):
        advance(step)

    early_coupling = after(coupling, gathered[0][1])
    turned_heads, turned_tails = split_terms(jnp.swapaxes(early_coupling, 1, 2))
    first_pieces = [group[:near] for group in gathered]
    first_pieces[0][0], turned_heads, turned_tails = lax.optimization_barrier(
        (first_pieces[0][0], turned_heads, turned_tails)
    )
    starts = partial_product(first_pieces, ancestor_inverse, sources[:near])
    advance(steps - 1)
    starts = partial_product(
        [group[near:early] for group in gathered],
        ancestor_inverse,
        sources[near:early],
        starts,
    )
    advance(steps)

    swap = (1 << col_bits) | 1

    def middle(at):
        low, up = at & 1, (at >> col_bits) & 1
        return at if low == up else at ^ swap

    first_moves = [(at, middle(at)) for at in range(total)]
    last_moves = [
        (middle(r * col_count + c), c * row_count + r)
        for r in range(row_count)
        for c in range(col_count)
    ]
    lower_stack = lax.ppermute(
        lower_stack,
        both,
        [(c * row_count + r, r * col_count + c) for r in range(row_count) for c in range(col_count)],
    )

    lane = row_index // 2
    lane_ref = lane.reshape(1).astype(jnp.int32)
    sibling = [(at, at ^ 1) for at in range(row_count)]
    lane_moves = [
        [(at, (at + 2 * shift) % row_count) for at in range(row_count)]
        for shift in range(1, lanes)
    ]

    def lane_sums(given, kept):
        other = lax.ppermute(given, "row", sibling)
        mine, *coded = add_encode(kept, other, lane_ref, lanes)
        return mine, [
            lax.ppermute(part, "row", moves)
            for part, moves in zip(coded, lane_moves, strict=True)
        ]

    base = {}

    def base_columns(columns, others):
        here, diagonal = lax.optimization_barrier((coupling, diagonal_inverse, *others))[:2]
        for k in columns:
            for j in range(k):
                value = -matmul(base[j, 0], here[pair_index(k, 0)])
                for i in range(1, k):
                    value = value - matmul(base[j, i], here[pair_index(k, i)])
                base[j, k] = value
                base[k, j] = value.T
            value = diagonal[k]
            for j in range(k):
                value = value - left_dot(here[pair_index(k, j)], base[j, k])
            base[k, k] = value

    by_cols = []
    out_cols = out_rows = None
    for k in range(nodes):
        given, kept = final_product(
            k, gathered[k][early:], ancestor_inverse, sources[early:], core, lanes, starts
        )
        row_sums = lane_sums(given, kept)
        if k == nodes - 1:
            base_columns(range(k), by_cols[-1:])
            held = lax.optimization_barrier((row_sums[0], base[k - 1, k - 1]))
            row_sums, base[k - 1, k - 1] = (held[0], row_sums[1]), held[1]
        value, coded, out_cols = chain(
            k, nodes, *row_sums, turned_heads, turned_tails, by_cols, out_cols
        )
        by_cols.append(value)
        coded = lax.ppermute(coded, both, first_moves)
        coded = lax.ppermute(coded, both, last_moves)
        out_rows = turn(k, nodes, coded, out_rows)

    lower_stack, late_coupling, _ = lax.optimization_barrier((lower_stack, coupling, by_cols[-2]))
    mixed = []
    for k in range(nodes):
        value = lower_stack[k].astype(jnp.float32)
        for j in range(k):
            value = value - left_dot(late_coupling[pair_index(k, j)], mixed[j])
        mixed.append(value)
    mixed_heads, mixed_tails = split_terms(jnp.stack(mixed))
    left = jnp.concatenate([mixed_tails, mixed_heads, mixed_heads], axis=2)

    count = nodes * (nodes + 1) // 2
    listing = [(j, k) for k in range(nodes) for j in range(k + 1)]
    turned_listing = listing[count // 2 :] + listing[: count // 2]

    def by_core(at):
        one, two = ([pair[at] for pair in pairs] for pairs in (listing, turned_listing))
        return jnp.where(core[0] == 0, jnp.asarray(one, jnp.int32), jnp.asarray(two, jnp.int32))

    low, up = by_core(0), by_core(1)
    kept, given = inner(low, up, left, out_cols)
    half_rows = kept.shape[0] * width
    kept, given = kept.reshape(half_rows, width), given.reshape(half_rows, width)
    flat_bits = (row_count * col_count).bit_length() - 1
    planes = [[0, *range(col_bits + 1, flat_bits)], list(range(1, col_bits))]
    plane_moves = [
        [[(at, at ^ spread_bits(other, bits)) for at in range(total)] for other in range(1, 1 << len(bits))]
        for bits in planes
    ]
    parts_of = [1 << len(bits) for bits in planes]
    mine_of = [gather_bits(flat_index, bits) for bits in planes]

    def starts_of(level, rows):
        around = mine_of[level] ^ jnp.arange(parts_of[level], dtype=jnp.int32)
        return (around * (rows // parts_of[level])).astype(jnp.int32)

    def exchange(arrays, level):
        return [
            lax.ppermute(array, both, moves)
            for array, moves in zip(arrays, plane_moves[level], strict=True)
        ]

    other = lax.ppermute(given, "row", sibling)
    mine, *coded = deal([kept, other], [], starts_of(0, half_rows))
    coded = exchange(coded, 0)
    base_columns(range(nodes - 1, nodes), [mine])
    base = jnp.stack([base[j, k] for k in range(nodes) for j in range(k + 1)])
    mine, base = lax.optimization_barrier((mine, base))
    mine, *coded = deal([mine], coded, starts_of(1, mine.shape[0]))
    coded = exchange(coded, 1)
    (summed,) = deal([mine], coded, jnp.zeros((1,), jnp.int32))
    pile = heap([summed, *exchange([summed] * (parts_of[1] - 1), 1)])
    piles = [pile, *exchange([pile] * (parts_of[0] - 1), 0)]
    *late, out_rows = lax.optimization_barrier((*piles[2:], out_rows))
    piles = [*piles[:2], *late]
    piles += [lax.ppermute(pile, "row", sibling) for pile in piles]
    rows_at = half_rows // (parts_of[0] * parts_of[1])
    around = [mine_of[at] ^ jnp.arange(parts_of[at], dtype=jnp.int32) for at in range(2)]
    within = (around[0][:, None] * parts_of[1] + around[1][None, :]).reshape(-1) * rows_at
    place = jnp.concatenate(
        [core[0] * half_rows + within, (1 - core[0]) * half_rows + within]
    ).astype(jnp.int32)
    pile, base = lax.optimization_barrier((piles[0], base))
    node_blocks = finish(place, [pile, *piles[1:]], base, nodes, width)
    return out_rows, out_cols, node_blocks


def solution(mesh):
    placed = (P("row", "col"), P(None, both, None), P(), P(), P())

    return jax.shard_map(
        local,
        mesh=mesh,
        in_specs=placed,
        out_specs=(P(None, both, None), P(None, ("col", "row"), None), P()),
        check_vma=False,
    )
```

```python
import functools

import jax
import jax.numpy as jnp
from jax import lax
from jax.experimental import pallas as pl
from jax.experimental.pallas import tpu as pltpu
from jax.sharding import PartitionSpec as P

both = ("row", "col")
high = lax.Precision.HIGH


def matmul(left, right):
    return jnp.dot(left, right, precision=high)


def left_dot(left, right):
    return lax.dot_general(left, right, (((0,), (0,)), ((), ())), precision=high)


def pair_index(later, earlier):
    return later * (later - 1) // 2 + earlier


def split_terms(value):
    head = lax.reduce_precision(value, 8, 7)
    return head.astype(jnp.bfloat16), (value - head).astype(jnp.bfloat16)


def after(value, *others):
    return lax.optimization_barrier((value, *others))[0]


def ring_order(count):
    return list(range(0, count, 2)) + list(range(count - 1, 0, -2))


def ring_moves(order):
    count = len(order)
    ahead = [(order[at], order[(at + 1) % count]) for at in range(count)]
    return ahead, [(target, source) for source, target in ahead]


def ring_step(pieces, moves, last):
    up, down = (pieces[0], pieces[0]) if len(pieces) == 1 else pieces[-2:]
    if last:
        half = up.shape[0] // 2
        up, down = up[:half], down[half:]
    return [*pieces, lax.ppermute(up, "col", moves[0]), lax.ppermute(down, "col", moves[1])]


def ring_sources(order, col_index):
    count = len(order)
    place = [0] * count
    for at, device in enumerate(order):
        place[device] = at
    my_place = jnp.asarray(place, jnp.int32)[col_index]
    table = jnp.asarray(order, jnp.int32)
    steps = [0]
    for step in range(1, count // 2):
        steps += [-step, step]
    steps.append(count // 2)
    return table[(my_place + jnp.asarray(steps, jnp.int32)) % count]


def two_terms(block):
    value = block[...]
    head = value.astype(jnp.bfloat16)
    tail = (value - head.astype(jnp.float32)).astype(jnp.bfloat16)
    return jnp.concatenate([head, tail], axis=0)


def put_double(doubled, piece, span=slice(None)):
    depth = piece.shape[1]
    doubled[span, :depth] = piece[...]
    doubled[span, depth:] = piece[...]


def partial_body(nodes, count, resume, sources, *refs):
    pieces = refs[: nodes * count]
    block = refs[nodes * count]
    total, doubled = refs[-2:]
    node, step = pl.program_id(0), pl.program_id(1)
    for at, piece in enumerate(pieces):

        @pl.when((node == at // count) & (step == at % count))
        def _(piece=piece):
            put_double(doubled, piece)

    part = jnp.dot(doubled[...], two_terms(block), preferred_element_type=jnp.float32)

    @pl.when(step == 0)
    def _():
        total[...] = refs[nodes * count + 1][...] + part if resume else part

    @pl.when(step > 0)
    def _():
        total[...] += part


def final_body(count, lanes, out_piece, sources, core, *refs):
    pieces = refs[: count + 1]
    block, start, given, kept, total, doubled = refs[count + 1 :]
    step = pl.program_id(0)
    for at in range(count - 1):

        @pl.when(step == at)
        def _(at=at):
            put_double(doubled, pieces[at])

    @pl.when(step == count - 1)
    def _():
        half = pieces[count].shape[0]
        put_double(doubled, pieces[count - 1], slice(0, half))
        put_double(doubled, pieces[count], slice(half, 2 * half))

    part = jnp.dot(doubled[...], two_terms(block), preferred_element_type=jnp.float32)

    @pl.when(step == 0)
    def _():
        total[...] = start[...] + part

    @pl.when(step > 0)
    def _():
        total[...] += part

    @pl.when(step == count - 1)
    def _():
        for lane in range(lanes):
            for side in range(2):
                first = (2 * lane + side) * out_piece

                @pl.when(core[0] == side)
                def _(lane=lane, first=first):
                    kept[lane] = total[:, first : first + out_piece]

                @pl.when(core[0] != side)
                def _(lane=lane, first=first):
                    given[lane] = total[:, first : first + out_piece]


def product_call(body, grid, prefetch, args, in_specs, out_shape, out_specs, scratch, flops, **more):
    return pl.pallas_call(
        body,
        grid_spec=pltpu.PrefetchScalarGridSpec(
            num_scalar_prefetch=prefetch,
            grid=grid,
            in_specs=in_specs,
            out_specs=out_specs,
            scratch_shapes=scratch,
        ),
        out_shape=out_shape,
        compiler_params=pltpu.CompilerParams(
            dimension_semantics=("arbitrary",) * len(grid), vmem_limit_bytes=56 << 20
        ),
        cost_estimate=pl.CostEstimate(
            flops=flops, bytes_accessed=flops // 512, transcendentals=0
        ),
        **more,
    )(*args)


def partial_product(groups, block, sources, start=None):
    nodes, count = len(groups), len(groups[0])
    width, piece = groups[0][0].shape
    cols = block.shape[1]
    pieces = [array for group in groups for array in group]
    total = pl.BlockSpec((None, width, cols), lambda node, step, sources: (node, 0, 0))
    in_specs = [pl.BlockSpec(pieces[0].shape, lambda node, step, sources: (0, 0))] * len(pieces)
    in_specs.append(pl.BlockSpec((piece, cols), lambda node, step, sources: (sources[step], 0)))
    args = [sources, *pieces, block]
    aliases = {}
    if start is not None:
        aliases = {len(args): 0}
        in_specs.append(total)
        args.append(start)
    return product_call(
        functools.partial(partial_body, nodes, count, start is not None),
        (nodes, count), 1, args, in_specs,
        jax.ShapeDtypeStruct((nodes, width, cols), jnp.float32), total,
        [pltpu.VMEM((width, 2 * piece), jnp.bfloat16)],
        4 * nodes * count * width * piece * cols, input_output_aliases=aliases,
    )


def final_product(node, pieces, block, sources, core, lanes, start):
    count = len(pieces) - 1
    width, piece = pieces[0].shape
    cols = block.shape[1]
    out_piece = cols // (2 * lanes)
    half = jax.ShapeDtypeStruct((lanes, width, out_piece), jnp.float32)
    half_spec = pl.BlockSpec(half.shape, lambda step, *_: (0, 0, 0))
    in_specs = [pl.BlockSpec(array.shape, lambda step, *_: (0, 0)) for array in pieces]
    in_specs.append(pl.BlockSpec((piece, cols), lambda step, sources, core: (sources[step], 0)))
    in_specs.append(pl.BlockSpec((None, width, cols), lambda step, *_: (node, 0, 0)))
    return product_call(
        functools.partial(final_body, count, lanes, out_piece), (count,), 2,
        [sources, core, *pieces, block, start], in_specs, [half, half], [half_spec, half_spec],
        [pltpu.VMEM((width, cols), jnp.float32), pltpu.VMEM((width, 2 * piece), jnp.bfloat16)],
        4 * count * width * piece * cols,
    )


pad_rows = 16


def step_of(lanes):
    return 128 if lanes % 128 == 0 else lanes


def encoded(value):
    top = jnp.max(jnp.abs(value), axis=-2, keepdims=True)
    exponent = jnp.ceil(jnp.log2(jnp.maximum(top, 1e-30)) + 0.01)
    whole = jnp.round(value * jnp.exp2(15.0 - exponent)).astype(jnp.int32)
    wide = jnp.broadcast_to(exponent, (pad_rows, value.shape[-1])).astype(jnp.int32)
    return whole.astype(jnp.int16), wide.astype(jnp.int16)


def put_coded(ref, value, lead=()):
    rows = value.shape[0]
    whole, wide = encoded(value)
    ref[(*lead, slice(0, rows), slice(None))] = whole
    ref[(*lead, slice(rows, rows + pad_rows), slice(None))] = wide


def get_coded(ref, lead=()):
    rows = ref.shape[-2] - pad_rows
    whole = ref[(*lead, slice(0, rows), slice(None))].astype(jnp.int32).astype(jnp.float32)
    wide = ref[(*lead, slice(rows, rows + pad_rows), slice(None))].astype(jnp.int32)
    return whole * jnp.exp2(wide.astype(jnp.float32)[0:1, :] - 15.0)


def simple_call(body, args, in_specs, out_shape, out_specs, grid, prefetch=0, **more):
    size = sum(array.size * array.dtype.itemsize for array in args)
    return pl.pallas_call(
        body,
        grid_spec=pltpu.PrefetchScalarGridSpec(
            num_scalar_prefetch=prefetch,
            grid=grid,
            in_specs=in_specs,
            out_specs=out_specs,
            scratch_shapes=more.pop("scratch_shapes", ()),
        ),
        out_shape=out_shape,
        compiler_params=pltpu.CompilerParams(
            dimension_semantics=("arbitrary",) * len(grid), vmem_limit_bytes=48 << 20
        ),
        cost_estimate=pl.CostEstimate(flops=size, bytes_accessed=size, transcendentals=0),
        **more,
    )(*args)


def prepare_body(nodes, block_rows, first_row, ancestors, *refs):
    source, outs = refs[0], refs[1:]
    rows = source.shape[1]
    slots = ancestors.shape[1]
    row = lax.broadcasted_iota(jnp.int32, (rows, 1), 0) + first_row[0]
    first_block = lax.div(first_row[0], block_rows)
    for node in range(nodes):
        keep = None
        for ahead in range((rows - 1) // block_rows + 2):
            block = first_block + ahead
            listed = ancestors[node, 0] == block
            for slot in range(1, slots):
                listed = listed | (ancestors[node, slot] == block)
            inside = (row >= block * block_rows) & (row < (block + 1) * block_rows) & listed
            keep = inside if keep is None else keep | inside
        value = jnp.where(keep, source[node].astype(jnp.float32), 0.0)
        turned = value.T.astype(jnp.bfloat16)
        outs[node][...] = turned
        outs[nodes][node] = turned


def prepare(factor, ancestors, first_row):
    nodes, rows, width = factor.shape
    shape = jax.ShapeDtypeStruct((width, rows), jnp.bfloat16)
    spec = pl.BlockSpec((width, rows), lambda at, *_: (0, 0))
    return simple_call(
        functools.partial(prepare_body, nodes, width),
        [first_row, ancestors, factor],
        [pl.BlockSpec(factor.shape, lambda at, *_: (0, 0, 0))],
        [shape] * nodes + [jax.ShapeDtypeStruct((nodes, width, rows), jnp.bfloat16)],
        [spec] * nodes + [pl.BlockSpec((nodes, width, rows), lambda at, *_: (0, 0, 0))],
        (1,), 2,
    )


def add_encode_body(shifts, lane, *refs):
    total = refs[2 * (shifts + 1)]
    total[...] = refs[0][...] + refs[1][...]
    for at in range(shifts):
        value = refs[2 * at + 2][...] + refs[2 * at + 3][...]
        put_coded(refs[2 * (shifts + 1) + 1 + at], value)


def add_encode(kept, other, lane, lanes):
    _, rows, width = kept.shape
    lane_step = step_of(width)
    in_specs, args = [], []
    for shift in range(lanes):
        spec = pl.BlockSpec(
            (None, rows, lane_step),
            lambda at, lane, shift=shift: (lax.rem(lane[0] + shift, lanes), 0, at),
        )
        in_specs += [spec, spec]
        args += [kept, other]
    out_specs = [pl.BlockSpec((rows, lane_step), lambda at, lane: (0, at))]
    out_shape = [jax.ShapeDtypeStruct((rows, width), jnp.float32)]
    for _ in range(1, lanes):
        out_specs.append(pl.BlockSpec((rows + pad_rows, lane_step), lambda at, lane: (0, at)))
        out_shape.append(jax.ShapeDtypeStruct((rows + pad_rows, width), jnp.int16))
    return simple_call(
        functools.partial(add_encode_body, lanes - 1), [lane, *args], in_specs,
        out_shape, out_specs, (width // lane_step,), 1,
    )


def split_dots(pairs):
    total = None
    for (left_head, left_tail), right in pairs:
        right_head = right.astype(jnp.bfloat16)
        right_tail = (right - right_head.astype(jnp.float32)).astype(jnp.bfloat16)
        for left, value in ((left_tail, right_head), (left_head, right_tail), (left_head, right_head)):
            part = jnp.dot(left, value, preferred_element_type=jnp.float32)
            total = part if total is None else total + part
    return total


def chain_body(node, lanes, *refs):
    mine, *received = refs[:lanes]
    heads = refs[lanes : lanes + node]
    tails = refs[lanes + node : lanes + 2 * node]
    earlier = refs[lanes + 2 * node : lanes + 3 * node]
    value, coded, turned = refs[-3:]
    total = mine[...]
    for ref in received:
        total = total + get_coded(ref)
    if node:
        total = total + split_dots(
            [((h[...], t[...]), e[...]) for h, t, e in zip(heads, tails, earlier, strict=True)]
        )
    total = -total
    value[...] = total
    put_coded(coded, total)
    turned[...] = total.T


def chain(node, nodes, mine, received, heads, tails, earlier, turned):
    rows, width = mine.shape
    lane_step = step_of(width)
    lanes = 1 + len(received)
    first = node * (node - 1) // 2
    column = lambda rows: pl.BlockSpec((rows, lane_step), lambda at: (0, at))
    in_specs = [column(rows)] + [column(rows + pad_rows)] * len(received)
    factor_specs = [
        pl.BlockSpec((None, rows, rows), lambda at, j=j: (first + j, 0, 0)) for j in range(node)
    ]
    in_specs += factor_specs + factor_specs + [column(rows)] * node
    args = [mine, *received, *[heads] * node, *[tails] * node, *earlier]
    aliases = {}
    if turned is not None:
        aliases = {len(args): 2}
        args.append(turned)
        in_specs.append(pl.BlockSpec(memory_space=pl.ANY))
    return simple_call(
        functools.partial(chain_body, node, lanes), args, in_specs,
        [
            jax.ShapeDtypeStruct((rows, width), jnp.float32),
            jax.ShapeDtypeStruct((rows + pad_rows, width), jnp.int16),
            jax.ShapeDtypeStruct((nodes, width, rows), jnp.float32),
        ],
        [
            column(rows),
            column(rows + pad_rows),
            pl.BlockSpec((None, lane_step, rows), lambda at: (node, at, 0)),
        ],
        (width // lane_step,), input_output_aliases=aliases,
    )


def turn_body(*refs):
    refs[-1][...] = get_coded(refs[0]).T


def turn(node, nodes, coded, turned):
    padded, width = coded.shape
    lane_step = step_of(width)
    rows = padded - pad_rows
    args, in_specs = [coded], [pl.BlockSpec((padded, lane_step), lambda at: (0, at))]
    aliases = {}
    if turned is not None:
        aliases = {1: 0}
        args.append(turned)
        in_specs.append(pl.BlockSpec(memory_space=pl.ANY))
    return simple_call(
        turn_body, args, in_specs,
        jax.ShapeDtypeStruct((nodes, width, rows), jnp.float32),
        pl.BlockSpec((None, lane_step, rows), lambda at: (node, at, 0)),
        (width // lane_step,), input_output_aliases=aliases,
    )


def inner_body(half, low, up, left, rows, mine, given):
    value = rows[...]
    head = value.astype(jnp.bfloat16)
    tail = (value - head.astype(jnp.float32)).astype(jnp.bfloat16)
    value = jnp.dot(
        left[...], jnp.concatenate([head, tail, head], axis=0), preferred_element_type=jnp.float32
    )

    @pl.when(pl.program_id(0) < half)
    def _():
        mine[...] = value

    @pl.when(pl.program_id(0) >= half)
    def _():
        given[...] = value


def inner(low, up, left, rows):
    nodes, piece, width = rows.shape
    count = nodes * (nodes + 1) // 2
    half = count // 2
    shape = jax.ShapeDtypeStruct((half, width, width), jnp.float32)
    return simple_call(
        functools.partial(inner_body, half), [low, up, left, rows],
        [
            pl.BlockSpec((None, width, left.shape[2]), lambda at, low, up: (low[at], 0, 0)),
            pl.BlockSpec((None, piece, width), lambda at, low, up: (up[at], 0, 0)),
        ],
        [shape, shape],
        [
            pl.BlockSpec((None, width, width), lambda at, *_: (jnp.minimum(at, half - 1), 0, 0)),
            pl.BlockSpec((None, width, width), lambda at, *_: (jnp.maximum(at - half, 0), 0, 0)),
        ],
        (count,), 2,
    )


def deal_body(plain, coded, count, starts, *refs):
    total = refs[0][...]
    for ref in refs[1:plain]:
        total = total + ref[...]
    for ref in refs[plain : plain + coded]:
        total = total + get_coded(ref)
    outs = refs[plain + coded :]
    if count == 1:
        put_coded(outs[0], total)
        return
    whole = outs[-1]
    whole[...] = total
    rows = total.shape[0] // count
    for at in range(count):
        part = whole[pl.ds(pl.multiple_of(starts[at], 8), rows), :]
        if at == 0:
            outs[0][...] = part
        else:
            put_coded(outs[at], part)


def deal(plain, coded, starts):
    rows, width = plain[0].shape
    lane_step = step_of(width)
    count = starts.shape[0]
    column = lambda rows: pl.BlockSpec((rows, lane_step), lambda at, starts: (0, at))
    part = rows // count
    shapes = [jax.ShapeDtypeStruct((part, width), jnp.float32)] if count > 1 else []
    shapes += [jax.ShapeDtypeStruct((part + pad_rows, width), jnp.int16)] * max(count - 1, 1)
    return simple_call(
        functools.partial(deal_body, len(plain), len(coded), count),
        [starts, *plain, *coded],
        [column(rows)] * len(plain) + [column(rows + pad_rows)] * len(coded),
        shapes, [column(shape.shape[0]) for shape in shapes], (width // lane_step,), 1,
        scratch_shapes=[pltpu.VMEM((rows, lane_step), jnp.float32)] if count > 1 else [],
    )


def heap_body(*refs):
    for at, ref in enumerate(refs[:-1]):
        refs[-1][at] = ref[...]


def heap(parts):
    rows, width = parts[0].shape
    lane_step = step_of(width)
    return simple_call(
        heap_body, parts,
        [pl.BlockSpec((rows, lane_step), lambda at: (0, at))] * len(parts),
        jax.ShapeDtypeStruct((len(parts), rows, width), parts[0].dtype),
        pl.BlockSpec((len(parts), rows, lane_step), lambda at: (0, 0, at)),
        (width // lane_step,),
    )


def finish_body(arrays, width, place, row_of, col_of, *refs):
    parts = refs[:arrays]
    base, out, sums = refs[arrays:]
    step = pl.program_id(0)
    count, padded, _ = parts[0].shape
    rows = padded - pad_rows

    @pl.when(step == 0)
    def _():
        for at, ref in enumerate(parts):
            for piece in range(count):
                start = pl.multiple_of(place[at * count + piece], 8)
                sums[pl.ds(start, rows), :] = get_coded(ref, (piece,))

    row, col = row_of[step], col_of[step]
    low, up = jnp.minimum(row, col), jnp.maximum(row, col)
    start = pl.multiple_of((up * (up + 1) // 2 + low) * width, width)
    value = base[...] - sums[pl.ds(start, width), :]

    @pl.when(row <= col)
    def _():
        out[...] = value

    @pl.when(row > col)
    def _():
        out[...] = value.T


def finish(place, parts, base, nodes, width):
    visits = []
    for up in range(nodes):
        for low in range(up):
            visits += [(low, up), (up, low)]
        visits.append((up, up))
    row_of = jnp.asarray([row for row, _ in visits], jnp.int32)
    col_of = jnp.asarray([col for _, col in visits], jnp.int32)

    def base_map(step, place, row_of, col_of):
        low = jnp.minimum(row_of[step], col_of[step])
        up = jnp.maximum(row_of[step], col_of[step])
        return (up * (up + 1) // 2 + low, 0, 0)

    whole = pl.BlockSpec(parts[0].shape, lambda step, *_: (0, 0, 0))
    return simple_call(
        functools.partial(finish_body, len(parts), width),
        [place, row_of, col_of, *parts, base],
        [whole] * len(parts) + [pl.BlockSpec((None, width, width), base_map)],
        jax.ShapeDtypeStruct((nodes, nodes, width, width), jnp.float32),
        pl.BlockSpec(
            (None, None, width, width),
            lambda step, place, row_of, col_of: (row_of[step], col_of[step], 0, 0),
        ),
        (nodes * nodes,), 3,
        scratch_shapes=[pltpu.VMEM((nodes * (nodes + 1) // 2 * width, width), jnp.float32)],
    )


def spread_bits(number, bits):
    return sum(((number >> at) & 1) << bit for at, bit in enumerate(bits))


def gather_bits(index, bits):
    return sum(((index >> bit) & 1) << at for at, bit in enumerate(bits))


def local(ancestor_inverse, factor, coupling, diagonal_inverse, ancestors):
    row_count = lax.axis_size("row")
    col_count = lax.axis_size("col")
    total = row_count * col_count
    row_index = lax.axis_index("row")
    col_index = lax.axis_index("col")
    flat_index = row_index * col_count + col_index
    nodes, piece_rows, width = factor.shape
    col_bits = col_count.bit_length() - 1
    first_row = (flat_index * piece_rows).reshape(1).astype(jnp.int32)
    *lower, lower_stack = prepare(factor, ancestors, first_row)

    order = ring_order(col_count)
    sources = ring_sources(order, col_index)
    core = (row_index % 2).reshape(1).astype(jnp.int32)
    moves = ring_moves(order)
    lanes = row_count // 2
    steps = col_count // 2
    near, early = 3, 1 + 2 * (steps - 2)
    gathered = [[lower[node]] for node in range(nodes)]

    def advance(step):
        for node in range(nodes):
            gathered[node] = ring_step(gathered[node], moves, step == steps)

    for step in range(1, steps - 1):
        advance(step)

    early_coupling = after(coupling, gathered[0][1])
    turned_heads, turned_tails = split_terms(jnp.swapaxes(early_coupling, 1, 2))
    first_pieces = [group[:near] for group in gathered]
    first_pieces[0][0], turned_heads, turned_tails = lax.optimization_barrier(
        (first_pieces[0][0], turned_heads, turned_tails)
    )
    starts = partial_product(first_pieces, ancestor_inverse, sources[:near])
    advance(steps - 1)
    starts = partial_product(
        [group[near:early] for group in gathered],
        ancestor_inverse,
        sources[near:early],
        starts,
    )
    advance(steps)

    swap = (1 << col_bits) | 1

    def middle(at):
        low, up = at & 1, (at >> col_bits) & 1
        return at if low == up else at ^ swap

    first_moves = [(at, middle(at)) for at in range(total)]
    last_moves = [
        (middle(r * col_count + c), c * row_count + r)
        for r in range(row_count)
        for c in range(col_count)
    ]
    lower_stack = lax.ppermute(
        lower_stack,
        both,
        [
            (c * row_count + r, r * col_count + c)
            for r in range(row_count)
            for c in range(col_count)
            if c * row_count + r != r * col_count + c
        ],
    )

    lane = row_index // 2
    lane_ref = lane.reshape(1).astype(jnp.int32)
    sibling = [(at, at ^ 1) for at in range(row_count)]
    lane_moves = [
        [(at, (at + 2 * shift) % row_count) for at in range(row_count)]
        for shift in range(1, lanes)
    ]

    def lane_sums(given, kept):
        other = lax.ppermute(given, "row", sibling)
        mine, *coded = add_encode(kept, other, lane_ref, lanes)
        return mine, [
            lax.ppermute(part, "row", moves)
            for part, moves in zip(coded, lane_moves, strict=True)
        ]

    base = {}

    def base_columns(columns, others):
        here, diagonal = lax.optimization_barrier((coupling, diagonal_inverse, *others))[:2]
        for k in columns:
            for j in range(k):
                value = -matmul(base[j, 0], here[pair_index(k, 0)])
                for i in range(1, k):
                    value = value - matmul(base[j, i], here[pair_index(k, i)])
                base[j, k] = value
                base[k, j] = value.T
            value = diagonal[k]
            for j in range(k):
                value = value - left_dot(here[pair_index(k, j)], base[j, k])
            base[k, k] = value

    by_cols = []
    out_cols = out_rows = None
    for k in range(nodes):
        given, kept = final_product(
            k, gathered[k][early:], ancestor_inverse, sources[early:], core, lanes, starts
        )
        row_sums = lane_sums(given, kept)
        if k == nodes - 1:
            base_columns(range(k), by_cols[-1:])
            held = lax.optimization_barrier((row_sums[0], base[k - 1, k - 1]))
            row_sums, base[k - 1, k - 1] = (held[0], row_sums[1]), held[1]
        value, coded, out_cols = chain(
            k, nodes, *row_sums, turned_heads, turned_tails, by_cols, out_cols
        )
        by_cols.append(value)
        coded = lax.ppermute(coded, both, first_moves)
        coded = lax.ppermute(coded, both, last_moves)
        out_rows = turn(k, nodes, coded, out_rows)

    stays = col_index * row_count + row_index == flat_index
    lower_stack, late_coupling, _ = lax.optimization_barrier((lower_stack, coupling, by_cols[-2]))
    mixed = []
    for k in range(nodes):
        value = jnp.where(stays, lower[k], lower_stack[k]).astype(jnp.float32)
        for j in range(k):
            value = value - left_dot(late_coupling[pair_index(k, j)], mixed[j])
        mixed.append(value)
    mixed_heads, mixed_tails = split_terms(jnp.stack(mixed))
    left = jnp.concatenate([mixed_tails, mixed_heads, mixed_heads], axis=2)

    count = nodes * (nodes + 1) // 2
    listing = [(j, k) for k in range(nodes) for j in range(k + 1)]
    turned_listing = listing[count // 2 :] + listing[: count // 2]

    def by_core(at):
        one, two = ([pair[at] for pair in pairs] for pairs in (listing, turned_listing))
        return jnp.where(core[0] == 0, jnp.asarray(one, jnp.int32), jnp.asarray(two, jnp.int32))

    low, up = by_core(0), by_core(1)
    kept, given = inner(low, up, left, out_cols)
    half_rows = kept.shape[0] * width
    kept, given = kept.reshape(half_rows, width), given.reshape(half_rows, width)
    flat_bits = (row_count * col_count).bit_length() - 1
    planes = [[0, *range(col_bits + 1, flat_bits)], list(range(1, col_bits))]
    plane_moves = [
        [[(at, at ^ spread_bits(other, bits)) for at in range(total)] for other in range(1, 1 << len(bits))]
        for bits in planes
    ]
    parts_of = [1 << len(bits) for bits in planes]
    mine_of = [gather_bits(flat_index, bits) for bits in planes]

    def starts_of(level, rows):
        around = mine_of[level] ^ jnp.arange(parts_of[level], dtype=jnp.int32)
        return (around * (rows // parts_of[level])).astype(jnp.int32)

    def exchange(arrays, level):
        return [
            lax.ppermute(array, both, moves)
            for array, moves in zip(arrays, plane_moves[level], strict=True)
        ]

    other = lax.ppermute(given, "row", sibling)
    mine, *coded = deal([kept, other], [], starts_of(0, half_rows))
    coded = exchange(coded, 0)
    base_columns(range(nodes - 1, nodes), [mine])
    base = jnp.stack([base[j, k] for k in range(nodes) for j in range(k + 1)])
    mine, base = lax.optimization_barrier((mine, base))
    mine, *coded = deal([mine], coded, starts_of(1, mine.shape[0]))
    coded = exchange(coded, 1)
    (summed,) = deal([mine], coded, jnp.zeros((1,), jnp.int32))
    pile = heap([summed, *exchange([summed] * (parts_of[1] - 1), 1)])
    piles = [pile, *exchange([pile] * (parts_of[0] - 1), 0)]
    *late, out_rows = lax.optimization_barrier((*piles[2:], out_rows))
    piles = [*piles[:2], *late]
    piles += [lax.ppermute(pile, "row", sibling) for pile in piles]
    rows_at = half_rows // (parts_of[0] * parts_of[1])
    around = [mine_of[at] ^ jnp.arange(parts_of[at], dtype=jnp.int32) for at in range(2)]
    within = (around[0][:, None] * parts_of[1] + around[1][None, :]).reshape(-1) * rows_at
    place = jnp.concatenate(
        [core[0] * half_rows + within, (1 - core[0]) * half_rows + within]
    ).astype(jnp.int32)
    pile, base = lax.optimization_barrier((piles[0], base))
    node_blocks = finish(place, [pile, *piles[1:]], base, nodes, width)
    return out_rows, out_cols, node_blocks


def solution(mesh):
    placed = (P("row", "col"), P(None, both, None), P(), P(), P())

    return jax.shard_map(
        local,
        mesh=mesh,
        in_specs=placed,
        out_specs=(P(None, both, None), P(None, ("col", "row"), None), P()),
        check_vma=False,
    )
```

```python
import functools

import jax
import jax.numpy as jnp
from jax import lax
from jax.experimental import pallas as pl
from jax.experimental.pallas import tpu as pltpu
from jax.sharding import PartitionSpec as P

both = ("row", "col")
high = lax.Precision.HIGH


def matmul(left, right):
    return jnp.dot(left, right, precision=high)


def left_dot(left, right):
    return lax.dot_general(left, right, (((0,), (0,)), ((), ())), precision=high)


def pair_index(later, earlier):
    return later * (later - 1) // 2 + earlier


def split_terms(value):
    head = lax.reduce_precision(value, 8, 7)
    return head.astype(jnp.bfloat16), (value - head).astype(jnp.bfloat16)


def after(value, *others):
    return lax.optimization_barrier((value, *others))[0]


def ring_order(count):
    return list(range(0, count, 2)) + list(range(count - 1, 0, -2))


def ring_moves(order):
    count = len(order)
    ahead = [(order[at], order[(at + 1) % count]) for at in range(count)]
    return ahead, [(target, source) for source, target in ahead]


def ring_step(pieces, moves, last):
    up, down = (pieces[0], pieces[0]) if len(pieces) == 1 else pieces[-2:]
    if last:
        half = up.shape[0] // 2
        up, down = up[:half], down[half:]
    return [*pieces, lax.ppermute(up, "col", moves[0]), lax.ppermute(down, "col", moves[1])]


def ring_sources(order, col_index):
    count = len(order)
    place = [0] * count
    for at, device in enumerate(order):
        place[device] = at
    my_place = jnp.asarray(place, jnp.int32)[col_index]
    table = jnp.asarray(order, jnp.int32)
    steps = [0]
    for step in range(1, count // 2):
        steps += [-step, step]
    steps.append(count // 2)
    return table[(my_place + jnp.asarray(steps, jnp.int32)) % count]


def two_terms(block):
    value = block[...]
    head = value.astype(jnp.bfloat16)
    tail = (value - head.astype(jnp.float32)).astype(jnp.bfloat16)
    return jnp.concatenate([head, tail], axis=0)


def put_double(doubled, piece, span=slice(None)):
    depth = piece.shape[1]
    doubled[span, :depth] = piece[...]
    doubled[span, depth:] = piece[...]


def add_product(doubled, terms, total, first, start):
    cols = total.shape[1]
    count = 3 if cols % 384 == 0 else 1
    span = cols // count

    def add(at, carry):
        here = pl.ds(pl.multiple_of(at * span, span), span)
        part = jnp.dot(doubled[...], terms[:, here], preferred_element_type=jnp.float32)
        begin = jnp.zeros_like(part) if start is None else start[:, here]
        total[:, here] = jnp.where(first, begin, total[:, here]) + part
        return carry

    lax.fori_loop(0, count, add, 0)


def partial_body(nodes, count, resume, sources, *refs):
    pieces = refs[: nodes * count]
    block = refs[nodes * count]
    total, doubled, terms = refs[-3:]
    node, step = pl.program_id(0), pl.program_id(1)
    for at, piece in enumerate(pieces):

        @pl.when((node == at // count) & (step == at % count))
        def _(piece=piece):
            put_double(doubled, piece)

    terms[...] = two_terms(block)
    start = refs[nodes * count + 1] if resume else None
    add_product(doubled, terms, total, step == 0, start)


def final_body(count, lanes, out_piece, sources, core, *refs):
    pieces = refs[: count + 1]
    block, start, given, kept, total, doubled, terms = refs[count + 1 :]
    step = pl.program_id(0)
    for at in range(count - 1):

        @pl.when(step == at)
        def _(at=at):
            put_double(doubled, pieces[at])

    @pl.when(step == count - 1)
    def _():
        half = pieces[count].shape[0]
        put_double(doubled, pieces[count - 1], slice(0, half))
        put_double(doubled, pieces[count], slice(half, 2 * half))

    terms[...] = two_terms(block)
    add_product(doubled, terms, total, step == 0, start)

    @pl.when(step == count - 1)
    def _():
        for lane in range(lanes):
            for side in range(2):
                first = (2 * lane + side) * out_piece

                @pl.when(core[0] == side)
                def _(lane=lane, first=first):
                    kept[lane] = total[:, first : first + out_piece]

                @pl.when(core[0] != side)
                def _(lane=lane, first=first):
                    given[lane] = total[:, first : first + out_piece]


def product_call(body, grid, prefetch, args, in_specs, out_shape, out_specs, scratch, flops, **more):
    return pl.pallas_call(
        body,
        grid_spec=pltpu.PrefetchScalarGridSpec(
            num_scalar_prefetch=prefetch,
            grid=grid,
            in_specs=in_specs,
            out_specs=out_specs,
            scratch_shapes=scratch,
        ),
        out_shape=out_shape,
        compiler_params=pltpu.CompilerParams(
            dimension_semantics=("arbitrary",) * len(grid), vmem_limit_bytes=56 << 20
        ),
        cost_estimate=pl.CostEstimate(
            flops=flops, bytes_accessed=flops // 512, transcendentals=0
        ),
        **more,
    )(*args)


def partial_product(groups, block, sources, start=None):
    nodes, count = len(groups), len(groups[0])
    width, piece = groups[0][0].shape
    cols = block.shape[1]
    pieces = [array for group in groups for array in group]
    total = pl.BlockSpec((None, width, cols), lambda node, step, sources: (node, 0, 0))
    in_specs = [pl.BlockSpec(pieces[0].shape, lambda node, step, sources: (0, 0))] * len(pieces)
    in_specs.append(pl.BlockSpec((piece, cols), lambda node, step, sources: (sources[step], 0)))
    args = [sources, *pieces, block]
    aliases = {}
    if start is not None:
        aliases = {len(args): 0}
        in_specs.append(total)
        args.append(start)
    return product_call(
        functools.partial(partial_body, nodes, count, start is not None),
        (nodes, count), 1, args, in_specs,
        jax.ShapeDtypeStruct((nodes, width, cols), jnp.float32), total,
        [
            pltpu.VMEM((width, 2 * piece), jnp.bfloat16),
            pltpu.VMEM((2 * piece, cols), jnp.bfloat16),
        ],
        4 * nodes * count * width * piece * cols, input_output_aliases=aliases,
    )


def final_product(node, pieces, block, sources, core, lanes, start):
    count = len(pieces) - 1
    width, piece = pieces[0].shape
    cols = block.shape[1]
    out_piece = cols // (2 * lanes)
    half = jax.ShapeDtypeStruct((lanes, width, out_piece), jnp.float32)
    half_spec = pl.BlockSpec(half.shape, lambda step, *_: (0, 0, 0))
    in_specs = [pl.BlockSpec(array.shape, lambda step, *_: (0, 0)) for array in pieces]
    in_specs.append(pl.BlockSpec((piece, cols), lambda step, sources, core: (sources[step], 0)))
    in_specs.append(pl.BlockSpec((None, width, cols), lambda step, *_: (node, 0, 0)))
    return product_call(
        functools.partial(final_body, count, lanes, out_piece), (count,), 2,
        [sources, core, *pieces, block, start], in_specs, [half, half], [half_spec, half_spec],
        [
            pltpu.VMEM((width, cols), jnp.float32),
            pltpu.VMEM((width, 2 * piece), jnp.bfloat16),
            pltpu.VMEM((2 * piece, cols), jnp.bfloat16),
        ],
        4 * count * width * piece * cols,
    )


pad_rows = 16


def step_of(lanes):
    return 128 if lanes % 128 == 0 else lanes


def encoded(value):
    top = jnp.max(jnp.abs(value), axis=-2, keepdims=True)
    exponent = jnp.ceil(jnp.log2(jnp.maximum(top, 1e-30)) + 0.01)
    whole = jnp.round(value * jnp.exp2(15.0 - exponent)).astype(jnp.int32)
    wide = jnp.broadcast_to(exponent, (pad_rows, value.shape[-1])).astype(jnp.int32)
    return whole.astype(jnp.int16), wide.astype(jnp.int16)


def put_coded(ref, value, lead=()):
    rows = value.shape[0]
    whole, wide = encoded(value)
    ref[(*lead, slice(0, rows), slice(None))] = whole
    ref[(*lead, slice(rows, rows + pad_rows), slice(None))] = wide


def get_coded(ref, lead=()):
    rows = ref.shape[-2] - pad_rows
    whole = ref[(*lead, slice(0, rows), slice(None))].astype(jnp.int32).astype(jnp.float32)
    wide = ref[(*lead, slice(rows, rows + pad_rows), slice(None))].astype(jnp.int32)
    return whole * jnp.exp2(wide.astype(jnp.float32)[0:1, :] - 15.0)


def simple_call(body, args, in_specs, out_shape, out_specs, grid, prefetch=0, **more):
    size = sum(array.size * array.dtype.itemsize for array in args)
    return pl.pallas_call(
        body,
        grid_spec=pltpu.PrefetchScalarGridSpec(
            num_scalar_prefetch=prefetch,
            grid=grid,
            in_specs=in_specs,
            out_specs=out_specs,
            scratch_shapes=more.pop("scratch_shapes", ()),
        ),
        out_shape=out_shape,
        compiler_params=pltpu.CompilerParams(
            dimension_semantics=("arbitrary",) * len(grid), vmem_limit_bytes=48 << 20
        ),
        cost_estimate=pl.CostEstimate(flops=size, bytes_accessed=size, transcendentals=0),
        **more,
    )(*args)


def prepare_body(nodes, block_rows, first_row, ancestors, *refs):
    source, outs = refs[0], refs[1:]
    rows = source.shape[1]
    slots = ancestors.shape[1]
    row = lax.broadcasted_iota(jnp.int32, (rows, 1), 0) + first_row[0]
    first_block = lax.div(first_row[0], block_rows)
    for node in range(nodes):
        keep = None
        for ahead in range((rows - 1) // block_rows + 2):
            block = first_block + ahead
            listed = ancestors[node, 0] == block
            for slot in range(1, slots):
                listed = listed | (ancestors[node, slot] == block)
            inside = (row >= block * block_rows) & (row < (block + 1) * block_rows) & listed
            keep = inside if keep is None else keep | inside
        value = jnp.where(keep, source[node].astype(jnp.float32), 0.0)
        turned = value.T.astype(jnp.bfloat16)
        outs[node][...] = turned
        outs[nodes][node] = turned


def prepare(factor, ancestors, first_row):
    nodes, rows, width = factor.shape
    shape = jax.ShapeDtypeStruct((width, rows), jnp.bfloat16)
    spec = pl.BlockSpec((width, rows), lambda at, *_: (0, 0))
    return simple_call(
        functools.partial(prepare_body, nodes, width),
        [first_row, ancestors, factor],
        [pl.BlockSpec(factor.shape, lambda at, *_: (0, 0, 0))],
        [shape] * nodes + [jax.ShapeDtypeStruct((nodes, width, rows), jnp.bfloat16)],
        [spec] * nodes + [pl.BlockSpec((nodes, width, rows), lambda at, *_: (0, 0, 0))],
        (1,), 2,
    )


def add_encode_body(shifts, lane, *refs):
    total = refs[2 * (shifts + 1)]
    total[...] = refs[0][...] + refs[1][...]
    for at in range(shifts):
        value = refs[2 * at + 2][...] + refs[2 * at + 3][...]
        put_coded(refs[2 * (shifts + 1) + 1 + at], value)


def add_encode(kept, other, lane, lanes):
    _, rows, width = kept.shape
    lane_step = step_of(width)
    in_specs, args = [], []
    for shift in range(lanes):
        spec = pl.BlockSpec(
            (None, rows, lane_step),
            lambda at, lane, shift=shift: (lax.rem(lane[0] + shift, lanes), 0, at),
        )
        in_specs += [spec, spec]
        args += [kept, other]
    out_specs = [pl.BlockSpec((rows, lane_step), lambda at, lane: (0, at))]
    out_shape = [jax.ShapeDtypeStruct((rows, width), jnp.float32)]
    for _ in range(1, lanes):
        out_specs.append(pl.BlockSpec((rows + pad_rows, lane_step), lambda at, lane: (0, at)))
        out_shape.append(jax.ShapeDtypeStruct((rows + pad_rows, width), jnp.int16))
    return simple_call(
        functools.partial(add_encode_body, lanes - 1), [lane, *args], in_specs,
        out_shape, out_specs, (width // lane_step,), 1,
    )


def split_dots(pairs):
    total = None
    for (left_head, left_tail), right in pairs:
        right_head = right.astype(jnp.bfloat16)
        right_tail = (right - right_head.astype(jnp.float32)).astype(jnp.bfloat16)
        for left, value in ((left_tail, right_head), (left_head, right_tail), (left_head, right_head)):
            part = jnp.dot(left, value, preferred_element_type=jnp.float32)
            total = part if total is None else total + part
    return total


def chain_body(node, lanes, *refs):
    mine, *received = refs[:lanes]
    heads = refs[lanes : lanes + node]
    tails = refs[lanes + node : lanes + 2 * node]
    earlier = refs[lanes + 2 * node : lanes + 3 * node]
    value, coded, turned = refs[-3:]
    total = mine[...]
    for ref in received:
        total = total + get_coded(ref)
    if node:
        total = total + split_dots(
            [((h[...], t[...]), e[...]) for h, t, e in zip(heads, tails, earlier, strict=True)]
        )
    total = -total
    value[...] = total
    put_coded(coded, total)
    turned[...] = total.T


def chain(node, nodes, mine, received, heads, tails, earlier, turned):
    rows, width = mine.shape
    lane_step = step_of(width)
    lanes = 1 + len(received)
    first = node * (node - 1) // 2
    column = lambda rows: pl.BlockSpec((rows, lane_step), lambda at: (0, at))
    in_specs = [column(rows)] + [column(rows + pad_rows)] * len(received)
    factor_specs = [
        pl.BlockSpec((None, rows, rows), lambda at, j=j: (first + j, 0, 0)) for j in range(node)
    ]
    in_specs += factor_specs + factor_specs + [column(rows)] * node
    args = [mine, *received, *[heads] * node, *[tails] * node, *earlier]
    aliases = {}
    if turned is not None:
        aliases = {len(args): 2}
        args.append(turned)
        in_specs.append(pl.BlockSpec(memory_space=pl.ANY))
    return simple_call(
        functools.partial(chain_body, node, lanes), args, in_specs,
        [
            jax.ShapeDtypeStruct((rows, width), jnp.float32),
            jax.ShapeDtypeStruct((rows + pad_rows, width), jnp.int16),
            jax.ShapeDtypeStruct((nodes, width, rows), jnp.float32),
        ],
        [
            column(rows),
            column(rows + pad_rows),
            pl.BlockSpec((None, lane_step, rows), lambda at: (node, at, 0)),
        ],
        (width // lane_step,), input_output_aliases=aliases,
    )


def turn_body(*refs):
    refs[-1][...] = get_coded(refs[0]).T


def turn(node, nodes, coded, turned):
    padded, width = coded.shape
    lane_step = step_of(width)
    rows = padded - pad_rows
    args, in_specs = [coded], [pl.BlockSpec((padded, lane_step), lambda at: (0, at))]
    aliases = {}
    if turned is not None:
        aliases = {1: 0}
        args.append(turned)
        in_specs.append(pl.BlockSpec(memory_space=pl.ANY))
    return simple_call(
        turn_body, args, in_specs,
        jax.ShapeDtypeStruct((nodes, width, rows), jnp.float32),
        pl.BlockSpec((None, lane_step, rows), lambda at: (node, at, 0)),
        (width // lane_step,), input_output_aliases=aliases,
    )


def inner_body(half, low, up, left, rows, mine, given):
    value = rows[...]
    head = value.astype(jnp.bfloat16)
    tail = (value - head.astype(jnp.float32)).astype(jnp.bfloat16)
    value = jnp.dot(
        left[...], jnp.concatenate([head, tail, head], axis=0), preferred_element_type=jnp.float32
    )

    @pl.when(pl.program_id(0) < half)
    def _():
        mine[...] = value

    @pl.when(pl.program_id(0) >= half)
    def _():
        given[...] = value


def inner(low, up, left, rows):
    nodes, piece, width = rows.shape
    count = nodes * (nodes + 1) // 2
    half = count // 2
    shape = jax.ShapeDtypeStruct((half, width, width), jnp.float32)
    return simple_call(
        functools.partial(inner_body, half), [low, up, left, rows],
        [
            pl.BlockSpec((None, width, left.shape[2]), lambda at, low, up: (low[at], 0, 0)),
            pl.BlockSpec((None, piece, width), lambda at, low, up: (up[at], 0, 0)),
        ],
        [shape, shape],
        [
            pl.BlockSpec((None, width, width), lambda at, *_: (jnp.minimum(at, half - 1), 0, 0)),
            pl.BlockSpec((None, width, width), lambda at, *_: (jnp.maximum(at - half, 0), 0, 0)),
        ],
        (count,), 2,
    )


def deal_body(plain, coded, count, starts, *refs):
    total = refs[0][...]
    for ref in refs[1:plain]:
        total = total + ref[...]
    for ref in refs[plain : plain + coded]:
        total = total + get_coded(ref)
    outs = refs[plain + coded :]
    if count == 1:
        put_coded(outs[0], total)
        return
    whole = outs[-1]
    whole[...] = total
    rows = total.shape[0] // count
    for at in range(count):
        part = whole[pl.ds(pl.multiple_of(starts[at], 8), rows), :]
        if at == 0:
            outs[0][...] = part
        else:
            put_coded(outs[at], part)


def deal(plain, coded, starts):
    rows, width = plain[0].shape
    lane_step = step_of(width)
    count = starts.shape[0]
    column = lambda rows: pl.BlockSpec((rows, lane_step), lambda at, starts: (0, at))
    part = rows // count
    shapes = [jax.ShapeDtypeStruct((part, width), jnp.float32)] if count > 1 else []
    shapes += [jax.ShapeDtypeStruct((part + pad_rows, width), jnp.int16)] * max(count - 1, 1)
    return simple_call(
        functools.partial(deal_body, len(plain), len(coded), count),
        [starts, *plain, *coded],
        [column(rows)] * len(plain) + [column(rows + pad_rows)] * len(coded),
        shapes, [column(shape.shape[0]) for shape in shapes], (width // lane_step,), 1,
        scratch_shapes=[pltpu.VMEM((rows, lane_step), jnp.float32)] if count > 1 else [],
    )


def heap_body(*refs):
    for at, ref in enumerate(refs[:-1]):
        refs[-1][at] = ref[...]


def heap(parts):
    rows, width = parts[0].shape
    lane_step = step_of(width)
    return simple_call(
        heap_body, parts,
        [pl.BlockSpec((rows, lane_step), lambda at: (0, at))] * len(parts),
        jax.ShapeDtypeStruct((len(parts), rows, width), parts[0].dtype),
        pl.BlockSpec((len(parts), rows, lane_step), lambda at: (0, 0, at)),
        (width // lane_step,),
    )


def finish_body(arrays, width, place, row_of, col_of, *refs):
    parts = refs[:arrays]
    base, out, sums = refs[arrays:]
    step = pl.program_id(0)
    count, padded, _ = parts[0].shape
    rows = padded - pad_rows

    @pl.when(step == 0)
    def _():
        for at, ref in enumerate(parts):

            def put(piece, carry, at=at, ref=ref):
                start = pl.multiple_of(place[at * count + piece], 8)
                sums[pl.ds(start, rows), :] = get_coded(ref, (piece,))
                return carry

            lax.fori_loop(0, count, put, 0)

    row, col = row_of[step], col_of[step]
    low, up = jnp.minimum(row, col), jnp.maximum(row, col)
    start = pl.multiple_of((up * (up + 1) // 2 + low) * width, width)
    value = base[...] - sums[pl.ds(start, width), :]

    @pl.when(row <= col)
    def _():
        out[...] = value

    @pl.when(row > col)
    def _():
        out[...] = value.T


def finish(place, parts, base, nodes, width):
    visits = []
    for up in range(nodes):
        for low in range(up):
            visits += [(low, up), (up, low)]
        visits.append((up, up))
    row_of = jnp.asarray([row for row, _ in visits], jnp.int32)
    col_of = jnp.asarray([col for _, col in visits], jnp.int32)

    def base_map(step, place, row_of, col_of):
        low = jnp.minimum(row_of[step], col_of[step])
        up = jnp.maximum(row_of[step], col_of[step])
        return (up * (up + 1) // 2 + low, 0, 0)

    whole = pl.BlockSpec(parts[0].shape, lambda step, *_: (0, 0, 0))
    return simple_call(
        functools.partial(finish_body, len(parts), width),
        [place, row_of, col_of, *parts, base],
        [whole] * len(parts) + [pl.BlockSpec((None, width, width), base_map)],
        jax.ShapeDtypeStruct((nodes, nodes, width, width), jnp.float32),
        pl.BlockSpec(
            (None, None, width, width),
            lambda step, place, row_of, col_of: (row_of[step], col_of[step], 0, 0),
        ),
        (nodes * nodes,), 3,
        scratch_shapes=[pltpu.VMEM((nodes * (nodes + 1) // 2 * width, width), jnp.float32)],
    )


def spread_bits(number, bits):
    return sum(((number >> at) & 1) << bit for at, bit in enumerate(bits))


def gather_bits(index, bits):
    return sum(((index >> bit) & 1) << at for at, bit in enumerate(bits))


def local(ancestor_inverse, factor, coupling, diagonal_inverse, ancestors):
    row_count = lax.axis_size("row")
    col_count = lax.axis_size("col")
    total = row_count * col_count
    row_index = lax.axis_index("row")
    col_index = lax.axis_index("col")
    flat_index = row_index * col_count + col_index
    nodes, piece_rows, width = factor.shape
    col_bits = col_count.bit_length() - 1
    first_row = (flat_index * piece_rows).reshape(1).astype(jnp.int32)
    *lower, lower_stack = prepare(factor, ancestors, first_row)

    order = ring_order(col_count)
    sources = ring_sources(order, col_index)
    core = (row_index % 2).reshape(1).astype(jnp.int32)
    moves = ring_moves(order)
    lanes = row_count // 2
    steps = col_count // 2
    near, early = 3, 1 + 2 * (steps - 2)
    gathered = [[lower[node]] for node in range(nodes)]

    def advance(step):
        for node in range(nodes):
            gathered[node] = ring_step(gathered[node], moves, step == steps)

    for step in range(1, steps - 1):
        advance(step)

    early_coupling = after(coupling, gathered[0][1])
    turned_heads, turned_tails = split_terms(jnp.swapaxes(early_coupling, 1, 2))
    first_pieces = [group[:near] for group in gathered]
    first_pieces[0][0], turned_heads, turned_tails = lax.optimization_barrier(
        (first_pieces[0][0], turned_heads, turned_tails)
    )
    starts = partial_product(first_pieces, ancestor_inverse, sources[:near])
    advance(steps - 1)
    starts = partial_product(
        [group[near:early] for group in gathered],
        ancestor_inverse,
        sources[near:early],
        starts,
    )
    advance(steps)

    swap = (1 << col_bits) | 1

    def middle(at):
        low, up = at & 1, (at >> col_bits) & 1
        return at if low == up else at ^ swap

    first_moves = [(at, middle(at)) for at in range(total)]
    last_moves = [
        (middle(r * col_count + c), c * row_count + r)
        for r in range(row_count)
        for c in range(col_count)
    ]
    lower_stack = lax.ppermute(
        lower_stack,
        both,
        [
            (c * row_count + r, r * col_count + c)
            for r in range(row_count)
            for c in range(col_count)
            if c * row_count + r != r * col_count + c
        ],
    )

    lane = row_index // 2
    lane_ref = lane.reshape(1).astype(jnp.int32)
    sibling = [(at, at ^ 1) for at in range(row_count)]
    lane_moves = [
        [(at, (at + 2 * shift) % row_count) for at in range(row_count)]
        for shift in range(1, lanes)
    ]

    def lane_sums(given, kept):
        other = lax.ppermute(given, "row", sibling)
        mine, *coded = add_encode(kept, other, lane_ref, lanes)
        return mine, [
            lax.ppermute(part, "row", moves)
            for part, moves in zip(coded, lane_moves, strict=True)
        ]

    base = {}

    def base_columns(columns, others):
        here, diagonal = lax.optimization_barrier((coupling, diagonal_inverse, *others))[:2]
        for k in columns:
            for j in range(k):
                value = -matmul(base[j, 0], here[pair_index(k, 0)])
                for i in range(1, k):
                    value = value - matmul(base[j, i], here[pair_index(k, i)])
                base[j, k] = value
                base[k, j] = value.T
            value = diagonal[k]
            for j in range(k):
                value = value - left_dot(here[pair_index(k, j)], base[j, k])
            base[k, k] = value

    by_cols = []
    out_cols = out_rows = None
    for k in range(nodes):
        given, kept = final_product(
            k, gathered[k][early:], ancestor_inverse, sources[early:], core, lanes, starts
        )
        row_sums = lane_sums(given, kept)
        if k == nodes - 1:
            base_columns(range(k), by_cols[-1:])
            held = lax.optimization_barrier((row_sums[0], base[k - 1, k - 1]))
            row_sums, base[k - 1, k - 1] = (held[0], row_sums[1]), held[1]
        value, coded, out_cols = chain(
            k, nodes, *row_sums, turned_heads, turned_tails, by_cols, out_cols
        )
        by_cols.append(value)
        coded = lax.ppermute(coded, both, first_moves)
        coded = lax.ppermute(coded, both, last_moves)
        out_rows = turn(k, nodes, coded, out_rows)

    stays = col_index * row_count + row_index == flat_index
    lower_stack, late_coupling, _ = lax.optimization_barrier((lower_stack, coupling, by_cols[-2]))
    mixed = []
    for k in range(nodes):
        value = jnp.where(stays, lower[k], lower_stack[k]).astype(jnp.float32)
        for j in range(k):
            value = value - left_dot(late_coupling[pair_index(k, j)], mixed[j])
        mixed.append(value)
    mixed_heads, mixed_tails = split_terms(jnp.stack(mixed))
    left = jnp.concatenate([mixed_tails, mixed_heads, mixed_heads], axis=2)

    count = nodes * (nodes + 1) // 2
    listing = [(j, k) for k in range(nodes) for j in range(k + 1)]
    turned_listing = listing[count // 2 :] + listing[: count // 2]

    def by_core(at):
        one, two = ([pair[at] for pair in pairs] for pairs in (listing, turned_listing))
        return jnp.where(core[0] == 0, jnp.asarray(one, jnp.int32), jnp.asarray(two, jnp.int32))

    low, up = by_core(0), by_core(1)
    kept, given = inner(low, up, left, out_cols)
    half_rows = kept.shape[0] * width
    kept, given = kept.reshape(half_rows, width), given.reshape(half_rows, width)
    flat_bits = (row_count * col_count).bit_length() - 1
    planes = [[0, *range(col_bits + 1, flat_bits)], list(range(1, col_bits))]
    plane_moves = [
        [[(at, at ^ spread_bits(other, bits)) for at in range(total)] for other in range(1, 1 << len(bits))]
        for bits in planes
    ]
    parts_of = [1 << len(bits) for bits in planes]
    mine_of = [gather_bits(flat_index, bits) for bits in planes]

    def starts_of(level, rows):
        around = mine_of[level] ^ jnp.arange(parts_of[level], dtype=jnp.int32)
        return (around * (rows // parts_of[level])).astype(jnp.int32)

    def exchange(arrays, level):
        return [
            lax.ppermute(array, both, moves)
            for array, moves in zip(arrays, plane_moves[level], strict=True)
        ]

    other = lax.ppermute(given, "row", sibling)
    mine, *coded = deal([kept, other], [], starts_of(0, half_rows))
    coded = exchange(coded, 0)
    base_columns(range(nodes - 1, nodes), [mine])
    base = jnp.stack([base[j, k] for k in range(nodes) for j in range(k + 1)])
    mine, base = lax.optimization_barrier((mine, base))
    mine, *coded = deal([mine], coded, starts_of(1, mine.shape[0]))
    coded = exchange(coded, 1)
    (summed,) = deal([mine], coded, jnp.zeros((1,), jnp.int32))
    pile = heap([summed, *exchange([summed] * (parts_of[1] - 1), 1)])
    piles = [pile, *exchange([pile] * (parts_of[0] - 1), 0)]
    *late, out_rows = lax.optimization_barrier((*piles[2:], out_rows))
    piles = [*piles[:2], *late]
    piles += [lax.ppermute(pile, "row", sibling) for pile in piles]
    rows_at = half_rows // (parts_of[0] * parts_of[1])
    around = [mine_of[at] ^ jnp.arange(parts_of[at], dtype=jnp.int32) for at in range(2)]
    within = (around[0][:, None] * parts_of[1] + around[1][None, :]).reshape(-1) * rows_at
    place = jnp.concatenate(
        [core[0] * half_rows + within, (1 - core[0]) * half_rows + within]
    ).astype(jnp.int32)
    pile, base = lax.optimization_barrier((piles[0], base))
    node_blocks = finish(place, [pile, *piles[1:]], base, nodes, width)
    return out_rows, out_cols, node_blocks


def solution(mesh):
    placed = (P("row", "col"), P(None, both, None), P(), P(), P())

    return jax.shard_map(
        local,
        mesh=mesh,
        in_specs=placed,
        out_specs=(P(None, both, None), P(None, ("col", "row"), None), P()),
        check_vma=False,
    )
```

```python
import functools

import jax
import jax.numpy as jnp
from jax import lax
from jax.experimental import pallas as pl
from jax.experimental.pallas import tpu as pltpu
from jax.sharding import PartitionSpec as P

both = ("row", "col")
high = lax.Precision.HIGH


def matmul(left, right):
    return jnp.dot(left, right, precision=high)


def left_dot(left, right):
    return lax.dot_general(left, right, (((0,), (0,)), ((), ())), precision=high)


def pair_index(later, earlier):
    return later * (later - 1) // 2 + earlier


def split_terms(value):
    head = lax.reduce_precision(value, 8, 7)
    return head.astype(jnp.bfloat16), (value - head).astype(jnp.bfloat16)


def after(value, *others):
    return lax.optimization_barrier((value, *others))[0]


def ring_order(count):
    return list(range(0, count, 2)) + list(range(count - 1, 0, -2))


def ring_moves(order):
    count = len(order)
    ahead = [(order[at], order[(at + 1) % count]) for at in range(count)]
    return ahead, [(target, source) for source, target in ahead]


def ring_step(pieces, moves, last):
    up, down = (pieces[0], pieces[0]) if len(pieces) == 1 else pieces[-2:]
    if last:
        half = up.shape[0] // 2
        up, down = up[:half], down[half:]
    return [*pieces, lax.ppermute(up, "col", moves[0]), lax.ppermute(down, "col", moves[1])]


def ring_sources(order, col_index):
    count = len(order)
    place = [0] * count
    for at, device in enumerate(order):
        place[device] = at
    my_place = jnp.asarray(place, jnp.int32)[col_index]
    table = jnp.asarray(order, jnp.int32)
    steps = [0]
    for step in range(1, count // 2):
        steps += [-step, step]
    steps.append(count // 2)
    return table[(my_place + jnp.asarray(steps, jnp.int32)) % count]


def two_terms(block):
    value = block[...]
    head = value.astype(jnp.bfloat16)
    tail = (value - head.astype(jnp.float32)).astype(jnp.bfloat16)
    return jnp.concatenate([head, tail], axis=0)


def put_double(doubled, piece, span=slice(None)):
    depth = piece.shape[1]
    doubled[span, :depth] = piece[...]
    doubled[span, depth:] = piece[...]


def add_product(doubled, terms, total, first, start):
    cols = total.shape[1]
    count = 3 if cols % 384 == 0 else 1
    span = cols // count

    def add(at, carry):
        here = pl.ds(pl.multiple_of(at * span, span), span)
        part = jnp.dot(doubled[...], terms[:, here], preferred_element_type=jnp.float32)
        begin = jnp.zeros_like(part) if start is None else start[:, here]
        total[:, here] = jnp.where(first, begin, total[:, here]) + part
        return carry

    lax.fori_loop(0, count, add, 0)


def partial_body(nodes, count, resume, sources, *refs):
    pieces = refs[: nodes * count]
    block = refs[nodes * count]
    total, doubled, terms = refs[-3:]
    node, step = pl.program_id(0), pl.program_id(1)
    for at, piece in enumerate(pieces):

        @pl.when((node == at // count) & (step == at % count))
        def _(piece=piece):
            put_double(doubled, piece)

    terms[...] = two_terms(block)
    start = refs[nodes * count + 1] if resume else None
    add_product(doubled, terms, total, step == 0, start)


def final_body(count, lanes, out_piece, sources, core, *refs):
    pieces = refs[: count + 1]
    block, start, given, kept, total, doubled = refs[count + 1 :]
    step = pl.program_id(0)
    for at in range(count - 1):

        @pl.when(step == at)
        def _(at=at):
            put_double(doubled, pieces[at])

    @pl.when(step == count - 1)
    def _():
        half = pieces[count].shape[0]
        put_double(doubled, pieces[count - 1], slice(0, half))
        put_double(doubled, pieces[count], slice(half, 2 * half))

    part = jnp.dot(doubled[...], two_terms(block), preferred_element_type=jnp.float32)

    total[...] = jnp.where(step == 0, start[...], total[...]) + part

    @pl.when(step == count - 1)
    def _():
        for lane in range(lanes):
            for side in range(2):
                first = (2 * lane + side) * out_piece

                @pl.when(core[0] == side)
                def _(lane=lane, first=first):
                    kept[lane] = total[:, first : first + out_piece]

                @pl.when(core[0] != side)
                def _(lane=lane, first=first):
                    given[lane] = total[:, first : first + out_piece]


def product_call(body, grid, prefetch, args, in_specs, out_shape, out_specs, scratch, flops, **more):
    return pl.pallas_call(
        body,
        grid_spec=pltpu.PrefetchScalarGridSpec(
            num_scalar_prefetch=prefetch,
            grid=grid,
            in_specs=in_specs,
            out_specs=out_specs,
            scratch_shapes=scratch,
        ),
        out_shape=out_shape,
        compiler_params=pltpu.CompilerParams(
            dimension_semantics=("arbitrary",) * len(grid), vmem_limit_bytes=56 << 20
        ),
        cost_estimate=pl.CostEstimate(
            flops=flops, bytes_accessed=flops // 512, transcendentals=0
        ),
        **more,
    )(*args)


def partial_product(groups, block, sources, start=None):
    nodes, count = len(groups), len(groups[0])
    width, piece = groups[0][0].shape
    cols = block.shape[1]
    pieces = [array for group in groups for array in group]
    total = pl.BlockSpec((None, width, cols), lambda node, step, sources: (node, 0, 0))
    in_specs = [pl.BlockSpec(pieces[0].shape, lambda node, step, sources: (0, 0))] * len(pieces)
    in_specs.append(pl.BlockSpec((piece, cols), lambda node, step, sources: (sources[step], 0)))
    args = [sources, *pieces, block]
    aliases = {}
    if start is not None:
        aliases = {len(args): 0}
        in_specs.append(total)
        args.append(start)
    return product_call(
        functools.partial(partial_body, nodes, count, start is not None),
        (nodes, count), 1, args, in_specs,
        jax.ShapeDtypeStruct((nodes, width, cols), jnp.float32), total,
        [
            pltpu.VMEM((width, 2 * piece), jnp.bfloat16),
            pltpu.VMEM((2 * piece, cols), jnp.bfloat16),
        ],
        4 * nodes * count * width * piece * cols, input_output_aliases=aliases,
    )


def final_product(node, pieces, block, sources, core, lanes, start):
    count = len(pieces) - 1
    width, piece = pieces[0].shape
    cols = block.shape[1]
    out_piece = cols // (2 * lanes)
    half = jax.ShapeDtypeStruct((lanes, width, out_piece), jnp.float32)
    half_spec = pl.BlockSpec(half.shape, lambda step, *_: (0, 0, 0))
    in_specs = [pl.BlockSpec(array.shape, lambda step, *_: (0, 0)) for array in pieces]
    in_specs.append(pl.BlockSpec((piece, cols), lambda step, sources, core: (sources[step], 0)))
    in_specs.append(pl.BlockSpec((None, width, cols), lambda step, *_: (node, 0, 0)))
    return product_call(
        functools.partial(final_body, count, lanes, out_piece), (count,), 2,
        [sources, core, *pieces, block, start], in_specs, [half, half], [half_spec, half_spec],
        [pltpu.VMEM((width, cols), jnp.float32), pltpu.VMEM((width, 2 * piece), jnp.bfloat16)],
        4 * count * width * piece * cols,
    )


pad_rows = 16


def step_of(lanes):
    return 128 if lanes % 128 == 0 else lanes


def encoded(value):
    top = jnp.max(jnp.abs(value), axis=-2, keepdims=True)
    exponent = jnp.ceil(jnp.log2(jnp.maximum(top, 1e-30)) + 0.01)
    whole = jnp.round(value * jnp.exp2(15.0 - exponent)).astype(jnp.int32)
    wide = jnp.broadcast_to(exponent, (pad_rows, value.shape[-1])).astype(jnp.int32)
    return whole.astype(jnp.int16), wide.astype(jnp.int16)


def put_coded(ref, value, lead=()):
    rows = value.shape[0]
    whole, wide = encoded(value)
    ref[(*lead, slice(0, rows), slice(None))] = whole
    ref[(*lead, slice(rows, rows + pad_rows), slice(None))] = wide


def get_coded(ref, lead=()):
    rows = ref.shape[-2] - pad_rows
    whole = ref[(*lead, slice(0, rows), slice(None))].astype(jnp.int32).astype(jnp.float32)
    wide = ref[(*lead, slice(rows, rows + pad_rows), slice(None))].astype(jnp.int32)
    return whole * jnp.exp2(wide.astype(jnp.float32)[0:1, :] - 15.0)


def simple_call(body, args, in_specs, out_shape, out_specs, grid, prefetch=0, **more):
    size = sum(array.size * array.dtype.itemsize for array in args)
    return pl.pallas_call(
        body,
        grid_spec=pltpu.PrefetchScalarGridSpec(
            num_scalar_prefetch=prefetch,
            grid=grid,
            in_specs=in_specs,
            out_specs=out_specs,
            scratch_shapes=more.pop("scratch_shapes", ()),
        ),
        out_shape=out_shape,
        compiler_params=pltpu.CompilerParams(
            dimension_semantics=("arbitrary",) * len(grid), vmem_limit_bytes=48 << 20
        ),
        cost_estimate=pl.CostEstimate(flops=size, bytes_accessed=size, transcendentals=0),
        **more,
    )(*args)


def prepare_body(nodes, block_rows, first_row, ancestors, *refs):
    source, outs = refs[0], refs[1:]
    rows = source.shape[1]
    slots = ancestors.shape[1]
    row = lax.broadcasted_iota(jnp.int32, (rows, 1), 0) + first_row[0]
    first_block = lax.div(first_row[0], block_rows)
    for node in range(nodes):
        keep = None
        for ahead in range((rows - 1) // block_rows + 2):
            block = first_block + ahead
            listed = ancestors[node, 0] == block
            for slot in range(1, slots):
                listed = listed | (ancestors[node, slot] == block)
            inside = (row >= block * block_rows) & (row < (block + 1) * block_rows) & listed
            keep = inside if keep is None else keep | inside
        value = jnp.where(keep, source[node].astype(jnp.float32), 0.0)
        turned = value.T.astype(jnp.bfloat16)
        outs[node][...] = turned
        outs[nodes][node] = turned


def prepare(factor, ancestors, first_row):
    nodes, rows, width = factor.shape
    shape = jax.ShapeDtypeStruct((width, rows), jnp.bfloat16)
    spec = pl.BlockSpec((width, rows), lambda at, *_: (0, 0))
    return simple_call(
        functools.partial(prepare_body, nodes, width),
        [first_row, ancestors, factor],
        [pl.BlockSpec(factor.shape, lambda at, *_: (0, 0, 0))],
        [shape] * nodes + [jax.ShapeDtypeStruct((nodes, width, rows), jnp.bfloat16)],
        [spec] * nodes + [pl.BlockSpec((nodes, width, rows), lambda at, *_: (0, 0, 0))],
        (1,), 2,
    )


def add_encode_body(shifts, lane, *refs):
    total = refs[2 * (shifts + 1)]
    total[...] = refs[0][...] + refs[1][...]
    for at in range(shifts):
        value = refs[2 * at + 2][...] + refs[2 * at + 3][...]
        put_coded(refs[2 * (shifts + 1) + 1 + at], value)


def add_encode(kept, other, lane, lanes):
    _, rows, width = kept.shape
    lane_step = step_of(width)
    in_specs, args = [], []
    for shift in range(lanes):
        spec = pl.BlockSpec(
            (None, rows, lane_step),
            lambda at, lane, shift=shift: (lax.rem(lane[0] + shift, lanes), 0, at),
        )
        in_specs += [spec, spec]
        args += [kept, other]
    out_specs = [pl.BlockSpec((rows, lane_step), lambda at, lane: (0, at))]
    out_shape = [jax.ShapeDtypeStruct((rows, width), jnp.float32)]
    for _ in range(1, lanes):
        out_specs.append(pl.BlockSpec((rows + pad_rows, lane_step), lambda at, lane: (0, at)))
        out_shape.append(jax.ShapeDtypeStruct((rows + pad_rows, width), jnp.int16))
    return simple_call(
        functools.partial(add_encode_body, lanes - 1), [lane, *args], in_specs,
        out_shape, out_specs, (width // lane_step,), 1,
    )


def split_dots(pairs):
    total = None
    for (left_head, left_tail), right in pairs:
        right_head = right.astype(jnp.bfloat16)
        right_tail = (right - right_head.astype(jnp.float32)).astype(jnp.bfloat16)
        for left, value in ((left_tail, right_head), (left_head, right_tail), (left_head, right_head)):
            part = jnp.dot(left, value, preferred_element_type=jnp.float32)
            total = part if total is None else total + part
    return total


def chain_body(node, lanes, *refs):
    mine, *received = refs[:lanes]
    heads = refs[lanes : lanes + node]
    tails = refs[lanes + node : lanes + 2 * node]
    earlier = refs[lanes + 2 * node : lanes + 3 * node]
    value, coded, turned = refs[-3:]
    total = mine[...]
    for ref in received:
        total = total + get_coded(ref)
    if node:
        total = total + split_dots(
            [((h[...], t[...]), e[...]) for h, t, e in zip(heads, tails, earlier, strict=True)]
        )
    total = -total
    value[...] = total
    put_coded(coded, total)
    turned[...] = total.T


def chain(node, nodes, mine, received, heads, tails, earlier, turned):
    rows, width = mine.shape
    lane_step = step_of(width)
    lanes = 1 + len(received)
    first = node * (node - 1) // 2
    column = lambda rows: pl.BlockSpec((rows, lane_step), lambda at: (0, at))
    in_specs = [column(rows)] + [column(rows + pad_rows)] * len(received)
    factor_specs = [
        pl.BlockSpec((None, rows, rows), lambda at, j=j: (first + j, 0, 0)) for j in range(node)
    ]
    in_specs += factor_specs + factor_specs + [column(rows)] * node
    args = [mine, *received, *[heads] * node, *[tails] * node, *earlier]
    aliases = {}
    if turned is not None:
        aliases = {len(args): 2}
        args.append(turned)
        in_specs.append(pl.BlockSpec(memory_space=pl.ANY))
    return simple_call(
        functools.partial(chain_body, node, lanes), args, in_specs,
        [
            jax.ShapeDtypeStruct((rows, width), jnp.float32),
            jax.ShapeDtypeStruct((rows + pad_rows, width), jnp.int16),
            jax.ShapeDtypeStruct((nodes, width, rows), jnp.float32),
        ],
        [
            column(rows),
            column(rows + pad_rows),
            pl.BlockSpec((None, lane_step, rows), lambda at: (node, at, 0)),
        ],
        (width // lane_step,), input_output_aliases=aliases,
    )


def turn_body(*refs):
    refs[-1][...] = get_coded(refs[0]).T


def turn(node, nodes, coded, turned):
    padded, width = coded.shape
    lane_step = step_of(width)
    rows = padded - pad_rows
    args, in_specs = [coded], [pl.BlockSpec((padded, lane_step), lambda at: (0, at))]
    aliases = {}
    if turned is not None:
        aliases = {1: 0}
        args.append(turned)
        in_specs.append(pl.BlockSpec(memory_space=pl.ANY))
    return simple_call(
        turn_body, args, in_specs,
        jax.ShapeDtypeStruct((nodes, width, rows), jnp.float32),
        pl.BlockSpec((None, lane_step, rows), lambda at: (node, at, 0)),
        (width // lane_step,), input_output_aliases=aliases,
    )


def inner_body(half, low, up, left, rows, mine, given):
    value = rows[...]
    head = value.astype(jnp.bfloat16)
    tail = (value - head.astype(jnp.float32)).astype(jnp.bfloat16)
    value = jnp.dot(
        left[...], jnp.concatenate([head, tail, head], axis=0), preferred_element_type=jnp.float32
    )

    @pl.when(pl.program_id(0) < half)
    def _():
        mine[...] = value

    @pl.when(pl.program_id(0) >= half)
    def _():
        given[...] = value


def inner(low, up, left, rows):
    nodes, piece, width = rows.shape
    count = nodes * (nodes + 1) // 2
    half = count // 2
    shape = jax.ShapeDtypeStruct((half, width, width), jnp.float32)
    return simple_call(
        functools.partial(inner_body, half), [low, up, left, rows],
        [
            pl.BlockSpec((None, width, left.shape[2]), lambda at, low, up: (low[at], 0, 0)),
            pl.BlockSpec((None, piece, width), lambda at, low, up: (up[at], 0, 0)),
        ],
        [shape, shape],
        [
            pl.BlockSpec((None, width, width), lambda at, *_: (jnp.minimum(at, half - 1), 0, 0)),
            pl.BlockSpec((None, width, width), lambda at, *_: (jnp.maximum(at - half, 0), 0, 0)),
        ],
        (count,), 2,
    )


def deal_body(plain, coded, count, starts, *refs):
    total = refs[0][...]
    for ref in refs[1:plain]:
        total = total + ref[...]
    for ref in refs[plain : plain + coded]:
        total = total + get_coded(ref)
    outs = refs[plain + coded :]
    if count == 1:
        put_coded(outs[0], total)
        return
    whole = outs[-1]
    whole[...] = total
    rows = total.shape[0] // count
    for at in range(count):
        part = whole[pl.ds(pl.multiple_of(starts[at], 8), rows), :]
        if at == 0:
            outs[0][...] = part
        else:
            put_coded(outs[at], part)


def deal(plain, coded, starts):
    rows, width = plain[0].shape
    lane_step = step_of(width)
    count = starts.shape[0]
    column = lambda rows: pl.BlockSpec((rows, lane_step), lambda at, starts: (0, at))
    part = rows // count
    shapes = [jax.ShapeDtypeStruct((part, width), jnp.float32)] if count > 1 else []
    shapes += [jax.ShapeDtypeStruct((part + pad_rows, width), jnp.int16)] * max(count - 1, 1)
    return simple_call(
        functools.partial(deal_body, len(plain), len(coded), count),
        [starts, *plain, *coded],
        [column(rows)] * len(plain) + [column(rows + pad_rows)] * len(coded),
        shapes, [column(shape.shape[0]) for shape in shapes], (width // lane_step,), 1,
        scratch_shapes=[pltpu.VMEM((rows, lane_step), jnp.float32)] if count > 1 else [],
    )


def heap_body(*refs):
    for at, ref in enumerate(refs[:-1]):
        refs[-1][at] = ref[...]


def heap(parts):
    rows, width = parts[0].shape
    lane_step = step_of(width)
    return simple_call(
        heap_body, parts,
        [pl.BlockSpec((rows, lane_step), lambda at: (0, at))] * len(parts),
        jax.ShapeDtypeStruct((len(parts), rows, width), parts[0].dtype),
        pl.BlockSpec((len(parts), rows, lane_step), lambda at: (0, 0, at)),
        (width // lane_step,),
    )


def finish_body(arrays, width, place, row_of, col_of, *refs):
    parts = refs[:arrays]
    base, out, sums = refs[arrays:]
    step = pl.program_id(0)
    count, padded, _ = parts[0].shape
    rows = padded - pad_rows

    @pl.when(step == 0)
    def _():
        for at, ref in enumerate(parts):

            def put(piece, carry, at=at, ref=ref):
                start = pl.multiple_of(place[at * count + piece], 8)
                sums[pl.ds(start, rows), :] = get_coded(ref, (piece,))
                return carry

            lax.fori_loop(0, count, put, 0)

    row, col = row_of[step], col_of[step]
    low, up = jnp.minimum(row, col), jnp.maximum(row, col)
    start = pl.multiple_of((up * (up + 1) // 2 + low) * width, width)
    value = base[...] - sums[pl.ds(start, width), :]

    @pl.when(row <= col)
    def _():
        out[...] = value

    @pl.when(row > col)
    def _():
        out[...] = value.T


def finish(place, parts, base, nodes, width):
    visits = []
    for up in range(nodes):
        for low in range(up):
            visits += [(low, up), (up, low)]
        visits.append((up, up))
    row_of = jnp.asarray([row for row, _ in visits], jnp.int32)
    col_of = jnp.asarray([col for _, col in visits], jnp.int32)

    def base_map(step, place, row_of, col_of):
        low = jnp.minimum(row_of[step], col_of[step])
        up = jnp.maximum(row_of[step], col_of[step])
        return (up * (up + 1) // 2 + low, 0, 0)

    whole = pl.BlockSpec(parts[0].shape, lambda step, *_: (0, 0, 0))
    return simple_call(
        functools.partial(finish_body, len(parts), width),
        [place, row_of, col_of, *parts, base],
        [whole] * len(parts) + [pl.BlockSpec((None, width, width), base_map)],
        jax.ShapeDtypeStruct((nodes, nodes, width, width), jnp.float32),
        pl.BlockSpec(
            (None, None, width, width),
            lambda step, place, row_of, col_of: (row_of[step], col_of[step], 0, 0),
        ),
        (nodes * nodes,), 3,
        scratch_shapes=[pltpu.VMEM((nodes * (nodes + 1) // 2 * width, width), jnp.float32)],
    )


def spread_bits(number, bits):
    return sum(((number >> at) & 1) << bit for at, bit in enumerate(bits))


def gather_bits(index, bits):
    return sum(((index >> bit) & 1) << at for at, bit in enumerate(bits))


def local(ancestor_inverse, factor, coupling, diagonal_inverse, ancestors):
    row_count = lax.axis_size("row")
    col_count = lax.axis_size("col")
    total = row_count * col_count
    row_index = lax.axis_index("row")
    col_index = lax.axis_index("col")
    flat_index = row_index * col_count + col_index
    nodes, piece_rows, width = factor.shape
    col_bits = col_count.bit_length() - 1
    first_row = (flat_index * piece_rows).reshape(1).astype(jnp.int32)
    *lower, lower_stack = prepare(factor, ancestors, first_row)

    order = ring_order(col_count)
    sources = ring_sources(order, col_index)
    core = (row_index % 2).reshape(1).astype(jnp.int32)
    moves = ring_moves(order)
    lanes = row_count // 2
    steps = col_count // 2
    near, early = 3, 1 + 2 * (steps - 2)
    gathered = [[lower[node]] for node in range(nodes)]

    def advance(step):
        for node in range(nodes):
            gathered[node] = ring_step(gathered[node], moves, step == steps)

    for step in range(1, steps - 1):
        advance(step)

    early_coupling = after(coupling, gathered[0][1])
    turned_heads, turned_tails = split_terms(jnp.swapaxes(early_coupling, 1, 2))
    first_pieces = [group[:near] for group in gathered]
    first_pieces[0][0], turned_heads, turned_tails = lax.optimization_barrier(
        (first_pieces[0][0], turned_heads, turned_tails)
    )
    starts = partial_product(first_pieces, ancestor_inverse, sources[:near])
    advance(steps - 1)
    starts = partial_product(
        [group[near:early] for group in gathered],
        ancestor_inverse,
        sources[near:early],
        starts,
    )
    advance(steps)

    swap = (1 << col_bits) | 1

    def middle(at):
        low, up = at & 1, (at >> col_bits) & 1
        return at if low == up else at ^ swap

    first_moves = [(at, middle(at)) for at in range(total)]
    last_moves = [
        (middle(r * col_count + c), c * row_count + r)
        for r in range(row_count)
        for c in range(col_count)
    ]
    lower_stack = lax.ppermute(
        lower_stack,
        both,
        [
            (c * row_count + r, r * col_count + c)
            for r in range(row_count)
            for c in range(col_count)
            if c * row_count + r != r * col_count + c
        ],
    )

    lane = row_index // 2
    lane_ref = lane.reshape(1).astype(jnp.int32)
    sibling = [(at, at ^ 1) for at in range(row_count)]
    lane_moves = [
        [(at, (at + 2 * shift) % row_count) for at in range(row_count)]
        for shift in range(1, lanes)
    ]

    def lane_sums(given, kept):
        other = lax.ppermute(given, "row", sibling)
        mine, *coded = add_encode(kept, other, lane_ref, lanes)
        return mine, [
            lax.ppermute(part, "row", moves)
            for part, moves in zip(coded, lane_moves, strict=True)
        ]

    base = {}

    def base_columns(columns, others):
        here, diagonal = lax.optimization_barrier((coupling, diagonal_inverse, *others))[:2]
        for k in columns:
            for j in range(k):
                value = -matmul(base[j, 0], here[pair_index(k, 0)])
                for i in range(1, k):
                    value = value - matmul(base[j, i], here[pair_index(k, i)])
                base[j, k] = value
                base[k, j] = value.T
            value = diagonal[k]
            for j in range(k):
                value = value - left_dot(here[pair_index(k, j)], base[j, k])
            base[k, k] = value

    by_cols = []
    out_cols = out_rows = None
    for k in range(nodes):
        given, kept = final_product(
            k, gathered[k][early:], ancestor_inverse, sources[early:], core, lanes, starts
        )
        row_sums = lane_sums(given, kept)
        if k == nodes - 1:
            base_columns(range(k), by_cols[-1:])
            held = lax.optimization_barrier((row_sums[0], base[k - 1, k - 1]))
            row_sums, base[k - 1, k - 1] = (held[0], row_sums[1]), held[1]
        value, coded, out_cols = chain(
            k, nodes, *row_sums, turned_heads, turned_tails, by_cols, out_cols
        )
        by_cols.append(value)
        coded = lax.ppermute(coded, both, first_moves)
        coded = lax.ppermute(coded, both, last_moves)
        out_rows = turn(k, nodes, coded, out_rows)

    stays = col_index * row_count + row_index == flat_index
    lower_stack, late_coupling, _ = lax.optimization_barrier((lower_stack, coupling, by_cols[-2]))
    mixed = []
    for k in range(nodes):
        value = jnp.where(stays, lower[k], lower_stack[k]).astype(jnp.float32)
        for j in range(k):
            value = value - left_dot(late_coupling[pair_index(k, j)], mixed[j])
        mixed.append(value)
    mixed_heads, mixed_tails = split_terms(jnp.stack(mixed))
    left = jnp.concatenate([mixed_tails, mixed_heads, mixed_heads], axis=2)

    count = nodes * (nodes + 1) // 2
    listing = [(j, k) for k in range(nodes) for j in range(k + 1)]
    turned_listing = listing[count // 2 :] + listing[: count // 2]

    def by_core(at):
        one, two = ([pair[at] for pair in pairs] for pairs in (listing, turned_listing))
        return jnp.where(core[0] == 0, jnp.asarray(one, jnp.int32), jnp.asarray(two, jnp.int32))

    low, up = by_core(0), by_core(1)
    kept, given = inner(low, up, left, out_cols)
    half_rows = kept.shape[0] * width
    kept, given = kept.reshape(half_rows, width), given.reshape(half_rows, width)
    flat_bits = (row_count * col_count).bit_length() - 1
    planes = [[0, *range(col_bits + 1, flat_bits)], list(range(1, col_bits))]
    plane_moves = [
        [[(at, at ^ spread_bits(other, bits)) for at in range(total)] for other in range(1, 1 << len(bits))]
        for bits in planes
    ]
    parts_of = [1 << len(bits) for bits in planes]
    mine_of = [gather_bits(flat_index, bits) for bits in planes]

    def starts_of(level, rows):
        around = mine_of[level] ^ jnp.arange(parts_of[level], dtype=jnp.int32)
        return (around * (rows // parts_of[level])).astype(jnp.int32)

    def exchange(arrays, level):
        return [
            lax.ppermute(array, both, moves)
            for array, moves in zip(arrays, plane_moves[level], strict=True)
        ]

    other = lax.ppermute(given, "row", sibling)
    mine, *coded = deal([kept, other], [], starts_of(0, half_rows))
    coded = exchange(coded, 0)
    base_columns(range(nodes - 1, nodes), [mine])
    base = jnp.stack([base[j, k] for k in range(nodes) for j in range(k + 1)])
    mine, base = lax.optimization_barrier((mine, base))
    mine, *coded = deal([mine], coded, starts_of(1, mine.shape[0]))
    coded = exchange(coded, 1)
    (summed,) = deal([mine], coded, jnp.zeros((1,), jnp.int32))
    pile = heap([summed, *exchange([summed] * (parts_of[1] - 1), 1)])
    piles = [pile, *exchange([pile] * (parts_of[0] - 1), 0)]
    *late, out_rows = lax.optimization_barrier((*piles[2:], out_rows))
    piles = [*piles[:2], *late]
    piles += [lax.ppermute(pile, "row", sibling) for pile in piles]
    rows_at = half_rows // (parts_of[0] * parts_of[1])
    around = [mine_of[at] ^ jnp.arange(parts_of[at], dtype=jnp.int32) for at in range(2)]
    within = (around[0][:, None] * parts_of[1] + around[1][None, :]).reshape(-1) * rows_at
    place = jnp.concatenate(
        [core[0] * half_rows + within, (1 - core[0]) * half_rows + within]
    ).astype(jnp.int32)
    pile, base = lax.optimization_barrier((piles[0], base))
    node_blocks = finish(place, [pile, *piles[1:]], base, nodes, width)
    return out_rows, out_cols, node_blocks


def solution(mesh):
    placed = (P("row", "col"), P(None, both, None), P(), P(), P())

    return jax.shard_map(
        local,
        mesh=mesh,
        in_specs=placed,
        out_specs=(P(None, both, None), P(None, ("col", "row"), None), P()),
        check_vma=False,
    )
```
